32 devices in a mesh: cube: 8 (over z, x), band: 4 (over y, core).
Axes of the slice: x: 2, y: 2, z: 4, core: 2. Of those that a mesh axis runs over, the one named last changes fastest.
Arguments:
- visible: bfloat16 [32, 4, 32, 768], P(('cube', 'band')), may hold values from -6 to 6
- kept_rows: int32 [32, 4, 32], P(('cube', 'band')), may hold values from 0 to 767, as said below
- slot_counts: int32 [32, 4], P(('cube', 'band')), may hold values from 16 to 32, as said below
- patches: int32 [16], P('cube'), may hold values from 216 to 384, as said below
- positions: bfloat16 [1536, 512], P('band'), may hold values from -4 to 4
- embedder: bfloat16 [768, 512], P('band'), may hold values from -0.21875 to 0.21875
- embedbias: bfloat16 [512], P('band'), may hold values from -1.75 to 1.75
- masktoken: bfloat16 [512], P('band'), may hold values from -6 to 6
- attngain: bfloat16 [512], P('band'), may hold values from 0.5 to 1.5
- attnbias: bfloat16 [512], P('band'), may hold values from -1.75 to 1.75
- qkvproj: bfloat16 [512, 1536], P('band'), may hold values from -0.375 to 0.375
- qvbias: bfloat16 [1024], P('band'), may hold values from -1.75 to 1.75
- outproj: bfloat16 [512, 512], P('band'), may hold values from -1 to 1
- outbias: bfloat16 [512], P('band'), may hold values from -1.75 to 1.75
- mlpgain: bfloat16 [512], P('band'), may hold values from 0.5 to 1.5
- mlpbias: bfloat16 [512], P('band'), may hold values from -1.75 to 1.75
- upproj: bfloat16 [512, 2048], P('band'), may hold values from -0.25 to 0.25
- upbias: bfloat16 [2048], P('band'), may hold values from -1.75 to 1.75
- downproj: bfloat16 [2048, 512], P('band'), may hold values from -0.125 to 0.125
- downbias: bfloat16 [512], P('band'), may hold values from -1.75 to 1.75
- cotangent: bfloat16 [16, 1536, 512], P('cube', 'band'), may hold values from -6 to 6
Outputs:
- activations: bfloat16 [16, 1536, 512], P('cube', 'band')
- visible_grad: bfloat16 [32, 4, 32, 768], P(('cube', 'band'))
- grad_embedder: float32 [768, 512], P('band')
- grad_embedbias: float32 [512], P('band')
- grad_masktoken: float32 [512], P('band')
- grad_attngain: float32 [512], P('band')
- grad_attnbias: float32 [512], P('band')
- grad_qkvproj: float32 [512, 1536], P('band')
- grad_qvbias: float32 [1024], P('band')
- grad_outproj: float32 [512, 512], P('band')
- grad_outbias: float32 [512], P('band')
- grad_mlpgain: float32 [512], P('band')
- grad_mlpbias: float32 [512], P('band')
- grad_upproj: float32 [512, 2048], P('band')
- grad_upbias: float32 [2048], P('band')
- grad_downproj: float32 [2048, 512], P('band')
- grad_downbias: float32 [512], P('band')
The draws below stay inside these ranges and needn't reach their ends.
Inputs may be any that keep to these rules, and one draw needn't show every extreme that they name: `patches`: each cube has 384 or 216 valid patch rows in every band group; the first cube has 384. `slot_counts`: in every group one owner receives 32 live slots from every device of the group. `kept_rows`: the live slots name rows s * 384 + p of their owner with p under patches of the group's cube s; no row of an owner is named by two live slots; other slots hold any row index.
All inputs are finite; a program needn't handle non-finite values.
Results may differ from the reference program's by a relative error of at most 0.023.
Values may be sent and summed in bfloat16 or wider, within the bound.
A program may use at most 192 MiB of HBM per device.

```python
import jax
import jax.numpy as jnp
from jax import lax

D = 512
E = 768
HEADS = 16
HDIM = 32
FF = 2048
CUBE_DEV = 384
SEQS = 2
CAP = 32
SHORT = 216
LEN = 1536
CUBES = 16
SOURCES = 32
N_CUBE = 8
N_BAND = 4


def layout_draw(key):
    kind_key = jax.random.fold_in(key, 101)
    count_key = jax.random.fold_in(key, 202)
    owner_key = jax.random.fold_in(key, 303)
    source_key = jax.random.fold_in(key, 404)
    order_key = jax.random.fold_in(key, 505)
    fill_key = jax.random.fold_in(key, 606)
    cube_ids = jnp.arange(N_CUBE, dtype=jnp.int32)
    seq_ids = jnp.arange(SEQS, dtype=jnp.int32)
    length_kind = jax.random.randint(kind_key, (N_CUBE, SEQS), 0, 8)
    longer = (length_kind < 5) | (cube_ids[:, None] == 0) & (seq_ids[None, :] == 0)
    patch_counts = jnp.where(longer, CUBE_DEV, SHORT).astype(jnp.int32)
    band_ids = jnp.arange(N_BAND, dtype=jnp.int32)
    half_cap = (CAP + 1) // 2
    slot_count = jax.random.randint(count_key, (N_CUBE, N_BAND, N_BAND), half_cap, CAP + 1)
    full_owner = jax.random.randint(owner_key, (N_CUBE,), 0, N_BAND)
    slot_count = jnp.where(band_ids[None, None, :] == full_owner[:, None, None], CAP, slot_count)
    light_source = jax.random.randint(source_key, (N_CUBE,), 0, N_BAND)
    light_owner = (full_owner + 1) % N_BAND
    light_pair = (band_ids[None, :, None] == light_source[:, None, None]) & (band_ids[None, None, :] == light_owner[:, None, None])
    slot_count = jnp.where(light_pair, half_cap, slot_count).astype(jnp.int32)
    rows_total = SEQS * CUBE_DEV
    row_ids = jnp.arange(rows_total, dtype=jnp.int32)
    row_valid = (row_ids % CUBE_DEV)[None, :] < jnp.repeat(patch_counts, CUBE_DEV, axis=1)
    noise_bits = jax.random.randint(order_key, (N_CUBE, N_BAND, rows_total), 0, 2 ** 18)
    row_score = noise_bits * rows_total + row_ids[None, None, :]
    row_score = jnp.where(row_valid[:, None, :], row_score, row_score + 2 ** 30)
    row_order = jnp.argsort(row_score, axis=-1, stable=True).astype(jnp.int32)
    offsets = jnp.cumsum(slot_count, axis=1) - slot_count
    slot_ids = jnp.arange(CAP, dtype=jnp.int32)
    pick_index = jnp.minimum(offsets[..., None] + slot_ids, rows_total - 1)
    spread_order = jnp.broadcast_to(row_order[:, None, :, :], (N_CUBE, N_BAND, N_BAND, rows_total))
    chosen = jnp.take_along_axis(spread_order, pick_index, axis=-1)
    filler = jax.random.randint(fill_key, (N_CUBE, N_BAND, N_BAND, CAP), 0, rows_total)
    kept_index = jnp.where(slot_ids < slot_count[..., None], chosen, filler).astype(jnp.int32)
    return (patch_counts.reshape(-1), slot_count.reshape(N_CUBE * N_BAND, N_BAND), kept_index.reshape(N_CUBE * N_BAND, N_BAND, CAP))


def draw_patches(key, part):
    return layout_draw(key)[0]


def draw_slot_counts(key, part):
    return layout_draw(key)[1]


def draw_kept_rows(key, part):
    return layout_draw(key)[2]


def shard_levels(key, extent, pieces, low, top_value):
    gain = 1.0
    for dim, blocks in pieces:
        steps = jax.random.uniform(jax.random.fold_in(jax.random.fold_in(key, 6), dim), (blocks,), jnp.float32, low / len(pieces), top_value / len(pieces))
        gain = gain * jnp.repeat(jnp.exp(steps), extent[dim] // blocks).reshape((-1,) + (1,) * (len(extent) - 1 - dim))
    return gain


def bell_draw(key, dims, scale, most, pieces=(), kind=jnp.bfloat16):
    values = jax.random.normal(key, dims, jnp.float32) * scale
    if len(pieces) > 0:
        values = shard_levels(key, dims, pieces, -0.22, 0.18) * values
    return jnp.clip(values, min=-most, max=most).astype(kind)


def setup_inputs(seed: int = 0) -> dict:
    key_list = jax.random.split(jax.random.key(seed), 22)
    visible = bell_draw(key_list[0], (SOURCES, N_BAND, CAP, E), 1.0, 6.0, ((0, 32),))
    kept_rows = draw_kept_rows(jax.random.fold_in(key_list[21], 71), 0)
    slot_counts = draw_slot_counts(jax.random.fold_in(key_list[21], 71), 0)
    patches = draw_patches(jax.random.fold_in(key_list[21], 71), 0)
    positions = bell_draw(key_list[4], (LEN, D), 0.5, 4.0, ((0, 4),))
    embedder = bell_draw(key_list[5], (E, D), E ** -0.5, 0.21875, ((0, 4),))
    embedbias = bell_draw(key_list[6], (D,), 0.3, 1.75, ((0, 4),))
    masktoken = bell_draw(key_list[7], (D,), 1.0, 6.0, ((0, 4),))
    attngain = jnp.clip(1.0 + 0.1 * jax.random.normal(key_list[8], (D,), jnp.float32), 0.5, 1.5).astype(jnp.bfloat16)
    attnbias = bell_draw(key_list[9], (D,), 0.3, 1.75, ((0, 4),))
    qkvproj = bell_draw(key_list[10], (D, 3 * D), (D // 2) ** -0.5, 0.375, ((0, 4),))
    qvbias = bell_draw(key_list[11], (2 * D,), 0.3, 1.75, ((0, 4),))
    outproj = bell_draw(key_list[12], (D, D), (D // 16) ** -0.5, 1.0, ((0, 4),))
    outbias = bell_draw(key_list[13], (D,), 0.3, 1.75, ((0, 4),))
    mlpgain = jnp.clip(1.0 + 0.1 * jax.random.normal(key_list[14], (D,), jnp.float32), 0.5, 1.5).astype(jnp.bfloat16)
    mlpbias = bell_draw(key_list[15], (D,), 0.3, 1.75, ((0, 4),))
    upproj = bell_draw(key_list[16], (D, FF), D ** -0.5, 0.25, ((0, 4),))
    upbias = bell_draw(key_list[17], (FF,), 0.3, 1.75, ((0, 4),))
    downproj = bell_draw(key_list[18], (FF, D), FF ** -0.5, 0.125, ((0, 4),))
    downbias = bell_draw(key_list[19], (D,), 0.3, 1.75, ((0, 4),))
    cotangent = bell_draw(key_list[20], (CUBES, LEN, D), 1.0, 6.0, ((0, 8), (1, 4)))
    return {"visible": visible, "kept_rows": kept_rows, "slot_counts": slot_counts, "patches": patches, "positions": positions, "embedder": embedder, "embedbias": embedbias, "masktoken": masktoken, "attngain": attngain, "attnbias": attnbias, "qkvproj": qkvproj, "qvbias": qvbias, "outproj": outproj, "outbias": outbias, "mlpgain": mlpgain, "mlpbias": mlpbias, "upproj": upproj, "upbias": upbias, "downproj": downproj, "downbias": downbias, "cotangent": cotangent}


epsilon = 1e-06
masked_score = -1e+30
highest = lax.Precision.HIGHEST

@jax.custom_vjp
def low(v):
    return lax.optimization_barrier(v.astype(jnp.bfloat16)).astype(jnp.float32)

@jax.custom_vjp
def low_back(v):
    return v

def low_keep(v):
    return (low(v), None)

def low_pass(kept, grad):
    return (grad,)

def back_keep(v):
    return (v, None)

def back_low(kept, grad):
    return (low(grad),)
low.defvjp(low_keep, low_pass)
low_back.defvjp(back_keep, back_low)

def normalize(values):
    center = values - lax.optimization_barrier(jnp.mean(values, axis=-1, keepdims=True))
    spread = lax.optimization_barrier(jnp.mean(center * center, axis=-1, keepdims=True))
    return center * lax.rsqrt(spread + epsilon)

def attend_cube(inputs):
    queries, keys_in, values_in, key_valid = inputs
    query_heads = queries.reshape(LEN, HEADS, HDIM)
    key_heads = keys_in.reshape(LEN, HEADS, HDIM)
    value_heads = values_in.reshape(LEN, HEADS, HDIM)
    scores = jnp.einsum('qhd,khd->hqk', query_heads, key_heads, precision=highest) * HDIM ** (-0.5)
    scores = jnp.where(key_valid[None, None, :], scores, masked_score)
    scores = low_back(scores)
    attn_probs = low(jax.nn.softmax(scores, axis=-1))
    mixed_heads = jnp.einsum('hqk,khd->qhd', attn_probs, value_heads, precision=highest)
    return low(low_back(mixed_heads.reshape(LEN, D)))

def forward(encodings, embedder, embedbias, masktoken, attngain, attnbias, qkvproj, qvbias, outproj, outbias, mlpgain, mlpbias, upproj, upbias, downproj, downbias, layout):
    flat_index, live_slot, kept_flag, position_rows, token_valid, key_valid = layout
    lifted = low_back(jnp.einsum('sdce,ef->sdcf', encodings, embedder, precision=highest) + embedbias)
    placed = jnp.zeros((CUBES * LEN, D), jnp.float32).at[flat_index].add((lifted * live_slot[..., None]).reshape(-1, D))
    embedded = placed.reshape(CUBES, LEN, D) + (1.0 - kept_flag)[..., None] * masktoken + position_rows[None]
    first_in = low(normalize(embedded) * attngain + attnbias)
    full_bias = jnp.concatenate([qvbias[:D], jnp.zeros((D,), jnp.float32), qvbias[D:]])
    projected = jnp.einsum('ctd,de->cte', first_in, qkvproj, precision=highest) + full_bias
    queries = low(low_back(projected[..., :D]))
    keys_all = low(low_back(projected[..., D:2 * D]))
    values_all = low(low_back(projected[..., 2 * D:]))
    mixed_heads = lax.map(jax.checkpoint(attend_cube), (queries, keys_all, values_all, key_valid))
    branch = low_back(jnp.einsum('ctd,de->cte', mixed_heads, outproj, precision=highest) + outbias)
    middle = embedded + branch
    second = low(normalize(middle) * mlpgain + mlpbias)
    hidden = low_back(jnp.einsum('ctd,df->ctf', second, upproj, precision=highest) + upbias)
    active = low(jax.nn.gelu(hidden, approximate=False))
    result = middle + jnp.einsum('ctf,fd->ctd', active, downproj, precision=highest) + downbias
    return token_valid[..., None] * result

def reference(visible, kept_rows, slot_counts, patches, positions, embedder, embedbias, masktoken, attngain, attnbias, qkvproj, qvbias, outproj, outbias, mlpgain, mlpbias, upproj, upbias, downproj, downbias, cotangent):
    group_index = (jnp.arange(SOURCES, dtype=jnp.int32) // N_BAND).astype(jnp.int32)[:, None, None]
    owner_index = jnp.arange(N_BAND, dtype=jnp.int32)[None, :, None]
    cube_index = group_index * SEQS + kept_rows // CUBE_DEV
    place_index = owner_index * CUBE_DEV + kept_rows % CUBE_DEV
    flat_index = (cube_index * LEN + place_index).reshape(-1).astype(jnp.int32)
    slot_index = jnp.arange(CAP, dtype=jnp.int32)
    live_slot = (slot_index[None, None, :] < slot_counts[:, :, None]).astype(jnp.float32)
    kept_flag = jnp.zeros((CUBES * LEN,), jnp.float32).at[flat_index].add(live_slot.reshape(-1)).reshape(CUBES, LEN)
    patch_index = jnp.arange(LEN, dtype=jnp.int32) % CUBE_DEV
    key_valid = patch_index[None, :] < patches[:, None]
    token_valid = key_valid.astype(jnp.float32)
    layout = (flat_index, live_slot, kept_flag, positions.astype(jnp.float32), token_valid, key_valid)
    params = (embedder.astype(jnp.float32), embedbias.astype(jnp.float32), masktoken.astype(jnp.float32), attngain.astype(jnp.float32), attnbias.astype(jnp.float32), qkvproj.astype(jnp.float32), qvbias.astype(jnp.float32), outproj.astype(jnp.float32), outbias.astype(jnp.float32), mlpgain.astype(jnp.float32), mlpbias.astype(jnp.float32), upproj.astype(jnp.float32), upbias.astype(jnp.float32), downproj.astype(jnp.float32), downbias.astype(jnp.float32))

    def wrapped(encodings, *weights):
        return forward(encodings, *weights, layout)
    result, pullback = jax.vjp(wrapped, visible.astype(jnp.float32), *params)
    gradients = pullback(cotangent.astype(jnp.float32))
    return (result.astype(jnp.bfloat16), gradients[0].astype(jnp.bfloat16), gradients[1], gradients[2], gradients[3], gradients[4], gradients[5], gradients[6], gradients[7], gradients[8], gradients[9], gradients[10], gradients[11], gradients[12], gradients[13], gradients[14], gradients[15])
```

```python
import functools

import jax
import jax.numpy as jnp
from jax import lax
from jax.experimental import pallas as pl
from jax.experimental.pallas import tpu as pltpu
from jax.sharding import PartitionSpec as P

HEADS = 16
HDIM = 32
EPS = 1e-06
LOG2E = 1.4426950408889634
QSCALE = HDIM ** (-0.5) * LOG2E
MESH = pl.DeviceIdType.MESH
NT = (((1,), (1,)), ((), ()))
f32 = jnp.float32
bf16 = jnp.bfloat16
ANY = pl.BlockSpec(memory_space=pl.ANY)
VM = pl.BlockSpec(memory_space=pltpu.VMEM)
VMEM_LIMIT = 60 * 2**20


def iota(shape, dim):
    return lax.broadcasted_iota(jnp.int32, shape, dim)


def normalize(values):
    center = values - jnp.mean(values, axis=-1, keepdims=True)
    spread = jnp.mean(center * center, axis=-1, keepdims=True)
    return center * lax.rsqrt(spread + EPS)


def place():
    cube, band = lax.axis_index("cube"), lax.axis_index("band")
    y, c = band // 2, band % 2
    return cube, band, y, c


def peers():
    cube, band, y, c = place()
    same_chip = (cube, 2 * y + 1 - c)
    across = (cube, 2 * (1 - y) + c)
    diagonal = (cube, 2 * (1 - y) + 1 - c)
    return same_chip, across, diagonal


def greet(devices):
    barrier = pltpu.get_barrier_semaphore()
    for device in devices:
        pl.semaphore_signal(barrier, inc=1, device_id=device, device_id_type=MESH)
    pl.semaphore_wait(barrier, len(devices))


def remote(src, dst, send, recv, device):
    return pltpu.make_async_remote_copy(
        src_ref=src, dst_ref=dst, send_sem=send, recv_sem=recv, device_id=device, device_id_type=MESH
    )


def rows(start, size):
    return pl.ds(pl.multiple_of(start, 16), size)


def params(collective_id=None):
    if collective_id is None:
        return pltpu.CompilerParams(vmem_limit_bytes=VMEM_LIMIT)
    return pltpu.CompilerParams(collective_id=collective_id, has_side_effects=True, vmem_limit_bytes=VMEM_LIMIT)


def mate_of(k):
    cube, b, _, _ = place()
    d = 1 << k
    return (cube + d - 2 * d * ((cube // d) % 2), b)


def unpack(vecf, spans):
    vectors = vecf[...].astype(f32)
    out = []
    for first, count, bands in spans:
        out.append(
            jnp.concatenate([vectors[d, k : k + 1] for d in bands for k in range(first, first + count)], axis=1)
        )
    return out


ALL = (0, 1, 2, 3)


def embed_kernel(
    vis, kept, emb, qkv, pos, *refs,
):
    vecs = refs[:10]
    (embedded, first_in, q_out, k_out, v_out, emb_out, qkv_out, enc_out, tgt_out, vecf,
     enc, tgt, embf, qkvf, posf, vec, kbuf, vbuf, lsem, ssem, rsem) = refs[10:]
    cube, b, y, c = place()
    x = cube % 2
    chip, across, diag = peers()
    mate = mate_of(0)
    bq = 2 * (1 - y) + c
    er, qr = emb.shape[0], qkv.shape[0]
    half = pos.shape[0]
    model = emb.shape[1]
    fill = jnp.zeros((vec.shape[0] - sum(v.shape[0] for v in vecs), 128), f32)
    vec[...] = jnp.concatenate([v[...].astype(f32) for v in vecs] + [fill], axis=0).astype(bf16)
    greet((chip, across, diag, mate))

    used = [0]
    local = []

    def send(src, dst, device):
        copy = remote(src, dst, ssem.at[used[0]], rsem.at[used[0]], device)
        used[0] += 1
        copy.start()
        return copy

    def keep(src, dst):
        copy = pltpu.make_async_copy(src, dst, lsem.at[len(local)])
        copy.start()
        local.append(copy)

    def cut(start, size, which):
        return rows(start + which * (size // 2), size // 2)

    ea, qa = rows(b * er, er), rows(b * qr, qr)
    far_vec = send(vec, vecf.at[b], across)
    small = [
        send(kept.at[c], tgt.at[b], across),
        send(vis.at[:, c], enc.at[b], across),
        send(kept.at[1 - c], tgt.at[b], diag),
        send(vis.at[:, 1 - c], enc.at[b], diag),
        send(kept.at[1 - c], tgt.at[b], chip),
        send(vec, vecf.at[b], chip),
        send(vis.at[:, 1 - c], enc.at[b], chip),
        send(emb, embf.at[ea], chip),
    ]
    far_emb = send(emb.at[cut(0, er, x)], embf.at[cut(b * er, er, x)], across)
    far_pos = send(pos.at[cut(0, half, x)], posf.at[y, cut(0, half, x)], across)
    far_qkv = send(qkv.at[cut(0, qr, x)], qkvf.at[cut(b * qr, qr, x)], across)
    near_qkv = send(qkv, qkvf.at[qa], chip)
    keep(kept.at[c], tgt.at[b])
    keep(vec, vecf.at[b])
    keep(vis.at[:, c], enc.at[b])
    keep(emb, embf.at[ea])
    keep(pos, posf.at[y])
    keep(qkv, qkvf.at[qa])

    far_vec.wait()
    relays = [send(vecf.at[bq], vecf.at[bq], chip)]
    far_emb.wait()
    got = cut(bq * er, er, x)
    side_emb = send(embf.at[got], embf.at[got], mate)
    relays.append(send(embf.at[got], embf.at[got], chip))
    far_pos.wait()
    got = cut(0, half, x)
    side_pos = send(posf.at[1 - y, got], posf.at[1 - y, got], mate)
    side_emb.wait()
    got = cut(bq * er, er, 1 - x)
    relays.append(send(embf.at[got], embf.at[got], chip))
    for copy in small + local + relays:
        copy.wait()
    side_pos.wait()

    target = jnp.max(tgt[...].astype(f32), axis=0)[0:1].astype(jnp.int32)
    tgt_out[...] = jnp.broadcast_to(target, tgt_out.shape)
    enc_all = enc[...].reshape(enc_out.shape)
    enc_out[...] = enc_all
    embedbias, mask, gain, bias, qbias, vbias = unpack(
        vecf, ((0, 1, ALL), (1, 1, ALL), (2, 1, ALL), (3, 1, ALL), (4, 2, (0, 1)), (4, 2, (2, 3)))
    )
    slots = enc_out.shape[0]

    def lift(h):
        span = pl.ds(h * half, half)
        cells = iota((half, slots), 0) + (y * half + h * 2 * half)
        hit = (cells == target).astype(f32)
        flag = jnp.sum(hit, axis=1, keepdims=True)
        picked = jnp.dot(hit.astype(bf16), enc_all, preferred_element_type=f32).astype(bf16)
        rows_in = jnp.dot(picked, embf[...], preferred_element_type=f32)
        v = rows_in + flag * embedbias + (1.0 - flag) * mask + posf[h].astype(f32)
        embedded[span] = v
        first_in[span] = (normalize(v) * gain + bias).astype(bf16)

    lift(0)
    far_qkv.wait()
    got = cut(bq * qr, qr, x)
    side_qkv = send(qkvf.at[got], qkvf.at[got], mate)
    relays = [send(qkvf.at[got], qkvf.at[got], chip)]
    lift(1)
    emb_out[...] = embf[...]
    side_qkv.wait()
    got = cut(bq * qr, qr, 1 - x)
    relays.append(send(qkvf.at[got], qkvf.at[got], chip))
    near_qkv.wait()
    for copy in relays:
        copy.wait()
    mine = rows(c * 2 * half, 2 * half)
    k = jnp.dot(first_in[...], qkvf[:, model : 2 * model], preferred_element_type=f32)
    kbuf[...] = k.astype(bf16)
    out = [send(kbuf, k_out.at[mine], chip)]
    v = jnp.dot(first_in[...], qkvf[:, 2 * model :], preferred_element_type=f32)
    vbuf[...] = (v + vbias).astype(bf16)
    out.append(send(vbuf, v_out.at[mine], chip))
    first_local = len(local)
    keep(kbuf, k_out.at[mine])
    keep(vbuf, v_out.at[mine])
    q = jnp.dot(first_in[...], qkvf[:, :model], preferred_element_type=f32)
    q_out[...] = ((q + qbias) * QSCALE).astype(bf16)
    qkv_out[...] = qkvf[...]
    for copy in out + local[first_local:]:
        copy.wait()


def embed(vis, kept, emb, qkv, pos, vecs):
    er, model = emb.shape
    qr, wide = qkv.shape
    half = pos.shape[0]
    enc_width = vis.shape[-1]
    cap = vis.shape[2]
    slots = 8 * cap
    tokens = 2 * half
    sds = jax.ShapeDtypeStruct
    return pl.pallas_call(
        embed_kernel,
        name="embed_project",
        out_shape=(
            sds((tokens, model), f32),
            sds((tokens, model), bf16),
            sds((tokens, model), bf16),
            sds((2 * tokens, model), bf16),
            sds((2 * tokens, model), bf16),
            sds((4 * er, model), bf16),
            sds((4 * qr, wide), bf16),
            sds((slots, enc_width), bf16),
            sds((8, slots), jnp.int32),
            sds((4, 16, 128), bf16),
        ),
        in_specs=[ANY] * 5 + [VM] * 10,
        out_specs=(VM, VM, VM, ANY, ANY, VM, VM, VM, VM, VM),
        scratch_shapes=[
            pltpu.VMEM((4, 2, cap, enc_width), bf16),
            pltpu.VMEM((4, 8, slots), jnp.int32),
            pltpu.VMEM((4 * er, model), bf16),
            pltpu.VMEM((4 * qr, wide), bf16),
            pltpu.VMEM((2, half, model), bf16),
            pltpu.VMEM((16, 128), bf16),
            pltpu.VMEM((tokens, model), bf16),
            pltpu.VMEM((tokens, model), bf16),
            pltpu.SemaphoreType.DMA((8,)),
            pltpu.SemaphoreType.DMA((24,)),
            pltpu.SemaphoreType.DMA((24,)),
        ],
        compiler_params=params(0),
    )(vis, kept, emb, qkv, pos, *vecs)


def forward_kernel(
    patch, q_ref, k_ref, v_ref, outw, upw, downw, cot,
    e_ref, o_ref, linv_ref, mix_ref, out_full, up_full, down_full, cot_full,
    kxa, kxb, vt, sa, sb, ots, ssem, rsem,
):
    p = pl.program_id(0)
    last = pl.num_programs(0) - 1
    cube, b, y, c = place()
    x = cube % 2
    chip, across, _ = peers()
    mate = mate_of(0)
    bq = 2 * (1 - y) + c
    shards = ((upw, up_full), (outw, out_full), (downw, down_full))

    def cut(k, band, which):
        size = shards[k][0].shape[0]
        return rows(band * size + which * (size // 2), size // 2)

    def far(k):
        size = shards[k][0].shape[0]
        part = rows(x * (size // 2), size // 2)
        return remote(shards[k][0].at[part], shards[k][1].at[cut(k, b, x)], ssem.at[k], rsem.at[k], across)

    def near(k):
        size = shards[k][0].shape[0]
        return remote(shards[k][0], shards[k][1].at[rows(b * size, size)], ssem.at[3 + k], rsem.at[3 + k], chip)

    def side(k):
        ref = shards[k][1].at[cut(k, bq, x)]
        return remote(ref, ref, ssem.at[6 + k], rsem.at[6 + k], mate)

    def relay(k, which):
        ref = shards[k][1].at[cut(k, bq, x if which == 0 else 1 - x)]
        at = 9 + 2 * k + which
        return remote(ref, ref, ssem.at[at], rsem.at[at], chip)

    def cot_far():
        return remote(cot.at[1 - y], cot_full, ssem.at[15], rsem.at[15], across)

    @pl.when(p == 0)
    def _():
        greet((chip, across, mate))
        far(0).start()
        far(1).start()
        far(2).start()
        cot_far().start()
        for k in range(3):
            near(k).start()

    for k, at in ((0, 2), (1, 3), (2, 4)):

        @pl.when(p == at)
        def _(k=k):
            far(k).wait()
            side(k).start()
            relay(k, 0).start()

    for k, at in ((0, 5), (1, 6), (2, 7)):

        @pl.when(p == at)
        def _(k=k):
            side(k).wait()
            relay(k, 1).start()

    keys = k_ref.shape[0]
    tokens = q_ref.shape[0]
    lane = iota((keys, 128), 1)
    pieces = 3
    block = tokens // pieces

    @pl.when(p == 0)
    def _():
        row = iota((keys, 128), 0)
        bias = jnp.where((row % cot.shape[1] >= patch[y]) & (lane == 0), -1e30, 0.0).astype(bf16)
        kxa[:, 128:256] = bias
        kxb[:, 128:256] = bias
        for g in range(v_ref.shape[1] // 128):
            cols = slice(g * 128, (g + 1) * 128)
            vt[cols] = v_ref[:, cols].astype(f32).T.astype(bf16)

    def lanes(h):
        return pl.ds(pl.multiple_of((h // 4) * 128, 128), 128)

    def prepare(h, kx):
        k = k_ref[:, lanes(h)]
        kx[:, 0:128] = jnp.where((lane // HDIM) == (h % 4), k, jnp.zeros_like(k))

    def score(h, kx, s, j):
        span = slice(j * block, (j + 1) * block)
        qx = jnp.concatenate([q_ref[span, lanes(h)], jnp.ones((block, 128), bf16)], axis=1)
        s[span] = lax.dot_general(qx, kx[...], NT, preferred_element_type=f32)

    ones = jnp.ones((16, keys), bf16)

    def soften(at, h, s, j):
        span = slice(j * block, (j + 1) * block)
        v = s[span]
        e = jnp.exp2(v - jnp.max(v, axis=1, keepdims=True)).astype(bf16)
        e_ref[at, span] = e
        lhs = jnp.concatenate([vt[pl.ds(pl.multiple_of(h * HDIM, HDIM), HDIM)], ones], axis=0)
        ot = lax.dot_general(lhs, e, NT, preferred_element_type=f32)
        li = 1.0 / ot[HDIM : HDIM + 8]
        o = ot[:HDIM] * li[0:1]
        o_ref[at * HDIM : (at + 1) * HDIM, span] = o
        ots[pl.ds(pl.multiple_of((p % 2) * 2 * HDIM + at * HDIM, HDIM), HDIM), span] = o
        linv_ref[at, :, span] = li

    @pl.when(p == 0)
    def _():
        prepare(0, kxa)
        for j in range(pieces):
            score(0, kxa, sa, j)

    after = jnp.minimum(2 * p + 2, 2 * last + 1)
    prepare(2 * p + 1, kxb)
    for j in range(pieces):
        score(2 * p + 1, kxb, sb, j)
        soften(0, 2 * p, sa, j)
    prepare(after, kxa)
    for j in range(pieces):
        score(after, kxa, sa, j)
        soften(1, 2 * p + 1, sb, j)

    @pl.when(p % 2 == 1)
    def _():
        mix_ref[...] = ots[...].T.astype(bf16)

    @pl.when(p == last)
    def _():
        cot_far().wait()
        for k in range(3):
            near(k).wait()
            relay(k, 0).wait()
            relay(k, 1).wait()


def attend(patch, q, k, v, outw, upw, downw, cot):
    tokens, model = q.shape
    keys = k.shape[0]
    sds = jax.ShapeDtypeStruct

    def fixed(shape):
        return pl.BlockSpec(shape, lambda p: (0, 0))

    return pl.pallas_call(
        forward_kernel,
        name="attend",
        grid=(HEADS // 2,),
        in_specs=[
            pl.BlockSpec(memory_space=pltpu.SMEM),
            fixed(q.shape),
            fixed(k.shape),
            fixed(v.shape),
            ANY, ANY, ANY, ANY,
        ],
        out_specs=[
            pl.BlockSpec((2, tokens, keys), lambda p: (p, 0, 0)),
            pl.BlockSpec((2 * HDIM, tokens), lambda p: (p, 0)),
            pl.BlockSpec((2, 8, tokens), lambda p: (p, 0, 0)),
            pl.BlockSpec((tokens, 128), lambda p: (0, p // 2)),
            ANY, ANY, ANY, ANY,
        ],
        out_shape=[
            sds((HEADS, tokens, keys), bf16),
            sds((model, tokens), f32),
            sds((HEADS, 8, tokens), f32),
            sds((tokens, model), bf16),
            sds((4 * outw.shape[0], outw.shape[1]), bf16),
            sds((4 * upw.shape[0], upw.shape[1]), bf16),
            sds((4 * downw.shape[0], downw.shape[1]), bf16),
            sds(cot.shape[1:], bf16),
        ],
        scratch_shapes=[
            pltpu.VMEM((keys, 256), bf16),
            pltpu.VMEM((keys, 256), bf16),
            pltpu.VMEM((model, keys), bf16),
            pltpu.VMEM((tokens, keys), f32),
            pltpu.VMEM((tokens, keys), f32),
            pltpu.VMEM((128, tokens), f32),
            pltpu.SemaphoreType.DMA((16,)),
            pltpu.SemaphoreType.DMA((16,)),
        ],
        compiler_params=params(1),
    )(patch, q, k, v, outw, upw, downw, cot)


def mlp_kernel(
    patch, vecf, mixed, embedded, out_got, up_got, down_got, cot_got, out_own, up_own, down_own, cot_own,
    act, grads, grad_middle, grad_mixed, sums,
    outw, upf, downf, cot, second_t, mixed_t, gout_t, second, active, hid, branch_b, wsem,
):
    _, b, y, _ = place()
    tokens, model = mixed.shape
    half = tokens // 2
    wide = upf.shape[1]
    parts = wide // model
    loads = []

    def load(src, dst):
        copy = pltpu.make_async_copy(src, dst, wsem.at[len(loads)])
        copy.start()
        loads.append(copy)

    for own, got, full in ((out_own, out_got, outw), (up_own, up_got, upf), (down_own, down_got, downf)):
        size = own.shape[0]
        load(own, full.at[rows(b * size, size)])
        for k in range(1, 4):
            part = rows((b + k) % 4 * size, size)
            load(got.at[part], full.at[part])
    load(cot_own.at[y], cot.at[y])
    load(cot_got, cot.at[1 - y])
    vectors = vecf[...].astype(f32)

    def whole(k):
        return jnp.concatenate([vectors[d, k : k + 1] for d in range(4)], axis=1)

    outbias, gain, bias, downbias = whole(6), whole(7), whole(8), whole(13)
    upbias = [jnp.concatenate([vectors[d, 9 + k : 10 + k] for k in range(4)], axis=1) for d in range(parts)]
    live = iota((half, 1), 0) < patch[y]
    valid = jnp.where(live, 1.0, 0.0)
    total = [jnp.zeros((1, model), f32)] * (4 + parts)
    for copy in loads[:4]:
        copy.wait()
    for h in range(2):
        span = pl.ds(h * half, half)
        mix = mixed[span]
        mixed_t[:, span] = mix.astype(f32).T.astype(bf16)
        middle = embedded[span] + (jnp.dot(mix, outw[...], preferred_element_type=f32) + outbias)
        center = middle - jnp.mean(middle, axis=-1, keepdims=True)
        rstd = lax.rsqrt(jnp.mean(center * center, axis=-1, keepdims=True) + EPS)
        normed = center * rstd
        sec = normed * gain + bias
        second_t[:, span] = sec.T.astype(bf16)
        sec = sec.astype(bf16)
        if h == 0:
            for copy in loads[4:]:
                copy.wait()
        gout = cot[h].astype(f32) * valid
        gout_t[:, span] = gout.T.astype(bf16)
        gout_b = gout.astype(bf16)
        total[0] += jnp.sum(gout, axis=0, keepdims=True)
        result = middle + downbias
        gsec = None
        for k in range(parts):
            cols = slice(k * model, (k + 1) * model)
            hidden = jnp.dot(sec, upf[:, cols], preferred_element_type=f32) + upbias[k]
            cdf = 0.5 + 0.5 * lax.erf(hidden * 0.7071067811865476)
            low = (hidden * cdf).astype(bf16)
            active[span, cols] = low
            slope = cdf + hidden * (0.3989422804014327 * jnp.exp(-0.5 * hidden * hidden))
            result += jnp.dot(low, downf[cols], preferred_element_type=f32)
            gact = lax.dot_general(gout_b, downf[cols], NT, preferred_element_type=f32)
            ghid = (gact * slope).astype(bf16)
            hid[span, cols] = ghid
            total[4 + k] += jnp.sum(ghid.astype(f32), axis=0, keepdims=True)
            term = lax.dot_general(ghid, upf[:, cols], NT, preferred_element_type=f32)
            gsec = term if gsec is None else gsec + term
        act[h] = (valid * result).astype(bf16)
        total[2] += jnp.sum(gsec * normed, axis=0, keepdims=True)
        total[3] += jnp.sum(gsec, axis=0, keepdims=True)
        gn = gsec * gain
        back = rstd * (
            gn - jnp.mean(gn, axis=-1, keepdims=True) - normed * jnp.mean(gn * normed, axis=-1, keepdims=True)
        )
        gmid = gout + back
        grad_middle[span] = gmid
        gb = gmid.astype(bf16)
        branch_b[span] = gb
        total[1] += jnp.sum(gb.astype(f32), axis=0, keepdims=True)
        grad_mixed[span] = lax.dot_general(gb, outw[...], NT, preferred_element_type=f32).astype(bf16)
    for k in range(parts):
        cols = slice(k * model, (k + 1) * model)
        grads[k, 0:model] = jnp.dot(gout_t[...], active[:, cols], preferred_element_type=f32).astype(bf16)
        gup = jnp.dot(second_t[...], hid[:, cols], preferred_element_type=f32).astype(bf16)
        size = model // 4
        for d in range(4):
            grads[d, model + k * size : model + (k + 1) * size] = gup[d * size : (d + 1) * size]
    base = model + parts * (model // 4)
    gout_w = jnp.dot(mixed_t[...], branch_b[...], preferred_element_type=f32).astype(bf16)
    for d in range(4):
        grads[d, base : base + model // 4] = gout_w[d * (model // 4) : (d + 1) * (model // 4)]
    sums[...] = jnp.concatenate(total, axis=0)


def mlp(patch, vecf, mixed, embedded, gathered, own):
    tokens, model = mixed.shape
    outw, upw, downw, cot = own
    wide = upw.shape[1]
    half = cot.shape[1]
    depth = model + wide // 4 + model // 4
    sds = jax.ShapeDtypeStruct
    return pl.pallas_call(
        mlp_kernel,
        name="mlp_both",
        out_shape=(
            sds((2, half, model), bf16),
            sds((4, depth, model), bf16),
            sds((tokens, model), f32),
            sds((tokens, model), bf16),
            sds((4 + wide // model, model), f32),
        ),
        in_specs=[pl.BlockSpec(memory_space=pltpu.SMEM), VM, VM, VM] + [ANY] * 8,
        out_specs=(VM, VM, VM, VM, VM),
        scratch_shapes=[
            pltpu.VMEM((model, model), bf16),
            pltpu.VMEM((model, wide), bf16),
            pltpu.VMEM((wide, model), bf16),
            pltpu.VMEM((2, half, model), bf16),
            pltpu.VMEM((model, tokens), bf16),
            pltpu.VMEM((model, tokens), bf16),
            pltpu.VMEM((model, tokens), bf16),
            pltpu.VMEM((tokens, model), bf16),
            pltpu.VMEM((tokens, wide), bf16),
            pltpu.VMEM((tokens, wide), bf16),
            pltpu.VMEM((tokens, model), bf16),
            pltpu.SemaphoreType.DMA((14,)),
        ],
        compiler_params=params(),
    )(patch, vecf, mixed, embedded, *gathered, *own)


def reducer(cubes, chunk, grads, got_core, got_y, work, gots, total, ssem, rsem):
    cube, b, y, c = place()
    chip, across, _ = peers()
    bits = cubes.bit_length() - 1
    own, other = 2 * y + c, 2 * (1 - y) + c

    def kept(k):
        start = 0
        for j in range(k):
            start = start + ((cube // (1 << j)) % 2) * (chunk >> (j + 1))
        return start

    def copies(s, t):
        base = t * chunk
        if s == 0:
            span = rows(base, chunk)
            return [
                remote(grads.at[1 - c, span], got_core.at[0, span], ssem.at[t, 0], rsem.at[t, 0], chip),
                remote(grads.at[3 - c, span], got_core.at[1, span], ssem.at[t, 1], rsem.at[t, 1], chip),
            ]
        if s == 1:
            span = rows(base, chunk)
            return [remote(work.at[1, span], got_y.at[span], ssem.at[t, 2], rsem.at[t, 2], across)]
        if s < 2 + bits:
            k = s - 2
            size = chunk >> (k + 1)
            bit = (cube // (1 << k)) % 2
            away = rows(base + kept(k) + (1 - bit) * size, size)
            return [
                remote(work.at[0, away], gots[k].at[rows(t * size, size)], ssem.at[t, s + 1], rsem.at[t, s + 1],
                       mate_of(k))
            ]
        k = 2 * bits + 1 - s
        span = rows(base + kept(k + 1), chunk >> (k + 1))
        return [remote(total.at[span], total.at[span], ssem.at[t, s + 1], rsem.at[t, s + 1], mate_of(k))]

    def run(s, t):
        base = t * chunk
        if s > 0:
            for copy in copies(s - 1, t):
                copy.wait()
        if s == 1:
            span = rows(base, chunk)
            work[1, span] = grads[other, span] + got_core[1 - y, span]
        elif s == 2:
            span = rows(base, chunk)
            work[0, span] = (grads[own, span] + got_core[y, span]) + got_y[span]
        elif 2 < s <= 2 + bits:
            k = s - 3
            size = chunk >> (k + 1)
            span = rows(base + kept(k + 1), size)
            value = work[0, span] + gots[k][rows(t * size, size)]
            if s < 2 + bits:
                work[0, span] = value
            else:
                total[span] = value
        if s < 2 + 2 * bits:
            for copy in copies(s, t):
                copy.start()

    return run, 2 + 2 * bits


def reducer_scratch(cubes, count, depth, width):
    bits = cubes.bit_length() - 1
    return [
        pltpu.VMEM((2, depth, width), bf16),
        pltpu.VMEM((depth, width), bf16),
        pltpu.VMEM((2, depth, width), bf16),
    ] + [pltpu.VMEM((depth >> (k + 1), width), bf16) for k in range(bits)] + [
        pltpu.SemaphoreType.DMA((count, 3 + 2 * bits)),
        pltpu.SemaphoreType.DMA((count, 3 + 2 * bits)),
    ]


def backward_kernel(
    cubes, chunk,
    q_ref, k_ref, v_ref, do_ref, o_ref, linv_ref, e_ref, act, grads,
    dq_ref, dk_out, dv_out, act_full, total_out,
    vb, kt, qt, dot_t, dox, partb, dqt, dkt, dvt, dk, dv, dk_in, dv_in, lsem, ssem, rsem, total, got_core, got_y, work, *rest,
):
    gots, (rs, rr) = rest[:-2], rest[-2:]
    n = pl.program_id(0)
    last = pl.num_programs(0) - 1
    h, g = n % 4, n // 4
    cube, b, y, c = place()
    chip, across, _ = peers()
    bits = cubes.bit_length() - 1
    keys = k_ref.shape[0]
    half_keys = keys // 2
    tokens = q_ref.shape[0]
    run, stages = reducer(cubes, chunk, grads, got_core, got_y, work, gots, total, rs, rr)
    count = grads.shape[1] // chunk
    period = 2
    when = [0, 2, 8] + [10 + 2 * k for k in range(stages - 2)]
    ticks = 2 * (last + 1)

    def poll(tick):
        for s in range(stages, -1, -1):
            late = tick - when[s]
            t = late // period

            @pl.when((late >= 0) & (late % period == 0) & (t < count))
            def _(s=s, t=t):
                run(s, t)

    def act_far():
        return remote(act.at[1 - y], act_full.at[y], ssem.at[8], rsem.at[8], across)

    def act_own():
        return pltpu.make_async_copy(act.at[y], act_full.at[y], lsem.at[0])

    @pl.when(n == 0)
    def _():
        greet((chip, across) + tuple(mate_of(k) for k in range(bits)))
        act_own().start()

    poll(2 * n)

    @pl.when(n == 10)
    def _():
        act_far().start()

    lane = iota((keys, 128), 1)

    @pl.when(h == 0)
    def _():
        vb[:, 128:256] = jnp.where(lane < 2, 1.0, 0.0).astype(bf16)
        kt[...] = k_ref[...].astype(f32).T.astype(bf16)
        qt[...] = q_ref[...].astype(f32).T.astype(bf16)
        dot_t[...] = do_ref[...].astype(f32).T

    v = v_ref[...]
    vb[:, 0:128] = jnp.where((lane // HDIM) == h, v, jnp.zeros_like(v))
    span = pl.ds(pl.multiple_of(h * HDIM, HDIM), HDIM)
    part = dot_t[span] * linv_ref[0, 0:1, :]
    inner = -jnp.sum(part * o_ref[...], axis=0, keepdims=True)
    high = inner.astype(bf16).astype(f32)
    row = iota((8, tokens), 0)
    ext = jnp.where(row == 0, high, jnp.where(row == 1, inner - high, 0.0))
    wide = jnp.concatenate([part, part, part, part, ext, jnp.zeros((120, tokens), f32)], axis=0)
    dox[...] = wide.T.astype(bf16)
    partb[...] = part.astype(bf16)
    pieces = 2
    block = tokens // pieces
    for j in range(pieces):
        cols = slice(j * block, (j + 1) * block)
        dp = lax.dot_general(dox[cols], vb[...], NT, preferred_element_type=f32)
        e = e_ref[0, cols]
        ds = (e.astype(f32) * dp).astype(bf16)
        dqt[span, cols] = lax.dot_general(kt[span], ds, NT, preferred_element_type=f32)
        kk = jnp.dot(qt[span, cols], ds, preferred_element_type=f32)
        vv = jnp.dot(partb[:, cols], e, preferred_element_type=f32)
        if j == 0:
            dkt[span] = kk
            dvt[span] = vv
            poll(2 * n + 1)
        else:
            dkt[span] += kk
            dvt[span] += vv

    def exchange(k):
        theirs = rows((1 - c) * half_keys, half_keys)
        return (
            remote(dk.at[k, theirs], dk_in.at[k], ssem.at[2 * k], rsem.at[2 * k], chip),
            remote(dv.at[k, theirs], dv_in.at[k], ssem.at[2 * k + 1], rsem.at[2 * k + 1], chip),
        )

    @pl.when(h == 3)
    def _():
        dq_ref[...] = (dqt[...].T * HDIM ** (-0.5)).astype(bf16)
        dk[g] = (dkt[...] * (1.0 / LOG2E)).T.astype(bf16)
        dv[g] = dvt[...].T.astype(bf16)
        for copy in exchange(g):
            copy.start()

    @pl.when(n == last)
    def _():
        mine = rows(c * half_keys, half_keys)
        for tick in range(ticks, when[stages] + period * (count - 1) + 1):
            for s in range(stages, -1, -1):
                late = tick - when[s]
                if late >= 0 and late % period == 0 and late // period < count:
                    run(s, late // period)
        give = pltpu.make_async_copy(total, total_out, lsem.at[1])
        give.start()
        for k in range(4):
            for copy in exchange(k):
                copy.wait()
            lanes = slice(k * 128, (k + 1) * 128)
            dk_out[:, lanes] = (dk[k, mine].astype(f32) + dk_in[k].astype(f32)).astype(bf16)
            dv_out[:, lanes] = (dv[k, mine].astype(f32) + dv_in[k].astype(f32)).astype(bf16)
        act_far().wait()
        act_own().wait()
        give.wait()


def attend_back(cubes, q, k, v, do, ot, linv, e, act, grads):
    tokens, model = q.shape
    keys = k.shape[0]
    depth, width = grads.shape[1:]
    chunk = 16 * cubes
    sds = jax.ShapeDtypeStruct

    def cols(size):
        return pl.BlockSpec((size, 128), lambda n: (0, n // 4))

    fixed = pl.BlockSpec((tokens, model), lambda n: (0, 0))
    return pl.pallas_call(
        functools.partial(backward_kernel, cubes, chunk),
        name="attend_back",
        grid=(HEADS,),
        in_specs=[
            cols(tokens), cols(keys), cols(keys), cols(tokens),
            pl.BlockSpec((HDIM, tokens), lambda n: (n, 0)),
            pl.BlockSpec((1, 8, tokens), lambda n: (n, 0, 0)),
            pl.BlockSpec((1, tokens, keys), lambda n: (n, 0, 0)),
            ANY,
            VM,
        ],
        out_specs=[cols(tokens), fixed, fixed, ANY, ANY],
        out_shape=[
            sds((tokens, model), bf16),
            sds((tokens, model), bf16),
            sds((tokens, model), bf16),
            sds(act.shape, bf16),
            sds((depth, width), bf16),
        ],
        scratch_shapes=[
            pltpu.VMEM((keys, 256), bf16),
            pltpu.VMEM((128, keys), bf16),
            pltpu.VMEM((128, tokens), bf16),
            pltpu.VMEM((128, tokens), f32),
            pltpu.VMEM((tokens, 256), bf16),
            pltpu.VMEM((HDIM, tokens), bf16),
            pltpu.VMEM((128, tokens), f32),
            pltpu.VMEM((128, keys), f32),
            pltpu.VMEM((128, keys), f32),
            pltpu.VMEM((4, keys, 128), bf16),
            pltpu.VMEM((4, keys, 128), bf16),
            pltpu.VMEM((4, tokens, 128), bf16),
            pltpu.VMEM((4, tokens, 128), bf16),
            pltpu.SemaphoreType.DMA((2,)),
            pltpu.SemaphoreType.DMA((9,)),
            pltpu.SemaphoreType.DMA((9,)),
            pltpu.VMEM((depth, width), bf16),
        ] + reducer_scratch(cubes, depth // chunk, depth, width),
        compiler_params=params(2),
    )(q, k, v, do, ot, linv, e, act, grads)


def project_back_kernel(
    cubes, chunk,
    dq, dk, dv, first_in, embedded, grad_middle, qkvw, embw, enc, tgt, vecf, sums,
    total, vis_out,
    grads, first_t, vgrad, vis_in, lsem, vs, vr, got_core, got_y, work, *rest,
):
    gots, (rs, rr) = rest[:-2], rest[-2:]
    cube, b, y, c = place()
    chip, across, diag = peers()
    bits = cubes.bit_length() - 1
    tokens, model = first_in.shape
    half = tokens // 2
    slots = enc.shape[0]
    er = embw.shape[0] // 4
    qr = model // 4
    run, stages = reducer(cubes, chunk, grads, got_core, got_y, work, gots, total, rs, rr)
    count = grads.shape[1] // chunk
    early = 3 * qr // chunk
    greet((chip, across, diag) + tuple(mate_of(k) for k in range(bits)))

    first_t[...] = first_in[...].astype(f32).T.astype(bf16)
    psums = []
    for k, part in enumerate((dq, dk, dv)):
        term = jnp.dot(first_t[...], part[...], preferred_element_type=f32).astype(bf16)
        for d in range(4):
            grads[d, k * qr : (k + 1) * qr] = term[d * qr : (d + 1) * qr]
        if (k + 1) * qr % chunk == 0 and qr == chunk:
            run(0, k)
    if qr != chunk:
        for t in range(early):
            run(0, t)
    qsum = jnp.sum(dq[...].astype(f32), axis=0, keepdims=True)
    vsum = jnp.sum(dv[...].astype(f32), axis=0, keepdims=True)
    (gain,) = unpack(vecf, ((2, 1, ALL),))
    target = tgt[...].astype(f32)
    column = target.T[:, 0:1].astype(jnp.int32)
    gsum = [jnp.zeros((1, model), f32)] * 3
    lifted = None
    for h in range(2):
        span = pl.ds(h * half, half)
        gf = lax.dot_general(dq[span], qkvw[:, 0:model], NT, preferred_element_type=f32)
        gf += lax.dot_general(dk[span], qkvw[:, model : 2 * model], NT, preferred_element_type=f32)
        gf += lax.dot_general(dv[span], qkvw[:, 2 * model :], NT, preferred_element_type=f32)
        for t in range(early):
            run(1 + h, t)
        value = embedded[span]
        center = value - jnp.mean(value, axis=-1, keepdims=True)
        rstd = lax.rsqrt(jnp.mean(center * center, axis=-1, keepdims=True) + EPS)
        normed = center * rstd
        gsum[0] += jnp.sum(gf * normed, axis=0, keepdims=True)
        gsum[1] += jnp.sum(gf, axis=0, keepdims=True)
        gn = gf * gain
        back = rstd * (
            gn - jnp.mean(gn, axis=-1, keepdims=True) - normed * jnp.mean(gn * normed, axis=-1, keepdims=True)
        )
        ge = grad_middle[span] + back
        offset = y * half + h * 2 * half
        hit = (iota((half, slots), 0) + offset == tgt[0:1]).astype(f32)
        flag = jnp.sum(hit, axis=1, keepdims=True)
        gsum[2] += jnp.sum((1.0 - flag) * ge, axis=0, keepdims=True)
        hit_t = (iota((slots, half), 1) + offset == column).astype(bf16)
        term = jnp.dot(hit_t, ge.astype(bf16), preferred_element_type=f32)
        lifted = term if lifted is None else lifted + term
    bsum = jnp.sum(lifted, axis=0, keepdims=True)
    low = lifted.astype(bf16)
    vgrad[...] = (
        lax.dot_general(low, embw[...], NT, preferred_element_type=f32).astype(bf16).reshape(vgrad.shape)
    )
    vis_copies = [
        remote(vgrad.at[2 * (1 - y) + c], vis_in.at[y, :, c], vs.at[0], vr.at[0], across),
        remote(vgrad.at[2 * (1 - y) + 1 - c], vis_in.at[y, :, c], vs.at[1], vr.at[1], diag),
        remote(vgrad.at[2 * y + 1 - c], vis_in.at[y, :, c], vs.at[2], vr.at[2], chip),
        pltpu.make_async_copy(vgrad.at[b], vis_in.at[y, :, c], lsem.at[0]),
    ]
    at = 3 * qr
    gemb = jnp.dot(enc[...].astype(f32).T.astype(bf16), low, preferred_element_type=f32).astype(bf16)
    for d in range(4):
        grads[d, at : at + er] = gemb[d * er : (d + 1) * er]

    def lanes(value, d, size=128):
        return value[:, d * size : (d + 1) * size]

    down_s, out_s, gain_s, bias_s = (sums[k : k + 1] for k in range(4))
    pad = grads.shape[1] - at - er
    for d in range(4):
        part = qsum if d < 2 else vsum
        blank = jnp.zeros((1, model // 2), f32)
        packed = [
            jnp.concatenate([lanes(bsum, d), lanes(gsum[2], d), lanes(gsum[0], d), lanes(gsum[1], d)], axis=1),
            jnp.concatenate([lanes(part, d % 2, 256), lanes(out_s, d), lanes(gain_s, d)], axis=1),
            sums[4 + d : 5 + d],
            jnp.concatenate([lanes(bias_s, d), lanes(down_s, d), blank], axis=1),
        ]
        packed = jnp.concatenate(packed + [jnp.zeros((pad - 4, model), f32)], axis=0)
        grads[d, at + er :] = packed.astype(bf16)
    for t in range(early, count):
        run(0, t)
    for copy in vis_copies:
        copy.start()
    for t in range(early):
        run(3, t)
    for t in range(early, count):
        run(1, t)
    for t in range(early):
        run(4, t)
    for t in range(early):
        run(5, t)
    for step in range(2, stages + 1):
        for t in range(early, count):
            run(step, t)
        if step + 4 <= stages:
            for t in range(early):
                run(step + 4, t)
    for copy in vis_copies:
        copy.wait()
    vis_out[...] = vis_in[0] + vis_in[1]


def project_back(cubes, dq, dk, dv, first_in, embedded, grad_middle, qkvw, embw, enc, tgt, vecf, sums, cap):
    tokens, model = first_in.shape
    chunk = 16 * cubes
    depth = 3 * model // 4 + embw.shape[0] // 4 + 16
    depth = depth + -depth % chunk
    enc_width = enc.shape[1]
    slots = enc.shape[0]
    sds = jax.ShapeDtypeStruct
    return pl.pallas_call(
        functools.partial(project_back_kernel, cubes, chunk),
        name="project_back",
        out_shape=(sds((depth, model), bf16), sds((2, 2, cap, enc_width), bf16)),
        in_specs=[VM] * 12,
        out_specs=(VM, VM),
        scratch_shapes=[
            pltpu.VMEM((4, depth, model), bf16),
            pltpu.VMEM((model, tokens), bf16),
            pltpu.VMEM((4, 2, cap, enc_width), bf16),
            pltpu.VMEM((2, 2, 2, cap, enc_width), bf16),
            pltpu.SemaphoreType.DMA((1,)),
            pltpu.SemaphoreType.DMA((3,)),
            pltpu.SemaphoreType.DMA((3,)),
        ] + reducer_scratch(cubes, depth // chunk, depth, model),
        compiler_params=params(3),
    )(dq, dk, dv, first_in, embedded, grad_middle, qkvw, embw, enc, tgt, vecf, sums)


def finish_kernel(first, second, down, up, out, qkv, emb, *vectors):
    model = down.shape[1]
    parts = up.shape[1] // model
    size = up.shape[0]
    down[...] = first[0:model].astype(f32).T
    for k in range(parts):
        up[:, k * model : (k + 1) * model] = first[model + k * size : model + (k + 1) * size].astype(f32)
    at = model + parts * size
    out[...] = first[at : at + size].astype(f32)
    for k in range(3):
        qkv[:, k * model : (k + 1) * model] = second[k * size : (k + 1) * size].astype(f32)
    at = 3 * size
    er = emb.shape[0]
    emb[...] = second[at : at + er].astype(f32)
    packed = second[at + er : at + er + 16].astype(f32)
    pieces = iter(vectors)
    for row, widths in enumerate(((128, 128, 128, 128), (256, 128, 128), (512,), (128, 128))):
        lane = 0
        for width in widths:
            next(pieces)[...] = packed[row : row + 1, lane : lane + width]
            lane += width


def finish(first, second, shapes):
    sds = jax.ShapeDtypeStruct
    widths = (128, 128, 128, 128, 256, 128, 128, 512, 128, 128)
    return pl.pallas_call(
        finish_kernel,
        name="results",
        out_shape=tuple(sds(s, f32) for s in shapes) + tuple(sds((1, w), f32) for w in widths),
        in_specs=[VM, VM],
        out_specs=tuple([VM] * (len(shapes) + len(widths))),
        compiler_params=params(),
    )(first, second)


def shards(
    cubes,
    visible, kept_rows, slot_counts, patches, positions, embedder, embedbias, masktoken, attngain, attnbias,
    qkvproj, qvbias, outproj, outbias, mlpgain, mlpbias, upproj, upbias, downproj, downbias, cotangent,
):
    cells = cotangent.shape[1]
    cap, enc_width = visible.shape[2:]
    _, b, _, _ = place()
    slot = jnp.arange(cap, dtype=jnp.int32)
    live = jnp.where(slot[None, :] < slot_counts[0][:, None], kept_rows[0], -1)
    code = jnp.where(live >= 0, live + 2 * cells * (jnp.arange(4, dtype=jnp.int32)[:, None] // 2), -1)
    code = jnp.moveaxis(code.reshape(2, 2, cap), 1, 0).reshape(2, 1, 2 * cap)
    source = jnp.arange(4, dtype=jnp.int32)[None, :, None]
    kept = jnp.where(source == b, code, -1).reshape(2, 1, 8 * cap)
    kept = jnp.broadcast_to(kept, (2, 8, 8 * cap))
    vis = visible.reshape(2, 2, cap, enc_width)
    vecs = [
        m.reshape(-1, 128)
        for m in (embedbias, masktoken, attngain, attnbias, qvbias, outbias, mlpgain, mlpbias, upbias, downbias)
    ]
    embedded, first_in, q, k, v, emb_full, qkv_full, enc, target, vecf = embed(
        vis, kept, embedder, qkvproj, positions, vecs
    )
    own = (outproj, upproj, downproj, cotangent)
    e, ot, linv, mixed, *gathered = attend(patches, q, k, v, *own)
    act, grads, grad_middle, grad_mixed, sums = mlp(patches, vecf, mixed, embedded, gathered, own)
    dq, dk, dv, activations, first = attend_back(cubes, q, k, v, grad_mixed, ot, linv, e, act, grads)
    second, visible_grad = project_back(
        cubes, dq, dk, dv, first_in, embedded, grad_middle, qkv_full, emb_full, enc, target, vecf, sums, cap
    )
    shapes = (downproj.shape, upproj.shape, outproj.shape, qkvproj.shape, embedder.shape)
    down_o, up_o, out_o, qkv_o, emb_o, *small = finish(first, second, shapes)
    ebias, mask, again, abias, qv, outb, mgain, upb, mbias, downb = (m.reshape(-1) for m in small)
    return (
        activations, visible_grad.reshape(visible.shape), emb_o, ebias, mask, again, abias, qkv_o, qv,
        out_o, outb, mgain, mbias, up_o, upb, down_o, downb,
    )


def solution(mesh):
    cubes = mesh.shape["cube"]
    split = P(("cube", "band"), None, None, None)
    mat, row = P("band", None), P("band")
    placed = (
        split, P(("cube", "band"), None, None), P(("cube", "band"), None), P("cube"), mat,
        mat, row, row, row, row, mat, row, mat, row, row, row, mat, row, mat, row, P("cube", "band", None),
    )
    return jax.shard_map(
        functools.partial(shards, cubes),
        mesh=mesh,
        in_specs=placed,
        out_specs=(
            P("cube", "band", None), split, mat, row, row, row, row, mat, row, mat, row, row, row, mat, row, mat, row,
        ),
        check_vma=False,
    )
```

```python
import functools

import jax
import jax.numpy as jnp
from jax import lax
from jax.experimental import pallas as pl
from jax.experimental.pallas import tpu as pltpu
from jax.sharding import PartitionSpec as P

HEADS = 16
LATE_CHUNKS = 1
SIDE_CHUNKS = 2
HDIM = 32
EPS = 1e-06
LOG2E = 1.4426950408889634
QSCALE = HDIM ** (-0.5) * LOG2E
MESH = pl.DeviceIdType.MESH
NT = (((1,), (1,)), ((), ()))
f32 = jnp.float32
bf16 = jnp.bfloat16
ANY = pl.BlockSpec(memory_space=pl.ANY)
VM = pl.BlockSpec(memory_space=pltpu.VMEM)
VMEM_LIMIT = 60 * 2**20


def iota(shape, dim):
    return lax.broadcasted_iota(jnp.int32, shape, dim)


def normalize(values):
    center = values - jnp.mean(values, axis=-1, keepdims=True)
    spread = jnp.mean(center * center, axis=-1, keepdims=True)
    return center * lax.rsqrt(spread + EPS)


def place():
    cube, band = lax.axis_index("cube"), lax.axis_index("band")
    y, c = band // 2, band % 2
    return cube, band, y, c


def peers():
    cube, band, y, c = place()
    same_chip = (cube, 2 * y + 1 - c)
    across = (cube, 2 * (1 - y) + c)
    diagonal = (cube, 2 * (1 - y) + 1 - c)
    return same_chip, across, diagonal


def greet(devices):
    barrier = pltpu.get_barrier_semaphore()
    for device in devices:
        pl.semaphore_signal(barrier, inc=1, device_id=device, device_id_type=MESH)
    pl.semaphore_wait(barrier, len(devices))


def remote(src, dst, send, recv, device):
    return pltpu.make_async_remote_copy(
        src_ref=src, dst_ref=dst, send_sem=send, recv_sem=recv, device_id=device, device_id_type=MESH
    )


def rows(start, size):
    return pl.ds(pl.multiple_of(start, 16), size)


def params(collective_id=None):
    if collective_id is None:
        return pltpu.CompilerParams(vmem_limit_bytes=VMEM_LIMIT)
    return pltpu.CompilerParams(collective_id=collective_id, has_side_effects=True, vmem_limit_bytes=VMEM_LIMIT)


def mate_of(k):
    cube, b, _, _ = place()
    d = 1 << k
    return (cube + d - 2 * d * ((cube // d) % 2), b)


def unpack(vecf, spans):
    vectors = vecf[...].astype(f32)
    out = []
    for first, count, bands in spans:
        out.append(
            jnp.concatenate([vectors[d, k : k + 1] for d in bands for k in range(first, first + count)], axis=1)
        )
    return out


ALL = (0, 1, 2, 3)


def embed_kernel(
    vis, kept, emb, qkv, pos, *refs,
):
    vecs = refs[:10]
    (embedded, first_in, q_out, k_out, v_out, emb_out, qkv_out, enc_out, tgt_out, vecf,
     enc, tgt, embf, qkvf, posf, vec, kbuf, vbuf, lsem, ssem, rsem) = refs[10:]
    cube, b, y, c = place()
    x = cube % 2
    chip, across, diag = peers()
    mate = mate_of(0)
    bq = 2 * (1 - y) + c
    er, qr = emb.shape[0], qkv.shape[0]
    half = pos.shape[0]
    model = emb.shape[1]
    fill = jnp.zeros((vec.shape[0] - sum(v.shape[0] for v in vecs), 128), f32)
    vec[...] = jnp.concatenate([v[...].astype(f32) for v in vecs] + [fill], axis=0).astype(bf16)
    greet((chip, across, diag, mate))

    used = [0]
    local = []

    def send(src, dst, device):
        copy = remote(src, dst, ssem.at[used[0]], rsem.at[used[0]], device)
        used[0] += 1
        copy.start()
        return copy

    def keep(src, dst):
        copy = pltpu.make_async_copy(src, dst, lsem.at[len(local)])
        copy.start()
        local.append(copy)

    def cut(start, size, which):
        return rows(start + which * (size // 2), size // 2)

    ea, qa = rows(b * er, er), rows(b * qr, qr)
    far_vec = send(vec, vecf.at[b], across)
    small = [
        send(kept.at[c], tgt.at[b], across),
        send(vis.at[:, c], enc.at[b], across),
        send(kept.at[1 - c], tgt.at[b], diag),
        send(vis.at[:, 1 - c], enc.at[b], diag),
        send(kept.at[1 - c], tgt.at[b], chip),
        send(vec, vecf.at[b], chip),
        send(vis.at[:, 1 - c], enc.at[b], chip),
        send(emb, embf.at[ea], chip),
    ]
    far_emb = send(emb.at[cut(0, er, x)], embf.at[cut(b * er, er, x)], across)
    far_pos = send(pos.at[cut(0, half, x)], posf.at[y, cut(0, half, x)], across)
    far_qkv = send(qkv.at[cut(0, qr, x)], qkvf.at[cut(b * qr, qr, x)], across)
    near_qkv = send(qkv, qkvf.at[qa], chip)
    keep(kept.at[c], tgt.at[b])
    keep(vec, vecf.at[b])
    keep(vis.at[:, c], enc.at[b])
    keep(emb, embf.at[ea])
    keep(pos, posf.at[y])
    keep(qkv, qkvf.at[qa])

    far_vec.wait()
    relays = [send(vecf.at[bq], vecf.at[bq], chip)]
    far_emb.wait()
    got = cut(bq * er, er, x)
    side_emb = send(embf.at[got], embf.at[got], mate)
    relays.append(send(embf.at[got], embf.at[got], chip))
    far_pos.wait()
    got = cut(0, half, x)
    side_pos = send(posf.at[1 - y, got], posf.at[1 - y, got], mate)
    side_emb.wait()
    got = cut(bq * er, er, 1 - x)
    relays.append(send(embf.at[got], embf.at[got], chip))
    far_qkv.wait()
    got = cut(bq * qr, qr, x)
    side_qkv = send(qkvf.at[got], qkvf.at[got], mate)
    late = [send(qkvf.at[got], qkvf.at[got], chip)]
    for copy in small + local + relays:
        copy.wait()
    side_pos.wait()

    target = jnp.max(tgt[...].astype(f32), axis=0)[0:1].astype(jnp.int32)
    tgt_out[...] = jnp.broadcast_to(target, tgt_out.shape)
    enc_all = enc[...].reshape(enc_out.shape)
    enc_out[...] = enc_all
    embedbias, mask, gain, bias, qbias, vbias = unpack(
        vecf, ((0, 1, ALL), (1, 1, ALL), (2, 1, ALL), (3, 1, ALL), (4, 2, (0, 1)), (4, 2, (2, 3)))
    )
    slots = enc_out.shape[0]

    def lift(h):
        span = pl.ds(h * half, half)
        cells = iota((half, slots), 0) + (y * half + h * 2 * half)
        hit = (cells == target).astype(f32)
        flag = jnp.sum(hit, axis=1, keepdims=True)
        picked = jnp.dot(hit.astype(bf16), enc_all, preferred_element_type=f32).astype(bf16)
        rows_in = jnp.dot(picked, embf[...], preferred_element_type=f32)
        v = rows_in + flag * embedbias + (1.0 - flag) * mask + posf[h].astype(f32)
        embedded[span] = v
        first_in[span] = (normalize(v) * gain + bias).astype(bf16)

    lift(0)
    lift(1)
    emb_out[...] = embf[...]
    side_qkv.wait()
    got = cut(bq * qr, qr, 1 - x)
    late.append(send(qkvf.at[got], qkvf.at[got], chip))
    near_qkv.wait()
    for copy in late:
        copy.wait()
    mine = rows(c * 2 * half, 2 * half)
    k = jnp.dot(first_in[...], qkvf[:, model : 2 * model], preferred_element_type=f32)
    kbuf[...] = k.astype(bf16)
    out = [send(kbuf, k_out.at[mine], chip)]
    v = jnp.dot(first_in[...], qkvf[:, 2 * model :], preferred_element_type=f32)
    vbuf[...] = (v + vbias).astype(bf16)
    out.append(send(vbuf, v_out.at[mine], chip))
    first_local = len(local)
    keep(kbuf, k_out.at[mine])
    keep(vbuf, v_out.at[mine])
    q = jnp.dot(first_in[...], qkvf[:, :model], preferred_element_type=f32)
    q_out[...] = ((q + qbias) * QSCALE).astype(bf16)
    qkv_out[...] = qkvf[...]
    for copy in out + local[first_local:]:
        copy.wait()


def embed(vis, kept, emb, qkv, pos, vecs):
    er, model = emb.shape
    qr, wide = qkv.shape
    half = pos.shape[0]
    enc_width = vis.shape[-1]
    cap = vis.shape[2]
    slots = 8 * cap
    tokens = 2 * half
    sds = jax.ShapeDtypeStruct
    return pl.pallas_call(
        embed_kernel,
        name="embed_project",
        out_shape=(
            sds((tokens, model), f32),
            sds((tokens, model), bf16),
            sds((tokens, model), bf16),
            sds((2 * tokens, model), bf16),
            sds((2 * tokens, model), bf16),
            sds((4 * er, model), bf16),
            sds((4 * qr, wide), bf16),
            sds((slots, enc_width), bf16),
            sds((8, slots), jnp.int32),
            sds((4, 16, 128), bf16),
        ),
        in_specs=[ANY] * 5 + [VM] * 10,
        out_specs=(VM, VM, VM, ANY, ANY, VM, VM, VM, VM, VM),
        scratch_shapes=[
            pltpu.VMEM((4, 2, cap, enc_width), bf16),
            pltpu.VMEM((4, 8, slots), jnp.int32),
            pltpu.VMEM((4 * er, model), bf16),
            pltpu.VMEM((4 * qr, wide), bf16),
            pltpu.VMEM((2, half, model), bf16),
            pltpu.VMEM((16, 128), bf16),
            pltpu.VMEM((tokens, model), bf16),
            pltpu.VMEM((tokens, model), bf16),
            pltpu.SemaphoreType.DMA((8,)),
            pltpu.SemaphoreType.DMA((24,)),
            pltpu.SemaphoreType.DMA((24,)),
        ],
        compiler_params=params(0),
    )(vis, kept, emb, qkv, pos, *vecs)


def forward_kernel(
    patch, q_ref, k_ref, v_ref, outw, upw, downw, cot,
    e_ref, o_ref, linv_ref, mix_ref, out_full, up_full, down_full, cot_full,
    kxa, kxb, vt, sa, sb, ots, ssem, rsem,
):
    p = pl.program_id(0)
    last = pl.num_programs(0) - 1
    cube, b, y, c = place()
    x = cube % 2
    chip, across, _ = peers()
    mate = mate_of(0)
    bq = 2 * (1 - y) + c
    shards = ((upw, up_full), (outw, out_full), (downw, down_full))

    def cut(k, band, which):
        size = shards[k][0].shape[0]
        return rows(band * size + which * (size // 2), size // 2)

    def far(k):
        size = shards[k][0].shape[0]
        part = rows(x * (size // 2), size // 2)
        return remote(shards[k][0].at[part], shards[k][1].at[cut(k, b, x)], ssem.at[k], rsem.at[k], across)

    def near(k):
        size = shards[k][0].shape[0]
        return remote(shards[k][0], shards[k][1].at[rows(b * size, size)], ssem.at[3 + k], rsem.at[3 + k], chip)

    def side(k):
        ref = shards[k][1].at[cut(k, bq, x)]
        return remote(ref, ref, ssem.at[6 + k], rsem.at[6 + k], mate)

    def relay(k, which):
        ref = shards[k][1].at[cut(k, bq, x if which == 0 else 1 - x)]
        at = 9 + 2 * k + which
        return remote(ref, ref, ssem.at[at], rsem.at[at], chip)

    def cot_far():
        return remote(cot.at[1 - y], cot_full, ssem.at[15], rsem.at[15], across)

    @pl.when(p == 0)
    def _():
        greet((chip, across, mate))
        far(0).start()
        far(1).start()
        far(2).start()
        cot_far().start()
        for k in range(3):
            near(k).start()

    for k, at in ((0, 2), (1, 3), (2, 4)):

        @pl.when(p == at)
        def _(k=k):
            far(k).wait()
            side(k).start()
            relay(k, 0).start()

    for k, at in ((0, 5), (1, 6), (2, 7)):

        @pl.when(p == at)
        def _(k=k):
            side(k).wait()
            relay(k, 1).start()

    keys = k_ref.shape[0]
    tokens = q_ref.shape[0]
    lane = iota((keys, 128), 1)
    pieces = 3
    block = tokens // pieces

    @pl.when(p == 0)
    def _():
        row = iota((keys, 128), 0)
        bias = jnp.where((row % cot.shape[1] >= patch[y]) & (lane == 0), -1e30, 0.0).astype(bf16)
        kxa[:, 128:256] = bias
        kxb[:, 128:256] = bias
        for g in range(v_ref.shape[1] // 128):
            cols = slice(g * 128, (g + 1) * 128)
            vt[cols] = v_ref[:, cols].astype(f32).T.astype(bf16)

    def lanes(h):
        return pl.ds(pl.multiple_of((h // 4) * 128, 128), 128)

    def prepare(h, kx):
        k = k_ref[:, lanes(h)]
        kx[:, 0:128] = jnp.where((lane // HDIM) == (h % 4), k, jnp.zeros_like(k))

    def score(h, kx, s, j):
        span = slice(j * block, (j + 1) * block)
        qx = jnp.concatenate([q_ref[span, lanes(h)], jnp.ones((block, 128), bf16)], axis=1)
        s[span] = lax.dot_general(qx, kx[...], NT, preferred_element_type=f32)

    ones = jnp.ones((16, keys), bf16)

    def soften(at, h, s, j):
        span = slice(j * block, (j + 1) * block)
        v = s[span]
        e = jnp.exp2(v - jnp.max(v, axis=1, keepdims=True)).astype(bf16)
        e_ref[at, span] = e
        lhs = jnp.concatenate([vt[pl.ds(pl.multiple_of(h * HDIM, HDIM), HDIM)], ones], axis=0)
        ot = lax.dot_general(lhs, e, NT, preferred_element_type=f32)
        li = 1.0 / ot[HDIM : HDIM + 8]
        o = ot[:HDIM] * li[0:1]
        o_ref[at * HDIM : (at + 1) * HDIM, span] = o
        ots[pl.ds(pl.multiple_of((p % 2) * 2 * HDIM + at * HDIM, HDIM), HDIM), span] = o
        linv_ref[at, :, span] = li

    @pl.when(p == 0)
    def _():
        prepare(0, kxa)
        for j in range(pieces):
            score(0, kxa, sa, j)

    after = jnp.minimum(2 * p + 2, 2 * last + 1)
    prepare(2 * p + 1, kxb)
    for j in range(pieces):
        score(2 * p + 1, kxb, sb, j)
        soften(0, 2 * p, sa, j)
    prepare(after, kxa)
    for j in range(pieces):
        score(after, kxa, sa, j)
        soften(1, 2 * p + 1, sb, j)

    @pl.when(p % 2 == 1)
    def _():
        mix_ref[...] = ots[...].T.astype(bf16)

    @pl.when(p == last)
    def _():
        cot_far().wait()
        for k in range(3):
            near(k).wait()
            relay(k, 0).wait()
            relay(k, 1).wait()


def attend(patch, q, k, v, outw, upw, downw, cot):
    tokens, model = q.shape
    keys = k.shape[0]
    sds = jax.ShapeDtypeStruct

    def fixed(shape):
        return pl.BlockSpec(shape, lambda p: (0, 0))

    return pl.pallas_call(
        forward_kernel,
        name="attend",
        grid=(HEADS // 2,),
        in_specs=[
            pl.BlockSpec(memory_space=pltpu.SMEM),
            fixed(q.shape),
            fixed(k.shape),
            fixed(v.shape),
            ANY, ANY, ANY, ANY,
        ],
        out_specs=[
            pl.BlockSpec((2, tokens, keys), lambda p: (p, 0, 0)),
            pl.BlockSpec((2 * HDIM, tokens), lambda p: (p, 0)),
            pl.BlockSpec((2, 8, tokens), lambda p: (p, 0, 0)),
            pl.BlockSpec((tokens, 128), lambda p: (0, p // 2)),
            ANY, ANY, ANY, ANY,
        ],
        out_shape=[
            sds((HEADS, tokens, keys), bf16),
            sds((model, tokens), f32),
            sds((HEADS, 8, tokens), f32),
            sds((tokens, model), bf16),
            sds((4 * outw.shape[0], outw.shape[1]), bf16),
            sds((4 * upw.shape[0], upw.shape[1]), bf16),
            sds((4 * downw.shape[0], downw.shape[1]), bf16),
            sds(cot.shape[1:], bf16),
        ],
        scratch_shapes=[
            pltpu.VMEM((keys, 256), bf16),
            pltpu.VMEM((keys, 256), bf16),
            pltpu.VMEM((model, keys), bf16),
            pltpu.VMEM((tokens, keys), f32),
            pltpu.VMEM((tokens, keys), f32),
            pltpu.VMEM((128, tokens), f32),
            pltpu.SemaphoreType.DMA((16,)),
            pltpu.SemaphoreType.DMA((16,)),
        ],
        compiler_params=params(1),
    )(patch, q, k, v, outw, upw, downw, cot)


def mlp_kernel(
    patch, vecf, mixed, mixed_t, embedded, out_got, up_got, down_got, cot_got, out_own, up_own, down_own, cot_own,
    act, grads, grad_middle, grad_mixed, sums,
    outw, upf, downf, cot, second_t, gout_t, second, active, hid, branch_b, wsem,
):
    _, b, y, _ = place()
    tokens, model = mixed.shape
    half = tokens // 2
    wide = upf.shape[1]
    parts = wide // model
    loads = []

    def load(src, dst):
        copy = pltpu.make_async_copy(src, dst, wsem.at[len(loads)])
        copy.start()
        loads.append(copy)

    for own, got, full in ((out_own, out_got, outw), (up_own, up_got, upf), (down_own, down_got, downf)):
        size = own.shape[0]
        load(own, full.at[rows(b * size, size)])
        for k in range(1, 4):
            part = rows((b + k) % 4 * size, size)
            load(got.at[part], full.at[part])
    load(cot_own.at[y], cot.at[y])
    load(cot_got, cot.at[1 - y])
    vectors = vecf[...].astype(f32)

    def whole(k):
        return jnp.concatenate([vectors[d, k : k + 1] for d in range(4)], axis=1)

    outbias, gain, bias, downbias = whole(6), whole(7), whole(8), whole(13)
    upbias = [jnp.concatenate([vectors[d, 9 + k : 10 + k] for k in range(4)], axis=1) for d in range(parts)]
    live = iota((half, 1), 0) < patch[y]
    valid = jnp.where(live, 1.0, 0.0)
    total = [jnp.zeros((1, model), f32)] * (4 + parts)
    for copy in loads[:4]:
        copy.wait()
    for h in range(2):
        span = pl.ds(h * half, half)
        mix = mixed[span]
        middle = embedded[span] + (jnp.dot(mix, outw[...], preferred_element_type=f32) + outbias)
        center = middle - jnp.mean(middle, axis=-1, keepdims=True)
        rstd = lax.rsqrt(jnp.mean(center * center, axis=-1, keepdims=True) + EPS)
        normed = center * rstd
        sec = normed * gain + bias
        second_t[:, span] = sec.T.astype(bf16)
        sec = sec.astype(bf16)
        if h == 0:
            for copy in loads[4:]:
                copy.wait()
        gout = cot[h].astype(f32) * valid
        gout_t[:, span] = gout.T.astype(bf16)
        gout_b = gout.astype(bf16)
        total[0] += jnp.sum(gout, axis=0, keepdims=True)
        result = middle + downbias
        gsec = None
        for k in range(parts):
            cols = slice(k * model, (k + 1) * model)
            hidden = jnp.dot(sec, upf[:, cols], preferred_element_type=f32) + upbias[k]
            cdf = 0.5 + 0.5 * lax.erf(hidden * 0.7071067811865476)
            low = (hidden * cdf).astype(bf16)
            active[span, cols] = low
            slope = cdf + hidden * (0.3989422804014327 * jnp.exp(-0.5 * hidden * hidden))
            result += jnp.dot(low, downf[cols], preferred_element_type=f32)
            gact = lax.dot_general(gout_b, downf[cols], NT, preferred_element_type=f32)
            ghid = (gact * slope).astype(bf16)
            hid[span, cols] = ghid
            total[4 + k] += jnp.sum(ghid.astype(f32), axis=0, keepdims=True)
            term = lax.dot_general(ghid, upf[:, cols], NT, preferred_element_type=f32)
            gsec = term if gsec is None else gsec + term
        act[h] = (valid * result).astype(bf16)
        total[2] += jnp.sum(gsec * normed, axis=0, keepdims=True)
        total[3] += jnp.sum(gsec, axis=0, keepdims=True)
        gn = gsec * gain
        back = rstd * (
            gn - jnp.mean(gn, axis=-1, keepdims=True) - normed * jnp.mean(gn * normed, axis=-1, keepdims=True)
        )
        gmid = gout + back
        grad_middle[span] = gmid
        gb = gmid.astype(bf16)
        branch_b[span] = gb
        total[1] += jnp.sum(gb.astype(f32), axis=0, keepdims=True)
        grad_mixed[:, span] = lax.dot_general(outw[...], gb, NT, preferred_element_type=f32).astype(bf16)
    for k in range(parts):
        cols = slice(k * model, (k + 1) * model)
        grads[k, 0:model] = jnp.dot(gout_t[...], active[:, cols], preferred_element_type=f32).astype(bf16)
        gup = jnp.dot(second_t[...], hid[:, cols], preferred_element_type=f32).astype(bf16)
        size = model // 4
        for d in range(4):
            grads[d, model + k * size : model + (k + 1) * size] = gup[d * size : (d + 1) * size]
    base = model + parts * (model // 4)
    gout_w = jnp.dot(mixed_t[...].astype(bf16), branch_b[...], preferred_element_type=f32).astype(bf16)
    for d in range(4):
        grads[d, base : base + model // 4] = gout_w[d * (model // 4) : (d + 1) * (model // 4)]
    spare = grads.shape[1] - base - model // 4
    if spare:
        grads[:, base + model // 4 :] = jnp.zeros((4, spare, model), bf16)
    sums[...] = jnp.concatenate(total, axis=0)


def mlp(cubes, patch, vecf, mixed, mixed_t, embedded, gathered, own):
    tokens, model = mixed.shape
    outw, upw, downw, cot = own
    wide = upw.shape[1]
    half = cot.shape[1]
    depth = model + wide // 4 + model // 4
    depth += -depth % chunk_rows(cubes)
    sds = jax.ShapeDtypeStruct
    return pl.pallas_call(
        mlp_kernel,
        name="mlp_both",
        out_shape=(
            sds((2, half, model), bf16),
            sds((4, depth, model), bf16),
            sds((tokens, model), f32),
            sds((model, tokens), bf16),
            sds((4 + wide // model, model), f32),
        ),
        in_specs=[pl.BlockSpec(memory_space=pltpu.SMEM), VM, VM, VM, VM] + [ANY] * 8,
        out_specs=(VM, VM, VM, VM, VM),
        scratch_shapes=[
            pltpu.VMEM((model, model), bf16),
            pltpu.VMEM((model, wide), bf16),
            pltpu.VMEM((wide, model), bf16),
            pltpu.VMEM((2, half, model), bf16),
            pltpu.VMEM((model, tokens), bf16),
            pltpu.VMEM((model, tokens), bf16),
            pltpu.VMEM((tokens, model), bf16),
            pltpu.VMEM((tokens, wide), bf16),
            pltpu.VMEM((tokens, wide), bf16),
            pltpu.VMEM((tokens, model), bf16),
            pltpu.SemaphoreType.DMA((14,)),
        ],
        compiler_params=params(),
    )(patch, vecf, mixed, mixed_t, embedded, *gathered, *own)


def chunk_rows(cubes):
    return max(128, 8 * cubes)


def reducer(cubes, chunk, grads, mine, got_core, got_y, work, gots, total, ssem, rsem):
    cube, b, y, c = place()
    chip, across, _ = peers()
    bits = cubes.bit_length() - 1
    own, other = 2 * y + c, 2 * (1 - y) + c
    top = bits + 1

    def kept(k):
        start = 0
        for j in range(k):
            start = start + ((cube // (1 << j)) % 2) * (chunk >> (j + 1))
        return start

    def back(s, t):
        k = 2 * bits - s
        span = rows(t * chunk + kept(k + 1), chunk >> (k + 1))
        return total.at[span], total.at[span], mate_of(k)

    def core(t):
        span = rows(t * chunk, chunk)
        return [
            remote(grads.at[1 - c, span], got_core.at[0, span], ssem.at[t, 0], rsem.at[t, 0], chip),
            remote(grads.at[3 - c, span], got_core.at[1, span], ssem.at[t, 1], rsem.at[t, 1], chip),
        ]

    def step(k, t, both):
        side = pl.ds(0, 2) if both else pl.ds(0, 1)
        if k < bits - 1:
            size = chunk >> (k + 1)
            bit = (cube // (1 << k)) % 2
            away = rows(t * chunk + kept(k) + (1 - bit) * size, size)
        else:
            size = chunk >> k
            away = rows(t * chunk + kept(k), size)
        return work.at[side, away], gots[k].at[side, rows(t * size, size)], mate_of(k)

    def copies(s, t, side):
        if s == 0:
            return core(t)
        if not side:
            if s == 1:
                span = rows(t * chunk, chunk)
                move = work.at[1, span], got_y.at[span], across
            elif s <= top:
                move = step(s - 2, t, False)
            else:
                move = back(s, t)
        elif s < top:
            move = step(s - 1, t, True)
        elif s == top:
            size = chunk >> (bits - 1)
            span = rows(t * chunk + kept(bits - 1), size)
            move = work.at[1, span], got_y.at[span], across
        else:
            move = back(s, t)
        return [remote(move[0], move[1], ssem.at[t, s + 1], rsem.at[t, s + 1], move[2])]

    def run(s, t, side=False):
        if s > 0:
            for copy in copies(s - 1, t, side):
                copy.wait()
        span = rows(t * chunk, chunk)
        if s == 1:
            work[1, span] = mine(other, span) + got_core[1 - y, span]
            if side:
                work[0, span] = mine(own, span) + got_core[y, span]
        elif s == 2 and not side:
            work[0, span] = (mine(own, span) + got_core[y, span]) + got_y[span]
        elif 2 <= s <= top + 1:
            k = s - 2 if side else s - 3
            if side and s == top + 1:
                size = chunk >> (bits - 1)
                span = rows(t * chunk + kept(bits - 1), size)
                total[span] = work[0, span] + got_y[span]
            else:
                size = chunk >> min(k + 1, bits - 1)
                span = rows(t * chunk + kept(min(k + 1, bits - 1)), size)
                part = rows(t * size, size)
                if side:
                    work[:, span] = work[:, span] + gots[k][:, part]
                elif s <= top:
                    work[0, span] = work[0, span] + gots[k][0, part]
                else:
                    total[span] = work[0, span] + gots[k][0, part]
        if s < 1 + 2 * bits:
            for copy in copies(s, t, side):
                copy.start()

    return run, 1 + 2 * bits


def reducer_scratch(cubes, count, depth, width):
    bits = cubes.bit_length() - 1
    return [
        pltpu.VMEM((2, depth, width), bf16),
        pltpu.VMEM((depth, width), bf16),
        pltpu.VMEM((2, depth, width), bf16),
    ] + [pltpu.VMEM((2, depth >> min(k + 1, bits - 1), width), bf16) for k in range(bits)] + [
        pltpu.SemaphoreType.DMA((count, 2 + 2 * bits)),
        pltpu.SemaphoreType.DMA((count, 2 + 2 * bits)),
    ]


def backward_kernel(
    cubes, chunk,
    q_ref, k_ref, v_ref, do_ref, o_ref, linv_ref, e_ref, act, grads,
    dq_ref, dk_out, dv_out, act_full, total_out,
    vb, kt, qt, dox, dopb, dkt, dvt, dk, dv, dk_in, dv_in, lsem, ssem, rsem,
    total, terms, got_core, got_y, work, *rest,
):
    gots, (rs, rr) = rest[:-2], rest[-2:]
    n = pl.program_id(0)
    last = pl.num_programs(0) - 1
    h, g = n % 4, n // 4
    cube, b, y, c = place()
    chip, across, _ = peers()
    bits = cubes.bit_length() - 1
    keys = k_ref.shape[0]
    half_keys = keys // 2
    tokens = q_ref.shape[0]
    count = total.shape[0] // chunk

    def mine(d, span):
        return terms[d // 2, span]

    def term_copy(k):
        return pltpu.make_async_copy(grads.at[2 * k + c, pl.ds(0, count * chunk)], terms.at[k], lsem.at[2 + k])

    run, stages = reducer(cubes, chunk, grads, mine, got_core, got_y, work, gots, total, rs, rr)
    direct = count - SIDE_CHUNKS
    when = ([7, 11, 14, 18, 21, 25] + [28 + 3 * k for k in range(stages)])[: stages - 1]
    beside = ([2, 7, 11, 16, 19, 22, 26] + [29 + 3 * k for k in range(stages)])[:stages]
    polls = 2 * (last + 1)
    plan = [(at, s, 0, direct, False) for s, at in enumerate(when, 2)]
    plan += [(at, s, direct, SIDE_CHUNKS, True) for s, at in enumerate(beside, 1)]
    plan = sorted(plan, key=lambda entry: -entry[1])

    def poll(parity):
        @pl.when(2 * n + parity <= (direct + 1) // 2)
        def _():
            for u in range(2):
                t = 2 * (2 * n + parity - 1) + u

                @pl.when((t >= 0) & (t < direct))
                def _(t=t):
                    run(1, t)

        for at, s, first, size, side in plan:
            if at % 2 == parity and size:
                t = n - at // 2

                @pl.when((t >= 0) & (t < size))
                def _(s=s, t=t, first=first, side=side):
                    run(s, first + t, side)

    def act_far():
        return remote(act.at[1 - y], act_full.at[y], ssem.at[8], rsem.at[8], across)

    def act_own():
        return pltpu.make_async_copy(act.at[y], act_full.at[y], lsem.at[0])

    @pl.when(n == 0)
    def _():
        term_copy(0).start()
        term_copy(1).start()
        greet((chip, across) + tuple(mate_of(k) for k in range(bits)))
        for t in range(direct):
            run(0, t)
            if t < SIDE_CHUNKS:
                run(0, direct + t)
        act_own().start()
        term_copy(0).wait()
        term_copy(1).wait()

    @pl.when(n > 0)
    def _():
        poll(0)

    @pl.when(n == 9)
    def _():
        act_far().start()

    lane = iota((keys, 128), 1)

    @pl.when(h == 0)
    def _():
        kt[...] = k_ref[...].astype(f32).T.astype(bf16)
        qt[...] = q_ref[...].astype(f32).T.astype(bf16)
        parts, sums = [], []
        for k in range(4):
            span = slice(k * HDIM, (k + 1) * HDIM)
            part = do_ref[span].astype(f32) * linv_ref[k, 0:1, :]
            parts.append(part)
            sums.append(jnp.sum(part * o_ref[span], axis=0, keepdims=True))
        part = jnp.concatenate(parts, axis=0)
        dopb[...] = part.astype(bf16)
        dox[:, 0:128] = part.T.astype(bf16)
        inner = -jnp.concatenate(sums + [jnp.zeros((4, tokens), f32)], axis=0)
        high = inner.astype(bf16).astype(f32)
        ext = jnp.concatenate([high, inner - high, jnp.zeros((112, tokens), f32)], axis=0)
        dox[:, 128:256] = ext.T.astype(bf16)

    v = v_ref[...]
    vb[:, 0:128] = jnp.where((lane // HDIM) == h, v, jnp.zeros_like(v))
    vb[:, 128:256] = jnp.where((lane == h) | (lane == 8 + h), 1.0, 0.0).astype(bf16)
    span = pl.ds(pl.multiple_of(h * HDIM, HDIM), HDIM)
    pieces = 2
    block = tokens // pieces
    for j in range(pieces):
        cols = slice(j * block, (j + 1) * block)
        dp = lax.dot_general(dox[cols], vb[...], NT, preferred_element_type=f32)
        e = e_ref[0, cols]
        ds = (e.astype(f32) * dp).astype(bf16)
        dqt = lax.dot_general(kt[span], ds, NT, preferred_element_type=f32)
        dq_ref[:, cols] = (dqt * HDIM ** (-0.5)).astype(bf16)
        kk = jnp.dot(qt[span, cols], ds, preferred_element_type=f32)
        vv = jnp.dot(dopb[span, cols], e, preferred_element_type=f32)
        if j == 0:
            dkt[...] = kk
            dvt[...] = vv
            poll(1)
        else:
            dk[g, span] = ((dkt[...] + kk) * (1.0 / LOG2E)).astype(bf16)
            dv[g, span] = (dvt[...] + vv).astype(bf16)

    def exchange(k):
        theirs = pl.ds(pl.multiple_of((1 - c) * half_keys, 128), half_keys)
        return (
            remote(dk.at[k, :, theirs], dk_in.at[k], ssem.at[2 * k], rsem.at[2 * k], chip),
            remote(dv.at[k, :, theirs], dv_in.at[k], ssem.at[2 * k + 1], rsem.at[2 * k + 1], chip),
        )

    @pl.when(h == 3)
    def _():
        for copy in exchange(g):
            copy.start()

    @pl.when(n == last)
    def _():
        mine = pl.ds(pl.multiple_of(c * half_keys, 128), half_keys)
        for tick in range(polls, max(when[-1] + 2 * direct, beside[-1] + 2 * SIDE_CHUNKS)):
            for at, s, first, size, side in plan:
                late = tick - at
                if late >= 0 and late % 2 == 0 and late // 2 < size:
                    run(s, first + late // 2, side)
        give = pltpu.make_async_copy(total, total_out, lsem.at[1])
        give.start()
        for k in range(4):
            for copy in exchange(k):
                copy.wait()
            band = slice(k * 128, (k + 1) * 128)
            dk_out[band] = dk[k, :, mine] + dk_in[k]
            dv_out[band] = dv[k, :, mine] + dv_in[k]
        act_far().wait()
        act_own().wait()
        give.wait()


def attend_back(cubes, q, k, v, do, ot, linv, e, act, grads):
    tokens, model = q.shape
    keys = k.shape[0]
    width = grads.shape[2]
    chunk = chunk_rows(cubes)
    depth = grads.shape[1] - LATE_CHUNKS * chunk
    sds = jax.ShapeDtypeStruct

    def cols(size):
        return pl.BlockSpec((size, 128), lambda n: (0, n // 4))

    fixed = pl.BlockSpec((model, tokens), lambda n: (0, 0))
    return pl.pallas_call(
        functools.partial(backward_kernel, cubes, chunk),
        name="attend_back",
        grid=(HEADS,),
        in_specs=[
            cols(tokens), cols(keys), cols(keys),
            pl.BlockSpec((128, tokens), lambda n: (n // 4, 0)),
            pl.BlockSpec((128, tokens), lambda n: (n // 4, 0)),
            pl.BlockSpec((4, 8, tokens), lambda n: (n // 4, 0, 0)),
            pl.BlockSpec((1, tokens, keys), lambda n: (n, 0, 0)),
            ANY,
            ANY,
        ],
        out_specs=[pl.BlockSpec((HDIM, tokens), lambda n: (n, 0)), fixed, fixed, ANY, ANY],
        out_shape=[
            sds((model, tokens), bf16),
            sds((model, tokens), bf16),
            sds((model, tokens), bf16),
            sds(act.shape, bf16),
            sds((depth, width), bf16),
        ],
        scratch_shapes=[
            pltpu.VMEM((keys, 256), bf16),
            pltpu.VMEM((128, keys), bf16),
            pltpu.VMEM((128, tokens), bf16),
            pltpu.VMEM((tokens, 256), bf16),
            pltpu.VMEM((128, tokens), bf16),
            pltpu.VMEM((HDIM, keys), f32),
            pltpu.VMEM((HDIM, keys), f32),
            pltpu.VMEM((4, 128, keys), bf16),
            pltpu.VMEM((4, 128, keys), bf16),
            pltpu.VMEM((4, 128, tokens), bf16),
            pltpu.VMEM((4, 128, tokens), bf16),
            pltpu.SemaphoreType.DMA((4,)),
            pltpu.SemaphoreType.DMA((9,)),
            pltpu.SemaphoreType.DMA((9,)),
            pltpu.VMEM((depth, width), bf16),
            pltpu.VMEM((2, depth, width), bf16),
        ] + reducer_scratch(cubes, depth // chunk, depth, width),
        compiler_params=params(2),
    )(q, k, v, do, ot, linv, e, act, grads)


def project_back_kernel(
    cubes, chunk,
    dq, dk, dv, first_in, embedded, grad_middle, qkvw, embw, enc, tgt, vecf, sums, early,
    total, vis_out,
    grads, first_t, gft, vgrad, vis_in, lsem, vs, vr, got_core, got_y, work, *rest,
):
    gots, (rs, rr) = rest[:-2], rest[-2:]
    cube, b, y, c = place()
    chip, across, diag = peers()
    bits = cubes.bit_length() - 1
    tokens, model = first_in.shape
    half = tokens // 2
    slots = enc.shape[0]
    er = embw.shape[0] // 4
    qr = model // 4
    first = LATE_CHUNKS * chunk
    left = range(LATE_CHUNKS)
    count = grads.shape[1] // chunk
    middle = range(LATE_CHUNKS, LATE_CHUNKS + 3 * qr // chunk)
    final = range(LATE_CHUNKS + 3 * qr // chunk, count)

    def mine(d, span):
        return grads[d, span]

    run, stages = reducer(cubes, chunk, grads, mine, got_core, got_y, work, gots, total, rs, rr)

    def runs(s, chunks):
        for t in chunks:
            run(s, t, t in left)

    fetch = pltpu.make_async_copy(
        early.at[:, pl.ds(early.shape[1] - first, first)], grads.at[:, pl.ds(0, first)], lsem.at[1]
    ) if first else None
    if first:
        fetch.start()
    greeted = (chip, across, diag) + tuple(mate_of(k) for k in range(bits))
    barrier = pltpu.get_barrier_semaphore()
    for device in greeted:
        pl.semaphore_signal(barrier, inc=1, device_id=device, device_id_type=MESH)

    first_t[...] = first_in[...].astype(f32).T.astype(bf16)
    if first:
        fetch.wait()
    pl.semaphore_wait(barrier, len(greeted))
    runs(0, left)
    for k, part in enumerate((dq, dk, dv)):
        term = lax.dot_general(first_t[...], part[...], NT, preferred_element_type=f32).astype(bf16)
        for d in range(4):
            grads[d, first + k * qr : first + (k + 1) * qr] = term[d * qr : (d + 1) * qr]
        if k == 1:
            runs(1, left)
    runs(0, middle)
    ones = jnp.ones((8, tokens), bf16)
    qsum = lax.dot_general(ones, dq[...], NT, preferred_element_type=f32)[0:1]
    vsum = lax.dot_general(ones, dv[...], NT, preferred_element_type=f32)[0:1]
    (gain,) = unpack(vecf, ((2, 1, ALL),))
    column = tgt[...].astype(f32).T[:, 0:1].astype(jnp.int32)
    gft[...] = (
        jnp.dot(qkvw[:, 0:model], dq[...], preferred_element_type=f32)
        + jnp.dot(qkvw[:, model : 2 * model], dk[...], preferred_element_type=f32)
        + jnp.dot(qkvw[:, 2 * model :], dv[...], preferred_element_type=f32)
    )
    runs(1, middle)
    gsum = [jnp.zeros((1, model), f32)] * 3
    lifted = None
    for h in range(2):
        span = pl.ds(h * half, half)
        gf = gft[:, span].T
        value = embedded[span]
        center = value - jnp.mean(value, axis=-1, keepdims=True)
        rstd = lax.rsqrt(jnp.mean(center * center, axis=-1, keepdims=True) + EPS)
        normed = center * rstd
        gsum[0] += jnp.sum(gf * normed, axis=0, keepdims=True)
        gsum[1] += jnp.sum(gf, axis=0, keepdims=True)
        gn = gf * gain
        back = rstd * (
            gn - jnp.mean(gn, axis=-1, keepdims=True) - normed * jnp.mean(gn * normed, axis=-1, keepdims=True)
        )
        ge = grad_middle[span] + back
        offset = y * half + h * 2 * half
        hit = (iota((half, slots), 0) + offset == tgt[0:1]).astype(f32)
        flag = jnp.sum(hit, axis=1, keepdims=True)
        gsum[2] += jnp.sum((1.0 - flag) * ge, axis=0, keepdims=True)
        hit_t = (iota((slots, half), 1) + offset == column).astype(bf16)
        term = jnp.dot(hit_t, ge.astype(bf16), preferred_element_type=f32)
        lifted = term if lifted is None else lifted + term
        runs(2 + h, left)
    bsum = jnp.sum(lifted, axis=0, keepdims=True)
    low = lifted.astype(bf16)
    at = first + 3 * qr
    gemb = jnp.dot(enc[...].astype(f32).T.astype(bf16), low, preferred_element_type=f32).astype(bf16)
    for d in range(4):
        grads[d, at : at + er] = gemb[d * er : (d + 1) * er]

    def lanes(value, d, size=128):
        return value[:, d * size : (d + 1) * size]

    down_s, out_s, gain_s, bias_s = (sums[k : k + 1] for k in range(4))
    pad = grads.shape[1] - at - er
    for d in range(4):
        part = qsum if d < 2 else vsum
        blank = jnp.zeros((1, model // 2), f32)
        packed = [
            jnp.concatenate([lanes(bsum, d), lanes(gsum[2], d), lanes(gsum[0], d), lanes(gsum[1], d)], axis=1),
            jnp.concatenate([lanes(part, d % 2, 256), lanes(out_s, d), lanes(gain_s, d)], axis=1),
            sums[4 + d : 5 + d],
            jnp.concatenate([lanes(bias_s, d), lanes(down_s, d), blank], axis=1),
        ]
        packed = jnp.concatenate(packed + [jnp.zeros((pad - 4, model), f32)], axis=0)
        grads[d, at + er :] = packed.astype(bf16)
    runs(0, final)
    runs(2, middle)
    runs(4, left)
    vgrad[...] = (
        lax.dot_general(low, embw[...], NT, preferred_element_type=f32).astype(bf16).reshape(vgrad.shape)
    )
    vis_copies = [
        remote(vgrad.at[2 * (1 - y) + c], vis_in.at[y, :, c], vs.at[0], vr.at[0], across),
        remote(vgrad.at[2 * (1 - y) + 1 - c], vis_in.at[y, :, c], vs.at[1], vr.at[1], diag),
        remote(vgrad.at[2 * y + 1 - c], vis_in.at[y, :, c], vs.at[2], vr.at[2], chip),
        pltpu.make_async_copy(vgrad.at[b], vis_in.at[y, :, c], lsem.at[0]),
    ]
    runs(1, final)
    for copy in vis_copies:
        copy.start()
    runs(3, middle)
    runs(5, left)
    for step in range(2, stages + 1):
        if 4 + step <= stages:
            runs(4 + step, left)
        if step + 2 <= stages:
            runs(step + 2, middle)
        runs(step, final)
    for copy in vis_copies:
        copy.wait()
    vis_out[...] = vis_in[0] + vis_in[1]


def project_back(cubes, dq, dk, dv, first_in, embedded, grad_middle, qkvw, embw, enc, tgt, vecf, sums, early, cap):
    tokens, model = first_in.shape
    chunk = chunk_rows(cubes)
    depth = 3 * model // 4 + embw.shape[0] // 4 + 16
    depth = depth + -depth % chunk + LATE_CHUNKS * chunk
    enc_width = enc.shape[1]
    slots = enc.shape[0]
    sds = jax.ShapeDtypeStruct
    return pl.pallas_call(
        functools.partial(project_back_kernel, cubes, chunk),
        name="project_back",
        out_shape=(sds((depth, model), bf16), sds((2, 2, cap, enc_width), bf16)),
        in_specs=[VM] * 12 + [ANY],
        out_specs=(VM, VM),
        scratch_shapes=[
            pltpu.VMEM((4, depth, model), bf16),
            pltpu.VMEM((model, tokens), bf16),
            pltpu.VMEM((model, tokens), f32),
            pltpu.VMEM((4, 2, cap, enc_width), bf16),
            pltpu.VMEM((2, 2, 2, cap, enc_width), bf16),
            pltpu.SemaphoreType.DMA((2,)),
            pltpu.SemaphoreType.DMA((3,)),
            pltpu.SemaphoreType.DMA((3,)),
        ] + reducer_scratch(cubes, depth // chunk, depth, model),
        compiler_params=params(3),
    )(dq, dk, dv, first_in, embedded, grad_middle, qkvw, embw, enc, tgt, vecf, sums, early)


def finish_kernel(late, first, second, down, up, out, qkv, emb, *vectors):
    model = down.shape[1]
    parts = up.shape[1] // model
    size = up.shape[0]
    start = first.shape[0]

    def early(at, count):
        if at + count <= start:
            return first[at : at + count].astype(f32)
        if at >= start:
            return second[at - start : at - start + count].astype(f32)
        return jnp.concatenate(
            [first[at:start].astype(f32), second[0 : at + count - start].astype(f32)], axis=0
        )

    down[...] = early(0, model).T
    for k in range(parts):
        up[:, k * model : (k + 1) * model] = early(model + k * size, size)
    out[...] = early(model + parts * size, size)
    for k in range(3):
        qkv[:, k * model : (k + 1) * model] = second[late + k * size : late + (k + 1) * size].astype(f32)
    at = late + 3 * size
    er = emb.shape[0]
    emb[...] = second[at : at + er].astype(f32)
    packed = second[at + er : at + er + 16].astype(f32)
    pieces = iter(vectors)
    for row, widths in enumerate(((128, 128, 128, 128), (256, 128, 128), (512,), (128, 128))):
        lane = 0
        for width in widths:
            next(pieces)[...] = packed[row : row + 1, lane : lane + width]
            lane += width


def finish(late, first, second, shapes):
    sds = jax.ShapeDtypeStruct
    widths = (128, 128, 128, 128, 256, 128, 128, 512, 128, 128)
    return pl.pallas_call(
        functools.partial(finish_kernel, late),
        name="results",
        out_shape=tuple(sds(s, f32) for s in shapes) + tuple(sds((1, w), f32) for w in widths),
        in_specs=[VM, VM],
        out_specs=tuple([VM] * (len(shapes) + len(widths))),
        compiler_params=params(),
    )(first, second)


def shards(
    cubes,
    visible, kept_rows, slot_counts, patches, positions, embedder, embedbias, masktoken, attngain, attnbias,
    qkvproj, qvbias, outproj, outbias, mlpgain, mlpbias, upproj, upbias, downproj, downbias, cotangent,
):
    cells = cotangent.shape[1]
    cap, enc_width = visible.shape[2:]
    _, b, _, _ = place()
    slot = jnp.arange(cap, dtype=jnp.int32)
    live = jnp.where(slot[None, :] < slot_counts[0][:, None], kept_rows[0], -1)
    code = jnp.where(live >= 0, live + 2 * cells * (jnp.arange(4, dtype=jnp.int32)[:, None] // 2), -1)
    code = jnp.moveaxis(code.reshape(2, 2, cap), 1, 0).reshape(2, 1, 2 * cap)
    source = jnp.arange(4, dtype=jnp.int32)[None, :, None]
    kept = jnp.where(source == b, code, -1).reshape(2, 1, 8 * cap)
    kept = jnp.broadcast_to(kept, (2, 8, 8 * cap))
    vis = visible.reshape(2, 2, cap, enc_width)
    vecs = [
        m.reshape(-1, 128)
        for m in (embedbias, masktoken, attngain, attnbias, qvbias, outbias, mlpgain, mlpbias, upbias, downbias)
    ]
    embedded, first_in, q, k, v, emb_full, qkv_full, enc, target, vecf = embed(
        vis, kept, embedder, qkvproj, positions, vecs
    )
    own = (outproj, upproj, downproj, cotangent)
    e, ot, linv, mixed, *gathered = attend(patches, q, k, v, *own)
    act, grads, grad_middle, grad_mixed, sums = mlp(cubes, patches, vecf, mixed, ot, embedded, gathered, own)
    dq, dk, dv, activations, first = attend_back(cubes, q, k, v, grad_mixed, ot, linv, e, act, grads)
    second, visible_grad = project_back(
        cubes, dq, dk, dv, first_in, embedded, grad_middle, qkv_full, emb_full, enc, target, vecf, sums, grads, cap
    )
    shapes = (downproj.shape, upproj.shape, outproj.shape, qkvproj.shape, embedder.shape)
    down_o, up_o, out_o, qkv_o, emb_o, *small = finish(LATE_CHUNKS * chunk_rows(cubes), first, second, shapes)
    ebias, mask, again, abias, qv, outb, mgain, upb, mbias, downb = (m.reshape(-1) for m in small)
    return (
        activations, visible_grad.reshape(visible.shape), emb_o, ebias, mask, again, abias, qkv_o, qv,
        out_o, outb, mgain, mbias, up_o, upb, down_o, downb,
    )


def solution(mesh):
    cubes = mesh.shape["cube"]
    split = P(("cube", "band"), None, None, None)
    mat, row = P("band", None), P("band")
    placed = (
        split, P(("cube", "band"), None, None), P(("cube", "band"), None), P("cube"), mat,
        mat, row, row, row, row, mat, row, mat, row, row, row, mat, row, mat, row, P("cube", "band", None),
    )
    return jax.shard_map(
        functools.partial(shards, cubes),
        mesh=mesh,
        in_specs=placed,
        out_specs=(
            P("cube", "band", None), split, mat, row, row, row, row, mat, row, mat, row, row, row, mat, row, mat, row,
        ),
        check_vma=False,
    )
```

```python
import functools

import jax
import jax.numpy as jnp
from jax import lax
from jax.experimental import pallas as pl
from jax.experimental.pallas import tpu as pltpu
from jax.sharding import PartitionSpec as P

HEADS = 16
LATE_CHUNKS = 1
SIDE_CHUNKS = 2
HDIM = 32
EPS = 1e-06
LOG2E = 1.4426950408889634
QSCALE = HDIM ** (-0.5) * LOG2E
MESH = pl.DeviceIdType.MESH
NT = (((1,), (1,)), ((), ()))
f32 = jnp.float32
bf16 = jnp.bfloat16
ANY = pl.BlockSpec(memory_space=pl.ANY)
VM = pl.BlockSpec(memory_space=pltpu.VMEM)
VMEM_LIMIT = 60 * 2**20


def iota(shape, dim):
    return lax.broadcasted_iota(jnp.int32, shape, dim)


def normalize(values):
    center = values - jnp.mean(values, axis=-1, keepdims=True)
    spread = jnp.mean(center * center, axis=-1, keepdims=True)
    return center * lax.rsqrt(spread + EPS)


def place():
    cube, band = lax.axis_index("cube"), lax.axis_index("band")
    y, c = band // 2, band % 2
    return cube, band, y, c


def peers():
    cube, band, y, c = place()
    same_chip = (cube, 2 * y + 1 - c)
    across = (cube, 2 * (1 - y) + c)
    diagonal = (cube, 2 * (1 - y) + 1 - c)
    return same_chip, across, diagonal


def hail(devices):
    barrier = pltpu.get_barrier_semaphore()
    for device in devices:
        pl.semaphore_signal(barrier, inc=1, device_id=device, device_id_type=MESH)


def meet(devices):
    pl.semaphore_wait(pltpu.get_barrier_semaphore(), len(devices))


def remote(src, dst, send, recv, device):
    return pltpu.make_async_remote_copy(
        src_ref=src, dst_ref=dst, send_sem=send, recv_sem=recv, device_id=device, device_id_type=MESH
    )


def rows(start, size):
    return pl.ds(pl.multiple_of(start, 16), size)


def params(collective_id=None):
    if collective_id is None:
        return pltpu.CompilerParams(vmem_limit_bytes=VMEM_LIMIT)
    return pltpu.CompilerParams(collective_id=collective_id, has_side_effects=True, vmem_limit_bytes=VMEM_LIMIT)


def mate_of(k):
    cube, b, _, _ = place()
    d = 1 << k
    return (cube + d - 2 * d * ((cube // d) % 2), b)


def corner():
    _, _, y, c = place()
    return (mate_of(0)[0], 2 * (1 - y) + c)


def unpack(vecf, spans):
    vectors = vecf[...].astype(f32)
    out = []
    for first, count, bands in spans:
        out.append(
            jnp.concatenate([vectors[d, k : k + 1] for d in bands for k in range(first, first + count)], axis=1)
        )
    return out


ALL = (0, 1, 2, 3)


def embed_kernel(
    vis, kept_rows, counts, emb, qkv, pos, *refs,
):
    vecs = refs[:10]
    (embedded, first_in, q_out, k_out, v_out, emb_out, qkv_out, enc_out, tgt_out, vecf,
     enc, tgt, embf, qkvf, posf, vec, kbuf, vbuf, qbuf, ebuf, fbuf, kept, lsem, ssem, rsem) = refs[10:]
    cube, b, y, c = place()
    x = cube % 2
    chip, across, diag = peers()
    mate = mate_of(0)
    bq = 2 * (1 - y) + c
    er, qr = emb.shape[0], qkv.shape[0]
    half = pos.shape[0]
    model = emb.shape[1]
    hail((chip, across, diag, mate))
    fill = jnp.zeros((vec.shape[0] - sum(v.shape[0] for v in vecs), 128), f32)
    vec[...] = jnp.concatenate([v[...].astype(f32) for v in vecs] + [fill], axis=0).astype(bf16)
    cap = vis.shape[2]
    names = kept_rows[...].astype(f32)
    high = jnp.floor(names * (1.0 / 32.0))
    wide = tgt.shape[2]
    spread = (iota((cap, wide), 1) % cap == iota((cap, wide), 0)).astype(bf16)
    names = 32.0 * jnp.dot(high.astype(bf16), spread, preferred_element_type=f32) + jnp.dot(
        (names - 32.0 * high).astype(bf16), spread, preferred_element_type=f32
    )
    lane = iota((1, wide), 1)
    upper = (lane // cap) % 2 == 1
    for d in range(2):
        row = jnp.where(upper, names[2 + d : 3 + d] + 4.0 * pos.shape[0] / 2.0, names[d : d + 1])
        bound = jnp.where(upper, counts[0, 2 + d], counts[0, d])
        live = (lane % cap < bound) & (lane // (2 * cap) == b)
        row = jnp.where(live, row, -1.0).astype(jnp.int32)
        kept[d] = jnp.broadcast_to(row, kept.shape[1:])
    meet((chip, across, diag, mate))

    used = [0]
    local = []

    def send(src, dst, device):
        copy = remote(src, dst, ssem.at[used[0]], rsem.at[used[0]], device)
        used[0] += 1
        copy.start()
        return copy

    def keep(src, dst):
        copy = pltpu.make_async_copy(src, dst, lsem.at[len(local)])
        copy.start()
        local.append(copy)

    def cut(start, size, which):
        return rows(start + which * (size // 2), size // 2)

    def quarter(band, which, k):
        return rows(band * qr + which * (qr // 2) + k * (qr // 4), qr // 4)

    ea, qa = rows(b * er, er), rows(b * qr, qr)
    far_vec = send(vec, vecf.at[b], across)
    small = [
        send(kept.at[c], tgt.at[b], across),
        send(vis.at[:, c], enc.at[b], across),
        send(kept.at[1 - c], tgt.at[b], diag),
        send(vis.at[:, 1 - c], enc.at[b], diag),
        send(kept.at[1 - c], tgt.at[b], chip),
        send(vec, vecf.at[b], chip),
        send(vis.at[:, 1 - c], enc.at[b], chip),
        send(emb, embf.at[ea], chip),
    ]
    far_emb = send(emb.at[cut(0, er, x)], embf.at[cut(b * er, er, x)], across)
    far_pos = send(pos.at[cut(0, half, x)], posf.at[y, cut(0, half, x)], across)
    far_qkv = [send(qkv.at[quarter(0, x, k)], qkvf.at[quarter(b, x, k)], across) for k in range(2)]
    near_qkv = send(qkv, qkvf.at[qa], chip)
    keep(kept.at[c], tgt.at[b])
    keep(vec, vecf.at[b])
    keep(vis.at[:, c], enc.at[b])
    keep(emb, embf.at[ea])
    keep(pos, posf.at[y])
    keep(qkv, qkvf.at[qa])

    far_vec.wait()
    relays = [send(vecf.at[bq], vecf.at[bq], chip)]
    far_emb.wait()
    got = cut(bq * er, er, x)
    side_emb = send(embf.at[got], embf.at[got], mate)
    relays.append(send(embf.at[got], embf.at[got], chip))
    side_emb.wait()
    got = cut(bq * er, er, 1 - x)
    relays.append(send(embf.at[got], embf.at[got], chip))
    far_pos.wait()
    got = cut(0, half, x)
    side_pos = send(posf.at[1 - y, got], posf.at[1 - y, got], mate)
    for copy in small + local + relays:
        copy.wait()

    target = jnp.max(tgt[...].astype(f32), axis=0)[0:1].astype(jnp.int32)
    tgt_out[...] = jnp.broadcast_to(target, tgt_out.shape)
    slots = 8 * cap
    enc_all = enc[...].reshape(slots, enc.shape[3])
    results = []

    def give(src, dst):
        copy = pltpu.make_async_copy(src, dst, lsem.at[8 + len(results)])
        copy.start()
        results.append(copy)

    give(enc, enc_out)
    give(embf, emb_out)
    embedbias, mask, gain, bias, qbias, vbias = unpack(
        vecf, ((0, 1, ALL), (1, 1, ALL), (2, 1, ALL), (3, 1, ALL), (4, 2, (0, 1)), (4, 2, (2, 3)))
    )

    def lift(h):
        span = rows(h * half, half)
        cells = iota((half, slots), 0) + (y * half + h * 2 * half)
        hit = (cells == target).astype(f32)
        flag = jnp.sum(hit, axis=1, keepdims=True)
        picked = jnp.dot(hit.astype(bf16), enc_all, preferred_element_type=f32).astype(bf16)
        rows_in = jnp.dot(picked, embf[...], preferred_element_type=f32)
        v = rows_in + flag * embedbias + (1.0 - flag) * mask + posf[h].astype(f32)
        ebuf[span] = v
        fbuf[span] = (normalize(v) * gain + bias).astype(bf16)
        give(ebuf.at[span], embedded.at[span])
        give(fbuf.at[span], first_in.at[span])

    lift(y)
    side_qkv, late = [], []
    for k in range(2):
        far_qkv[k].wait()
        got = quarter(bq, x, k)
        side_qkv.append(send(qkvf.at[got], qkvf.at[got], mate))
        late.append(send(qkvf.at[got], qkvf.at[got], chip))
    side_pos.wait()
    lift(1 - y)
    for k in range(2):
        side_qkv[k].wait()
        got = quarter(bq, 1 - x, k)
        late.append(send(qkvf.at[got], qkvf.at[got], chip))
    near_qkv.wait()
    for copy in late:
        copy.wait()
    give(qkvf, qkv_out)
    mine = rows(c * 2 * half, 2 * half)
    first = fbuf[...]
    k = jnp.dot(first, qkvf[:, model : 2 * model], preferred_element_type=f32)
    kbuf[...] = k.astype(bf16)
    out = [send(kbuf, k_out.at[mine], chip)]
    give(kbuf, k_out.at[mine])
    v = jnp.dot(first, qkvf[:, 2 * model :], preferred_element_type=f32)
    vbuf[...] = (v + vbias).astype(bf16)
    out.append(send(vbuf, v_out.at[mine], chip))
    give(vbuf, v_out.at[mine])
    q = jnp.dot(first, qkvf[:, :model], preferred_element_type=f32)
    qbuf[...] = ((q + qbias) * QSCALE).astype(bf16)
    give(qbuf, q_out)
    for copy in out + results:
        copy.wait()


def embed(vis, kept_rows, counts, emb, qkv, pos, vecs):
    er, model = emb.shape
    qr, wide = qkv.shape
    half = pos.shape[0]
    enc_width = vis.shape[-1]
    cap = vis.shape[2]
    slots = 8 * cap
    tokens = 2 * half
    sds = jax.ShapeDtypeStruct
    return pl.pallas_call(
        embed_kernel,
        name="embed_project",
        out_shape=(
            sds((tokens, model), f32),
            sds((tokens, model), bf16),
            sds((tokens, model), bf16),
            sds((2 * tokens, model), bf16),
            sds((2 * tokens, model), bf16),
            sds((4 * er, model), bf16),
            sds((4 * qr, wide), bf16),
            sds((4, 2, cap, enc_width), bf16),
            sds((8, slots), jnp.int32),
            sds((4, 16, 128), bf16),
        ),
        in_specs=[ANY, VM, pl.BlockSpec(memory_space=pltpu.SMEM), ANY, ANY, ANY] + [VM] * 10,
        out_specs=(ANY,) * 8 + (VM, VM),
        scratch_shapes=[
            pltpu.VMEM((4, 2, cap, enc_width), bf16),
            pltpu.VMEM((4, 8, slots), jnp.int32),
            pltpu.VMEM((4 * er, model), bf16),
            pltpu.VMEM((4 * qr, wide), bf16),
            pltpu.VMEM((2, half, model), bf16),
            pltpu.VMEM((16, 128), bf16),
            pltpu.VMEM((tokens, model), bf16),
            pltpu.VMEM((tokens, model), bf16),
            pltpu.VMEM((tokens, model), bf16),
            pltpu.VMEM((tokens, model), f32),
            pltpu.VMEM((tokens, model), bf16),
            pltpu.VMEM((2, 8, slots), jnp.int32),
            pltpu.SemaphoreType.DMA((20,)),
            pltpu.SemaphoreType.DMA((32,)),
            pltpu.SemaphoreType.DMA((32,)),
        ],
        compiler_params=params(0),
    )(vis, kept_rows, counts, emb, qkv, pos, *vecs)


def forward_kernel(
    patch, q_ref, k_ref, v_ref, outw, upw, downw, cot,
    e_ref, o_ref, linv_ref, mix_ref, out_full, up_full, down_full, cot_full,
    kxa, kxb, vt, sa, sb, ots, ssem, rsem,
):
    p = pl.program_id(0)
    last = pl.num_programs(0) - 1
    cube, b, y, c = place()
    x = cube % 2
    chip, across, _ = peers()
    mate = mate_of(0)
    bq = 2 * (1 - y) + c
    shards = ((upw, up_full), (outw, out_full), (downw, down_full))

    def cut(k, band, which):
        size = shards[k][0].shape[0]
        return rows(band * size + which * (size // 2), size // 2)

    def far(k):
        size = shards[k][0].shape[0]
        part = rows(x * (size // 2), size // 2)
        return remote(shards[k][0].at[part], shards[k][1].at[cut(k, b, x)], ssem.at[k], rsem.at[k], across)

    def near(k):
        size = shards[k][0].shape[0]
        return remote(shards[k][0], shards[k][1].at[rows(b * size, size)], ssem.at[3 + k], rsem.at[3 + k], chip)

    def side(k):
        ref = shards[k][1].at[cut(k, bq, x)]
        return remote(ref, ref, ssem.at[6 + k], rsem.at[6 + k], mate)

    def relay(k, which):
        ref = shards[k][1].at[cut(k, bq, x if which == 0 else 1 - x)]
        at = 9 + 2 * k + which
        return remote(ref, ref, ssem.at[at], rsem.at[at], chip)

    def cot_far():
        return remote(cot.at[1 - y], cot_full, ssem.at[15], rsem.at[15], across)

    @pl.when(p == 0)
    def _():
        hail((chip, across, mate))

    keys = k_ref.shape[0]
    tokens = q_ref.shape[0]
    lane = iota((keys, 128), 1)
    pieces = 3
    block = tokens // pieces

    @pl.when(p == 0)
    def _():
        row = iota((keys, 128), 0)
        bias = jnp.where((row % cot.shape[1] >= patch[y]) & (lane == 0), -1e30, 0.0).astype(bf16)
        kxa[:, 128:256] = bias
        kxb[:, 128:256] = bias
        for g in range(v_ref.shape[1] // 128):
            cols = slice(g * 128, (g + 1) * 128)
            vt[cols] = v_ref[:, cols].astype(f32).T.astype(bf16)

    def lanes(h):
        return pl.ds(pl.multiple_of((h // 4) * 128, 128), 128)

    def prepare(h, kx):
        k = k_ref[:, lanes(h)]
        kx[:, 0:128] = jnp.where((lane // HDIM) == (h % 4), k, jnp.zeros_like(k))

    def score(h, kx, s, j):
        span = slice(j * block, (j + 1) * block)
        qx = jnp.concatenate([q_ref[span, lanes(h)], jnp.ones((block, 128), bf16)], axis=1)
        s[span] = lax.dot_general(qx, kx[...], NT, preferred_element_type=f32)

    ones = jnp.ones((16, keys), bf16)

    def soften(at, h, s, j):
        span = slice(j * block, (j + 1) * block)
        v = s[span]
        e = jnp.exp2(v - jnp.max(v, axis=1, keepdims=True)).astype(bf16)
        e_ref[at, span] = e
        lhs = jnp.concatenate([vt[pl.ds(pl.multiple_of(h * HDIM, HDIM), HDIM)], ones], axis=0)
        ot = lax.dot_general(lhs, e, NT, preferred_element_type=f32)
        li = 1.0 / ot[HDIM : HDIM + 8]
        o = ot[:HDIM] * li[0:1]
        o_ref[at * HDIM : (at + 1) * HDIM, span] = o
        ots[pl.ds(pl.multiple_of((p % 2) * 2 * HDIM + at * HDIM, HDIM), HDIM), span] = o
        linv_ref[at, :, span] = li

    @pl.when(p == 0)
    def _():
        prepare(0, kxa)
        for j in range(pieces):
            score(0, kxa, sa, j)
        meet((chip, across, mate))
        far(0).start()
        far(1).start()
        far(2).start()
        cot_far().start()
        for k in range(3):
            near(k).start()

    for k, at in ((0, 2), (1, 3), (2, 4)):

        @pl.when(p == at)
        def _(k=k):
            far(k).wait()
            side(k).start()
            relay(k, 0).start()

    for k, at in ((0, 5), (1, 6), (2, 7)):

        @pl.when(p == at)
        def _(k=k):
            side(k).wait()
            relay(k, 1).start()

    after = jnp.minimum(2 * p + 2, 2 * last + 1)
    prepare(2 * p + 1, kxb)
    for j in range(pieces):
        score(2 * p + 1, kxb, sb, j)
        soften(0, 2 * p, sa, j)
    prepare(after, kxa)
    for j in range(pieces):
        score(after, kxa, sa, j)
        soften(1, 2 * p + 1, sb, j)

    @pl.when(p % 2 == 1)
    def _():
        mix_ref[...] = ots[...].T.astype(bf16)

    @pl.when(p == last)
    def _():
        cot_far().wait()
        for k in range(3):
            near(k).wait()
            relay(k, 0).wait()
            relay(k, 1).wait()


def attend(patch, q, k, v, outw, upw, downw, cot):
    tokens, model = q.shape
    keys = k.shape[0]
    sds = jax.ShapeDtypeStruct

    def fixed(shape):
        return pl.BlockSpec(shape, lambda p: (0, 0))

    return pl.pallas_call(
        forward_kernel,
        name="attend",
        grid=(HEADS // 2,),
        in_specs=[
            pl.BlockSpec(memory_space=pltpu.SMEM),
            fixed(q.shape),
            fixed(k.shape),
            fixed(v.shape),
            ANY, ANY, ANY, ANY,
        ],
        out_specs=[
            pl.BlockSpec((2, tokens, keys), lambda p: (p, 0, 0)),
            pl.BlockSpec((2 * HDIM, tokens), lambda p: (p, 0)),
            pl.BlockSpec((2, 8, tokens), lambda p: (p, 0, 0)),
            pl.BlockSpec((tokens, 128), lambda p: (0, p // 2)),
            ANY, ANY, ANY, ANY,
        ],
        out_shape=[
            sds((HEADS, tokens, keys), bf16),
            sds((model, tokens), f32),
            sds((HEADS, 8, tokens), f32),
            sds((tokens, model), bf16),
            sds((4 * outw.shape[0], outw.shape[1]), bf16),
            sds((4 * upw.shape[0], upw.shape[1]), bf16),
            sds((4 * downw.shape[0], downw.shape[1]), bf16),
            sds(cot.shape[1:], bf16),
        ],
        scratch_shapes=[
            pltpu.VMEM((keys, 256), bf16),
            pltpu.VMEM((keys, 256), bf16),
            pltpu.VMEM((model, keys), bf16),
            pltpu.VMEM((tokens, keys), f32),
            pltpu.VMEM((tokens, keys), f32),
            pltpu.VMEM((128, tokens), f32),
            pltpu.SemaphoreType.DMA((16,)),
            pltpu.SemaphoreType.DMA((16,)),
        ],
        compiler_params=params(1),
    )(patch, q, k, v, outw, upw, downw, cot)


def mlp_kernel(
    patch, vecf, mixed, mixed_t_in, embedded_in, out_got, up_got, down_got, cot_got, out_own, up_own, down_own, cot_own,
    act_out, grads_out, middle_out, mixed_out, sums,
    act, grads, grad_middle, grad_mixed, mixed_f, embedded_f, outw, upf, downf, cot, second_t, gout_t, second, active, hid, branch_b, wsem,
):
    _, b, y, _ = place()
    tokens, model = mixed.shape
    half = tokens // 2
    wide = upf.shape[1]
    parts = wide // model
    loads = []

    def load(src, dst):
        copy = pltpu.make_async_copy(src, dst, wsem.at[len(loads)])
        copy.start()
        loads.append(copy)

    mixed_t, embedded = mixed_f, embedded_f
    results = []

    def give(src, dst):
        copy = pltpu.make_async_copy(src, dst, wsem.at[16 + len(results)])
        copy.start()
        results.append(copy)

    for own, got, full in ((out_own, out_got, outw), (up_own, up_got, upf), (down_own, down_got, downf)):
        size = own.shape[0]
        load(own, full.at[rows(b * size, size)])
        for k in range(1, 4):
            part = rows((b + k) % 4 * size, size)
            load(got.at[part], full.at[part])
        if own is out_own:
            load(embedded_in, embedded_f)
    load(cot_own.at[y], cot.at[y])
    load(cot_got, cot.at[1 - y])
    load(mixed_t_in, mixed_f)
    vectors = vecf[...].astype(f32)

    def whole(k):
        return jnp.concatenate([vectors[d, k : k + 1] for d in range(4)], axis=1)

    outbias, gain, bias, downbias = whole(6), whole(7), whole(8), whole(13)
    upbias = [jnp.concatenate([vectors[d, 9 + k : 10 + k] for k in range(4)], axis=1) for d in range(parts)]
    live = iota((half, 1), 0) < patch[y]
    valid = jnp.where(live, 1.0, 0.0)
    total = [jnp.zeros((1, model), f32)] * (4 + parts)
    for copy in loads[:5]:
        copy.wait()
    for h in range(2):
        span = pl.ds(h * half, half)
        mix = mixed[span]
        middle = embedded[span] + (jnp.dot(mix, outw[...], preferred_element_type=f32) + outbias)
        center = middle - jnp.mean(middle, axis=-1, keepdims=True)
        rstd = lax.rsqrt(jnp.mean(center * center, axis=-1, keepdims=True) + EPS)
        normed = center * rstd
        sec = normed * gain + bias
        second_t[:, span] = sec.T.astype(bf16)
        sec = sec.astype(bf16)
        if h == 0:
            for copy in loads[5:-1]:
                copy.wait()
        gout = cot[h].astype(f32) * valid
        gout_t[:, span] = gout.T.astype(bf16)
        gout_b = gout.astype(bf16)
        total[0] += jnp.sum(gout, axis=0, keepdims=True)
        result = middle + downbias
        gsec = None
        for k in range(parts):
            cols = slice(k * model, (k + 1) * model)
            hidden = jnp.dot(sec, upf[:, cols], preferred_element_type=f32) + upbias[k]
            cdf = 0.5 + 0.5 * lax.erf(hidden * 0.7071067811865476)
            low = (hidden * cdf).astype(bf16)
            active[span, cols] = low
            slope = cdf + hidden * (0.3989422804014327 * jnp.exp(-0.5 * hidden * hidden))
            result += jnp.dot(low, downf[cols], preferred_element_type=f32)
            gact = lax.dot_general(gout_b, downf[cols], NT, preferred_element_type=f32)
            ghid = (gact * slope).astype(bf16)
            hid[span, cols] = ghid
            total[4 + k] += jnp.sum(ghid.astype(f32), axis=0, keepdims=True)
            term = lax.dot_general(ghid, upf[:, cols], NT, preferred_element_type=f32)
            gsec = term if gsec is None else gsec + term
        act[h] = (valid * result).astype(bf16)
        total[2] += jnp.sum(gsec * normed, axis=0, keepdims=True)
        total[3] += jnp.sum(gsec, axis=0, keepdims=True)
        gn = gsec * gain
        back = rstd * (
            gn - jnp.mean(gn, axis=-1, keepdims=True) - normed * jnp.mean(gn * normed, axis=-1, keepdims=True)
        )
        gmid = gout + back
        grad_middle[span] = gmid
        gb = gmid.astype(bf16)
        branch_b[span] = gb
        total[1] += jnp.sum(gb.astype(f32), axis=0, keepdims=True)
        grad_mixed[:, span] = lax.dot_general(outw[...], gb, NT, preferred_element_type=f32).astype(bf16)
        give(act.at[h], act_out.at[h])
        give(grad_middle.at[span], middle_out.at[span])
    give(grad_mixed, mixed_out)
    for k in range(parts):
        cols = slice(k * model, (k + 1) * model)
        grads[k, 0:model] = jnp.dot(gout_t[...], active[:, cols], preferred_element_type=f32).astype(bf16)
        gup = jnp.dot(second_t[...], hid[:, cols], preferred_element_type=f32).astype(bf16)
        size = model // 4
        for d in range(4):
            grads[d, model + k * size : model + (k + 1) * size] = gup[d * size : (d + 1) * size]
        give(grads.at[k, pl.ds(0, model)], grads_out.at[k, pl.ds(0, model)])
        part = pl.ds(model + k * size, size)
        give(grads.at[:, part], grads_out.at[:, part])
    base = model + parts * (model // 4)
    loads[-1].wait()
    gout_w = jnp.dot(mixed_t[...].astype(bf16), branch_b[...], preferred_element_type=f32).astype(bf16)
    for d in range(4):
        grads[d, base : base + model // 4] = gout_w[d * (model // 4) : (d + 1) * (model // 4)]
    spare = grads.shape[1] - base - model // 4
    if spare:
        grads[:, base + model // 4 :] = jnp.zeros((4, spare, model), bf16)
    part = pl.ds(base, grads.shape[1] - base)
    give(grads.at[:, part], grads_out.at[:, part])
    sums[...] = jnp.concatenate(total, axis=0)
    for copy in results:
        copy.wait()


def mlp(cubes, patch, vecf, mixed, mixed_t, embedded, gathered, own):
    tokens, model = mixed.shape
    outw, upw, downw, cot = own
    wide = upw.shape[1]
    half = cot.shape[1]
    depth = model + wide // 4 + model // 4
    depth += -depth % chunk_rows(cubes)
    sds = jax.ShapeDtypeStruct
    return pl.pallas_call(
        mlp_kernel,
        name="mlp_both",
        out_shape=(
            sds((2, half, model), bf16),
            sds((4, depth, model), bf16),
            sds((tokens, model), f32),
            sds((model, tokens), bf16),
            sds((4 + wide // model, model), f32),
        ),
        in_specs=[pl.BlockSpec(memory_space=pltpu.SMEM), VM, VM] + [ANY] * 10,
        out_specs=(ANY, ANY, ANY, ANY, VM),
        scratch_shapes=[
            pltpu.VMEM((2, half, model), bf16),
            pltpu.VMEM((4, depth, model), bf16),
            pltpu.VMEM((tokens, model), f32),
            pltpu.VMEM((model, tokens), bf16),
            pltpu.VMEM((model, tokens), f32),
            pltpu.VMEM((tokens, model), f32),
            pltpu.VMEM((model, model), bf16),
            pltpu.VMEM((model, wide), bf16),
            pltpu.VMEM((wide, model), bf16),
            pltpu.VMEM((2, half, model), bf16),
            pltpu.VMEM((model, tokens), bf16),
            pltpu.VMEM((model, tokens), bf16),
            pltpu.VMEM((tokens, model), bf16),
            pltpu.VMEM((tokens, wide), bf16),
            pltpu.VMEM((tokens, wide), bf16),
            pltpu.VMEM((tokens, model), bf16),
            pltpu.SemaphoreType.DMA((32,)),
        ],
        compiler_params=params(),
    )(patch, vecf, mixed, mixed_t, embedded, *gathered, *own)


def chunk_rows(cubes):
    return max(128, 8 * cubes)


def reducer(cubes, chunk, grads, mine, got_core, got_y, work, gots, total, ssem, rsem):
    cube, b, y, c = place()
    chip, across, _ = peers()
    bits = cubes.bit_length() - 1
    own, other = 2 * y + c, 2 * (1 - y) + c
    top = bits + 1

    def kept(k):
        start = 0
        for j in range(k):
            start = start + ((cube // (1 << j)) % 2) * (chunk >> (j + 1))
        return start

    def back(s, t):
        k = 2 * bits - s
        span = rows(t * chunk + kept(k + 1), chunk >> (k + 1))
        return total.at[span], total.at[span], mate_of(k)

    def core(t):
        span = rows(t * chunk, chunk)
        return [
            remote(grads.at[1 - c, span], got_core.at[0, span], ssem.at[t, 0], rsem.at[t, 0], chip),
            remote(grads.at[3 - c, span], got_core.at[1, span], ssem.at[t, 1], rsem.at[t, 1], chip),
        ]

    def step(k, t, both):
        side = pl.ds(0, 2) if both else pl.ds(0, 1)
        if k < bits - 1:
            size = chunk >> (k + 1)
            bit = (cube // (1 << k)) % 2
            away = rows(t * chunk + kept(k) + (1 - bit) * size, size)
        else:
            size = chunk >> k
            away = rows(t * chunk + kept(k), size)
        return work.at[side, away], gots[k].at[side, rows(t * size, size)], mate_of(k)

    def copies(s, t, side):
        if s == 0:
            return core(t)
        if side == "joint":
            first, second, part = halves(t)
            return [
                remote(work.at[1, first], got_y.at[first], ssem.at[t, 2], rsem.at[t, 2], across),
                remote(work.at[0, second], gots[0].at[0, part], ssem.at[t, 3], rsem.at[t, 3], mate_of(0)),
                remote(work.at[1, second], gots[0].at[1, part], ssem.at[t, more], rsem.at[t, more], corner()),
            ]
        if not side:
            if s == 1:
                span = rows(t * chunk, chunk)
                move = work.at[1, span], got_y.at[span], across
            elif s <= top:
                move = step(s - 2, t, False)
            else:
                move = back(s, t)
        elif s < top:
            move = step(s - 1, t, True)
        elif s == top:
            size = chunk >> (bits - 1)
            span = rows(t * chunk + kept(bits - 1), size)
            move = work.at[1, span], got_y.at[span], across
        else:
            move = back(s, t)
        return [remote(move[0], move[1], ssem.at[t, s + 1], rsem.at[t, s + 1], move[2])]

    more = 2 + 2 * bits

    def halves(t):
        size = chunk // 2
        x = cube % 2
        base = t * chunk
        return rows(base + x * size, size), rows(base + (1 - x) * size, size), rows(t * size, size)

    def run(s, t, side=False):
        if side == "joint" and s > 2:
            s, side = s + 1, False
        if side == "joint" and s == 2:
            for copy in copies(1, t, side):
                copy.wait()
            first, _, part = halves(t)
            work[0, first] = (work[0, first] + got_y[first]) + (gots[0][0, part] + gots[0][1, part])
            for copy in copies(3, t, False):
                copy.start()
            return
        if s > 0:
            for copy in copies(s - 1, t, side):
                copy.wait()
        span = rows(t * chunk, chunk)
        if s == 1:
            work[1, span] = mine(other, span) + got_core[1 - y, span]
            if side:
                work[0, span] = mine(own, span) + got_core[y, span]
        elif s == 2 and not side:
            work[0, span] = (mine(own, span) + got_core[y, span]) + got_y[span]
        elif 2 <= s <= top + 1:
            k = s - 2 if side else s - 3
            if side and s == top + 1:
                size = chunk >> (bits - 1)
                span = rows(t * chunk + kept(bits - 1), size)
                total[span] = work[0, span] + got_y[span]
            else:
                size = chunk >> min(k + 1, bits - 1)
                span = rows(t * chunk + kept(min(k + 1, bits - 1)), size)
                part = rows(t * size, size)
                if side:
                    work[:, span] = work[:, span] + gots[k][:, part]
                elif s <= top:
                    work[0, span] = work[0, span] + gots[k][0, part]
                else:
                    total[span] = work[0, span] + gots[k][0, part]
        if s < 1 + 2 * bits:
            for copy in copies(s, t, side):
                copy.start()

    return run, 1 + 2 * bits


def reducer_scratch(cubes, count, depth, width):
    bits = cubes.bit_length() - 1
    return [
        pltpu.VMEM((2, depth, width), bf16),
        pltpu.VMEM((depth, width), bf16),
        pltpu.VMEM((2, depth, width), bf16),
    ] + [pltpu.VMEM((2, depth >> min(k + 1, bits - 1), width), bf16) for k in range(bits)] + [
        pltpu.SemaphoreType.DMA((count, 3 + 2 * bits)),
        pltpu.SemaphoreType.DMA((count, 3 + 2 * bits)),
    ]


def backward_kernel(
    cubes, chunk,
    q_ref, k_ref, v_ref, do_ref, o_ref, linv_ref, e_ref, act, grads,
    dq_ref, dk_out, dv_out, act_full, total_out,
    vb, kt, qt, dox, dopb, dkt, dvt, dk, dv, dk_in, dv_in, lsem, ssem, rsem,
    total, terms, got_core, got_y, work, *rest,
):
    gots, (rs, rr) = rest[:-2], rest[-2:]
    n = pl.program_id(0)
    last = pl.num_programs(0) - 1
    h, g = n % 4, n // 4
    cube, b, y, c = place()
    chip, across, _ = peers()
    bits = cubes.bit_length() - 1
    keys = k_ref.shape[0]
    half_keys = keys // 2
    tokens = q_ref.shape[0]
    count = total.shape[0] // chunk

    def mine(d, span):
        return terms[d // 2, span]

    def term_copy(k):
        return pltpu.make_async_copy(grads.at[2 * k + c, pl.ds(0, count * chunk)], terms.at[k], lsem.at[2 + k])

    run, stages = reducer(cubes, chunk, grads, mine, got_core, got_y, work, gots, total, rs, rr)
    direct = count - SIDE_CHUNKS
    when = ([7, 11, 14, 18, 21, 25] + [28 + 3 * k for k in range(stages)])[: stages - 1]
    beside = ([2, 7, 11, 16, 19, 22, 26] + [29 + 3 * k for k in range(stages)])[:stages]
    polls = 2 * (last + 1)
    plan = [(at, s, 0, direct, False) for s, at in enumerate(when, 2)]
    plan += [(at, s, direct, SIDE_CHUNKS, True) for s, at in enumerate(beside, 1)]
    plan = sorted(plan, key=lambda entry: -entry[1])

    def poll(parity):
        @pl.when(2 * n + parity <= (direct + 1) // 2)
        def _():
            for u in range(2):
                t = 2 * (2 * n + parity - 1) + u

                @pl.when((t >= 0) & (t < direct))
                def _(t=t):
                    run(1, t)

        for at, s, first, size, side in plan:
            if at % 2 == parity and size:
                t = n - at // 2

                @pl.when((t >= 0) & (t < size))
                def _(s=s, t=t, first=first, side=side):
                    run(s, first + t, side)

    def act_far():
        return remote(act.at[1 - y], act_full.at[y], ssem.at[8], rsem.at[8], across)

    def act_own():
        return pltpu.make_async_copy(act.at[y], act_full.at[y], lsem.at[0])

    greeted = (chip, across) + tuple(mate_of(k) for k in range(bits))

    @pl.when(n == 0)
    def _():
        term_copy(0).start()
        term_copy(1).start()
        hail(greeted)
        act_own().start()

    lane = iota((keys, 128), 1)

    @pl.when(h == 0)
    def _():
        kt[...] = k_ref[...].astype(f32).T.astype(bf16)
        qt[...] = q_ref[...].astype(f32).T.astype(bf16)
        parts, sums = [], []
        for k in range(4):
            span = slice(k * HDIM, (k + 1) * HDIM)
            part = do_ref[span].astype(f32) * linv_ref[k, 0:1, :]
            parts.append(part)
            sums.append(jnp.sum(part * o_ref[span], axis=0, keepdims=True))
        part = jnp.concatenate(parts, axis=0)
        dopb[...] = part.astype(bf16)
        dox[:, 0:128] = part.T.astype(bf16)
        inner = -jnp.concatenate(sums + [jnp.zeros((4, tokens), f32)], axis=0)
        high = inner.astype(bf16).astype(f32)
        ext = jnp.concatenate([high, inner - high, jnp.zeros((112, tokens), f32)], axis=0)
        dox[:, 128:256] = ext.T.astype(bf16)

    @pl.when(n == 0)
    def _():
        meet(greeted)
        for t in range(direct):
            run(0, t)
            if t < SIDE_CHUNKS:
                run(0, direct + t)
        term_copy(0).wait()
        term_copy(1).wait()

    @pl.when(n > 0)
    def _():
        poll(0)

    @pl.when(n == 9)
    def _():
        act_far().start()

    v = v_ref[...]
    vb[:, 0:128] = jnp.where((lane // HDIM) == h, v, jnp.zeros_like(v))
    vb[:, 128:256] = jnp.where((lane == h) | (lane == 8 + h), 1.0, 0.0).astype(bf16)
    span = pl.ds(pl.multiple_of(h * HDIM, HDIM), HDIM)
    pieces = 2
    block = tokens // pieces
    for j in range(pieces):
        cols = slice(j * block, (j + 1) * block)
        dp = lax.dot_general(dox[cols], vb[...], NT, preferred_element_type=f32)
        e = e_ref[0, cols]
        ds = (e.astype(f32) * dp).astype(bf16)
        dqt = lax.dot_general(kt[span], ds, NT, preferred_element_type=f32)
        dq_ref[:, cols] = (dqt * HDIM ** (-0.5)).astype(bf16)
        kk = jnp.dot(qt[span, cols], ds, preferred_element_type=f32)
        vv = jnp.dot(dopb[span, cols], e, preferred_element_type=f32)
        if j == 0:
            dkt[...] = kk
            dvt[...] = vv
            poll(1)
        else:
            dk[g, span] = ((dkt[...] + kk) * (1.0 / LOG2E)).astype(bf16)
            dv[g, span] = (dvt[...] + vv).astype(bf16)

    def exchange(k):
        theirs = pl.ds(pl.multiple_of((1 - c) * half_keys, 128), half_keys)
        return (
            remote(dk.at[k, :, theirs], dk_in.at[k], ssem.at[2 * k], rsem.at[2 * k], chip),
            remote(dv.at[k, :, theirs], dv_in.at[k], ssem.at[2 * k + 1], rsem.at[2 * k + 1], chip),
        )

    @pl.when(h == 3)
    def _():
        for copy in exchange(g):
            copy.start()

    @pl.when(n == last)
    def _():
        mine = pl.ds(pl.multiple_of(c * half_keys, 128), half_keys)
        for tick in range(polls, max(when[-1] + 2 * direct, beside[-1] + 2 * SIDE_CHUNKS)):
            for at, s, first, size, side in plan:
                late = tick - at
                if late >= 0 and late % 2 == 0 and late // 2 < size:
                    run(s, first + late // 2, side)
        give = pltpu.make_async_copy(total, total_out, lsem.at[1])
        give.start()
        for k in range(4):
            for copy in exchange(k):
                copy.wait()
            band = slice(k * 128, (k + 1) * 128)
            dk_out[band] = dk[k, :, mine] + dk_in[k]
            dv_out[band] = dv[k, :, mine] + dv_in[k]
        act_far().wait()
        act_own().wait()
        give.wait()


def attend_back(cubes, q, k, v, do, ot, linv, e, act, grads):
    tokens, model = q.shape
    keys = k.shape[0]
    width = grads.shape[2]
    chunk = chunk_rows(cubes)
    depth = grads.shape[1] - LATE_CHUNKS * chunk
    sds = jax.ShapeDtypeStruct

    def cols(size):
        return pl.BlockSpec((size, 128), lambda n: (0, n // 4))

    fixed = pl.BlockSpec((model, tokens), lambda n: (0, 0))
    return pl.pallas_call(
        functools.partial(backward_kernel, cubes, chunk),
        name="attend_back",
        grid=(HEADS,),
        in_specs=[
            cols(tokens), cols(keys), cols(keys),
            pl.BlockSpec((128, tokens), lambda n: (n // 4, 0)),
            pl.BlockSpec((128, tokens), lambda n: (n // 4, 0)),
            pl.BlockSpec((4, 8, tokens), lambda n: (n // 4, 0, 0)),
            pl.BlockSpec((1, tokens, keys), lambda n: (n, 0, 0)),
            ANY,
            ANY,
        ],
        out_specs=[pl.BlockSpec((HDIM, tokens), lambda n: (n, 0)), fixed, fixed, ANY, ANY],
        out_shape=[
            sds((model, tokens), bf16),
            sds((model, tokens), bf16),
            sds((model, tokens), bf16),
            sds(act.shape, bf16),
            sds((depth, width), bf16),
        ],
        scratch_shapes=[
            pltpu.VMEM((keys, 256), bf16),
            pltpu.VMEM((128, keys), bf16),
            pltpu.VMEM((128, tokens), bf16),
            pltpu.VMEM((tokens, 256), bf16),
            pltpu.VMEM((128, tokens), bf16),
            pltpu.VMEM((HDIM, keys), f32),
            pltpu.VMEM((HDIM, keys), f32),
            pltpu.VMEM((4, 128, keys), bf16),
            pltpu.VMEM((4, 128, keys), bf16),
            pltpu.VMEM((4, 128, tokens), bf16),
            pltpu.VMEM((4, 128, tokens), bf16),
            pltpu.SemaphoreType.DMA((4,)),
            pltpu.SemaphoreType.DMA((9,)),
            pltpu.SemaphoreType.DMA((9,)),
            pltpu.VMEM((depth, width), bf16),
            pltpu.VMEM((2, depth, width), bf16),
        ] + reducer_scratch(cubes, depth // chunk, depth, width),
        compiler_params=params(2),
    )(q, k, v, do, ot, linv, e, act, grads)


def project_back_kernel(
    cubes, chunk,
    dq_in, dk_in, dv_in, first_hbm, embedded_in, middle_in, qkvw_in, embw_in, enc_in, tgt, vecf, sums, early,
    total, vis_out,
    dq, dk, dv, first_in, embedded, grad_middle, qkvw, embw, enc, isem,
    grads, first_t, gft, vgrad, vis_in, lsem, vs, vr, got_core, got_y, work, *rest,
):
    gots, (rs, rr) = rest[:-2], rest[-2:]
    cube, b, y, c = place()
    chip, across, diag = peers()
    bits = cubes.bit_length() - 1
    tokens, model = first_in.shape
    half = tokens // 2
    slots = enc.shape[0]
    er = embw.shape[0] // 4
    qr = model // 4
    first = LATE_CHUNKS * chunk
    left = range(LATE_CHUNKS)
    count = grads.shape[1] // chunk
    middle = range(LATE_CHUNKS, LATE_CHUNKS + 3 * qr // chunk)
    final = range(LATE_CHUNKS + 3 * qr // chunk, count)

    def mine(d, span):
        return grads[d, span]

    run, stages = reducer(cubes, chunk, grads, mine, got_core, got_y, work, gots, total, rs, rr)

    def runs(s, chunks):
        for t in chunks:
            run(s, t, "joint" if chunks is final else chunks is left)

    fetch = pltpu.make_async_copy(
        early.at[:, pl.ds(early.shape[1] - first, first)], grads.at[:, pl.ds(0, first)], lsem.at[1]
    ) if first else None
    if first:
        fetch.start()
    greeted = (chip, across, diag, corner()) + tuple(mate_of(k) for k in range(bits))
    hail(greeted)

    loads = []
    for k, (src, dst) in enumerate((
        (first_hbm, first_in), (dq_in, dq), (dk_in, dk), (dv_in, dv), (qkvw_in, qkvw), (embedded_in, embedded),
        (middle_in, grad_middle), (enc_in, enc), (embw_in, embw),
    )):
        loads.append(pltpu.make_async_copy(src, dst, isem.at[k]))
        loads[-1].start()
    loads[0].wait()
    first_t[...] = first_in[...].astype(f32).T.astype(bf16)
    if first:
        fetch.wait()
    meet(greeted)
    runs(0, left)
    for k, part in enumerate((dq, dk, dv)):
        loads[1 + k].wait()
        term = lax.dot_general(first_t[...], part[...], NT, preferred_element_type=f32).astype(bf16)
        for d in range(4):
            grads[d, first + k * qr : first + (k + 1) * qr] = term[d * qr : (d + 1) * qr]
        if k == 1:
            runs(1, left)
    runs(0, middle)
    ones = jnp.ones((8, tokens), bf16)
    qsum = lax.dot_general(ones, dq[...], NT, preferred_element_type=f32)[0:1]
    vsum = lax.dot_general(ones, dv[...], NT, preferred_element_type=f32)[0:1]
    (gain,) = unpack(vecf, ((2, 1, ALL),))
    column = tgt[...].astype(f32).T[:, 0:1].astype(jnp.int32)
    for copy in loads[4:]:
        copy.wait()
    gft[...] = (
        jnp.dot(qkvw[:, 0:model], dq[...], preferred_element_type=f32)
        + jnp.dot(qkvw[:, model : 2 * model], dk[...], preferred_element_type=f32)
        + jnp.dot(qkvw[:, 2 * model :], dv[...], preferred_element_type=f32)
    )
    runs(1, middle)
    gsum = [jnp.zeros((1, model), f32)] * 3
    lifted = None
    for h in range(2):
        span = pl.ds(h * half, half)
        gf = gft[:, span].T
        value = embedded[span]
        center = value - jnp.mean(value, axis=-1, keepdims=True)
        rstd = lax.rsqrt(jnp.mean(center * center, axis=-1, keepdims=True) + EPS)
        normed = center * rstd
        gsum[0] += jnp.sum(gf * normed, axis=0, keepdims=True)
        gsum[1] += jnp.sum(gf, axis=0, keepdims=True)
        gn = gf * gain
        back = rstd * (
            gn - jnp.mean(gn, axis=-1, keepdims=True) - normed * jnp.mean(gn * normed, axis=-1, keepdims=True)
        )
        ge = grad_middle[span] + back
        offset = y * half + h * 2 * half
        hit = (iota((half, slots), 0) + offset == tgt[0:1]).astype(f32)
        flag = jnp.sum(hit, axis=1, keepdims=True)
        gsum[2] += jnp.sum((1.0 - flag) * ge, axis=0, keepdims=True)
        hit_t = (iota((slots, half), 1) + offset == column).astype(bf16)
        term = jnp.dot(hit_t, ge.astype(bf16), preferred_element_type=f32)
        lifted = term if lifted is None else lifted + term
        runs(2 + h, left)
    bsum = jnp.sum(lifted, axis=0, keepdims=True)
    low = lifted.astype(bf16)
    at = first + 3 * qr
    gemb = jnp.dot(enc[...].astype(f32).T.astype(bf16), low, preferred_element_type=f32).astype(bf16)
    for d in range(4):
        grads[d, at : at + er] = gemb[d * er : (d + 1) * er]

    def lanes(value, d, size=128):
        return value[:, d * size : (d + 1) * size]

    down_s, out_s, gain_s, bias_s = (sums[k : k + 1] for k in range(4))
    pad = grads.shape[1] - at - er
    for d in range(4):
        part = qsum if d < 2 else vsum
        blank = jnp.zeros((1, model // 2), f32)
        packed = [
            jnp.concatenate([lanes(bsum, d), lanes(gsum[2], d), lanes(gsum[0], d), lanes(gsum[1], d)], axis=1),
            jnp.concatenate([lanes(part, d % 2, 256), lanes(out_s, d), lanes(gain_s, d)], axis=1),
            sums[4 + d : 5 + d],
            jnp.concatenate([lanes(bias_s, d), lanes(down_s, d), blank], axis=1),
        ]
        packed = jnp.concatenate(packed + [jnp.zeros((pad - 4, model), f32)], axis=0)
        grads[d, at + er :] = packed.astype(bf16)
    runs(0, final)
    runs(2, middle)
    runs(4, left)
    vgrad[...] = (
        lax.dot_general(low, embw[...], NT, preferred_element_type=f32).astype(bf16).reshape(vgrad.shape)
    )
    vis_copies = [
        remote(vgrad.at[2 * (1 - y) + c], vis_in.at[y, :, c], vs.at[0], vr.at[0], across),
        remote(vgrad.at[2 * (1 - y) + 1 - c], vis_in.at[y, :, c], vs.at[1], vr.at[1], diag),
        remote(vgrad.at[2 * y + 1 - c], vis_in.at[y, :, c], vs.at[2], vr.at[2], chip),
        pltpu.make_async_copy(vgrad.at[b], vis_in.at[y, :, c], lsem.at[0]),
    ]
    runs(1, final)
    for copy in vis_copies:
        copy.start()
    runs(3, middle)
    runs(5, left)
    for step in range(2, stages + 1):
        if 4 + step <= stages:
            runs(4 + step, left)
        if step + 2 <= stages:
            runs(step + 2, middle)
        if step < stages:
            runs(step, final)
    for copy in vis_copies:
        copy.wait()
    vis_out[...] = vis_in[0] + vis_in[1]


def project_back(cubes, dq, dk, dv, first_in, embedded, grad_middle, qkvw, embw, enc, tgt, vecf, sums, early, cap):
    tokens, model = first_in.shape
    chunk = chunk_rows(cubes)
    depth = 3 * model // 4 + embw.shape[0] // 4 + 16
    depth = depth + -depth % chunk + LATE_CHUNKS * chunk
    enc_width = enc.shape[1]
    slots = enc.shape[0]
    sds = jax.ShapeDtypeStruct
    return pl.pallas_call(
        functools.partial(project_back_kernel, cubes, chunk),
        name="project_back",
        out_shape=(sds((depth, model), bf16), sds((2, 2, cap, enc_width), bf16)),
        in_specs=[ANY] * 9 + [VM] * 3 + [ANY],
        out_specs=(VM, VM),
        scratch_shapes=[pltpu.VMEM((model, tokens), bf16)] * 3 + [
            pltpu.VMEM((tokens, model), bf16),
            pltpu.VMEM((tokens, model), f32),
            pltpu.VMEM((tokens, model), f32),
            pltpu.VMEM(qkvw.shape, bf16),
            pltpu.VMEM(embw.shape, bf16),
            pltpu.VMEM(enc.shape, bf16),
            pltpu.SemaphoreType.DMA((9,)),
            pltpu.VMEM((4, depth, model), bf16),
            pltpu.VMEM((model, tokens), bf16),
            pltpu.VMEM((model, tokens), f32),
            pltpu.VMEM((4, 2, cap, enc_width), bf16),
            pltpu.VMEM((2, 2, 2, cap, enc_width), bf16),
            pltpu.SemaphoreType.DMA((2,)),
            pltpu.SemaphoreType.DMA((3,)),
            pltpu.SemaphoreType.DMA((3,)),
        ] + reducer_scratch(cubes, depth // chunk, depth, model),
        compiler_params=params(3),
    )(dq, dk, dv, first_in, embedded, grad_middle, qkvw, embw, enc, tgt, vecf, sums, early)


def finish_kernel(late, first, second, down, up, out, qkv, emb, *vectors):
    model = down.shape[1]
    parts = up.shape[1] // model
    size = up.shape[0]
    start = first.shape[0]

    def early(at, count):
        if at + count <= start:
            return first[at : at + count].astype(f32)
        if at >= start:
            return second[at - start : at - start + count].astype(f32)
        return jnp.concatenate(
            [first[at:start].astype(f32), second[0 : at + count - start].astype(f32)], axis=0
        )

    down[...] = early(0, model).T
    for k in range(parts):
        up[:, k * model : (k + 1) * model] = early(model + k * size, size)
    out[...] = early(model + parts * size, size)
    for k in range(3):
        qkv[:, k * model : (k + 1) * model] = second[late + k * size : late + (k + 1) * size].astype(f32)
    at = late + 3 * size
    er = emb.shape[0]
    emb[...] = second[at : at + er].astype(f32)
    packed = second[at + er : at + er + 16].astype(f32)
    pieces = iter(vectors)
    for row, widths in enumerate(((128, 128, 128, 128), (256, 128, 128), (512,), (128, 128))):
        lane = 0
        for width in widths:
            next(pieces)[...] = packed[row : row + 1, lane : lane + width]
            lane += width


def finish(late, first, second, shapes):
    sds = jax.ShapeDtypeStruct
    widths = (128, 128, 128, 128, 256, 128, 128, 512, 128, 128)
    return pl.pallas_call(
        functools.partial(finish_kernel, late),
        name="results",
        out_shape=tuple(sds(s, f32) for s in shapes) + tuple(sds((1, w), f32) for w in widths),
        in_specs=[VM, VM],
        out_specs=tuple([VM] * (len(shapes) + len(widths))),
        compiler_params=params(),
    )(first, second)


def shards(
    cubes,
    visible, kept_rows, slot_counts, patches, positions, embedder, embedbias, masktoken, attngain, attnbias,
    qkvproj, qvbias, outproj, outbias, mlpgain, mlpbias, upproj, upbias, downproj, downbias, cotangent,
):
    cap, enc_width = visible.shape[2:]
    vis = visible.reshape(2, 2, cap, enc_width)
    vecs = [
        m.reshape(-1, 128)
        for m in (embedbias, masktoken, attngain, attnbias, qvbias, outbias, mlpgain, mlpbias, upbias, downbias)
    ]
    embedded, first_in, q, k, v, emb_full, qkv_full, enc, target, vecf = embed(
        vis, kept_rows[0], slot_counts, embedder, qkvproj, positions, vecs
    )
    own = (outproj, upproj, downproj, cotangent)
    e, ot, linv, mixed, *gathered = attend(patches, q, k, v, *own)
    act, grads, grad_middle, grad_mixed, sums = mlp(cubes, patches, vecf, mixed, ot, embedded, gathered, own)
    dq, dk, dv, activations, first = attend_back(cubes, q, k, v, grad_mixed, ot, linv, e, act, grads)
    second, visible_grad = project_back(
        cubes, dq, dk, dv, first_in, embedded, grad_middle, qkv_full, emb_full, enc.reshape(-1, enc_width), target, vecf, sums, grads, cap
    )
    shapes = (downproj.shape, upproj.shape, outproj.shape, qkvproj.shape, embedder.shape)
    down_o, up_o, out_o, qkv_o, emb_o, *small = finish(LATE_CHUNKS * chunk_rows(cubes), first, second, shapes)
    ebias, mask, again, abias, qv, outb, mgain, upb, mbias, downb = (m.reshape(-1) for m in small)
    return (
        activations, visible_grad.reshape(visible.shape), emb_o, ebias, mask, again, abias, qkv_o, qv,
        out_o, outb, mgain, mbias, up_o, upb, down_o, downb,
    )


def solution(mesh):
    cubes = mesh.shape["cube"]
    split = P(("cube", "band"), None, None, None)
    mat, row = P("band", None), P("band")
    placed = (
        split, P(("cube", "band"), None, None), P(("cube", "band"), None), P("cube"), mat,
        mat, row, row, row, row, mat, row, mat, row, row, row, mat, row, mat, row, P("cube", "band", None),
    )
    return jax.shard_map(
        functools.partial(shards, cubes),
        mesh=mesh,
        in_specs=placed,
        out_specs=(
            P("cube", "band", None), split, mat, row, row, row, row, mat, row, mat, row, row, row, mat, row, mat, row,
        ),
        check_vma=False,
    )
```

```python
import functools

import jax
import jax.numpy as jnp
from jax import lax
from jax.experimental import pallas as pl
from jax.experimental.pallas import tpu as pltpu
from jax.sharding import PartitionSpec as P

HEADS = 16
LATE_CHUNKS = 1
SIDE_CHUNKS = 2
HDIM = 32
EPS = 1e-06
LOG2E = 1.4426950408889634
QSCALE = HDIM ** (-0.5) * LOG2E
MESH = pl.DeviceIdType.MESH
NT = (((1,), (1,)), ((), ()))
f32 = jnp.float32
bf16 = jnp.bfloat16
ANY = pl.BlockSpec(memory_space=pl.ANY)
VM = pl.BlockSpec(memory_space=pltpu.VMEM)
VMEM_LIMIT = 60 * 2**20


def iota(shape, dim):
    return lax.broadcasted_iota(jnp.int32, shape, dim)


def normalize(values):
    center = values - jnp.mean(values, axis=-1, keepdims=True)
    spread = jnp.mean(center * center, axis=-1, keepdims=True)
    return center * lax.rsqrt(spread + EPS)


def place():
    cube, band = lax.axis_index("cube"), lax.axis_index("band")
    y, c = band // 2, band % 2
    return cube, band, y, c


def peers():
    cube, band, y, c = place()
    same_chip = (cube, 2 * y + 1 - c)
    across = (cube, 2 * (1 - y) + c)
    diagonal = (cube, 2 * (1 - y) + 1 - c)
    return same_chip, across, diagonal


def hail(devices):
    barrier = pltpu.get_barrier_semaphore()
    for device in devices:
        pl.semaphore_signal(barrier, inc=1, device_id=device, device_id_type=MESH)


def meet(devices):
    pl.semaphore_wait(pltpu.get_barrier_semaphore(), len(devices))


def remote(src, dst, send, recv, device):
    return pltpu.make_async_remote_copy(
        src_ref=src, dst_ref=dst, send_sem=send, recv_sem=recv, device_id=device, device_id_type=MESH
    )


def rows(start, size):
    return pl.ds(pl.multiple_of(start, 16), size)


def params(collective_id=None):
    if collective_id is None:
        return pltpu.CompilerParams(vmem_limit_bytes=VMEM_LIMIT)
    return pltpu.CompilerParams(collective_id=collective_id, has_side_effects=True, vmem_limit_bytes=VMEM_LIMIT)


def mate_of(k):
    cube, b, _, _ = place()
    d = 1 << k
    return (cube + d - 2 * d * ((cube // d) % 2), b)


def corner():
    _, _, y, c = place()
    return (mate_of(0)[0], 2 * (1 - y) + c)


def unpack(vecf, spans):
    vectors = vecf[...].astype(f32)
    out = []
    for first, count, bands in spans:
        out.append(
            jnp.concatenate([vectors[d, k : k + 1] for d in bands for k in range(first, first + count)], axis=1)
        )
    return out


ALL = (0, 1, 2, 3)


def embed_kernel(
    vis, kept_rows, counts, emb, qkv, pos, *refs,
):
    vecs = refs[:10]
    (embedded, first_in, q_out, k_out, v_out, emb_out, qkv_out, enc_out, tgt_out, vecf,
     enc, tgt, embf, qkvf, posf, vec, kbuf, vbuf, qbuf, ebuf, fbuf, kept, lsem, ssem, rsem) = refs[10:]
    cube, b, y, c = place()
    x = cube % 2
    chip, across, diag = peers()
    mate = mate_of(0)
    bq = 2 * (1 - y) + c
    er, qr = emb.shape[0], qkv.shape[0]
    half = pos.shape[0]
    model = emb.shape[1]
    hail((chip, across, diag, mate))
    fill = jnp.zeros((vec.shape[0] - sum(v.shape[0] for v in vecs), 128), f32)
    vec[...] = jnp.concatenate([v[...].astype(f32) for v in vecs] + [fill], axis=0).astype(bf16)
    cap = vis.shape[2]
    names = kept_rows[...].astype(f32)
    high = jnp.floor(names * (1.0 / 32.0))
    wide = tgt.shape[2]
    spread = (iota((cap, wide), 1) % cap == iota((cap, wide), 0)).astype(bf16)
    names = 32.0 * jnp.dot(high.astype(bf16), spread, preferred_element_type=f32) + jnp.dot(
        (names - 32.0 * high).astype(bf16), spread, preferred_element_type=f32
    )
    lane = iota((1, wide), 1)
    upper = (lane // cap) % 2 == 1
    for d in range(2):
        row = jnp.where(upper, names[2 + d : 3 + d] + 4.0 * pos.shape[0] / 2.0, names[d : d + 1])
        bound = jnp.where(upper, counts[0, 2 + d], counts[0, d])
        live = (lane % cap < bound) & (lane // (2 * cap) == b)
        row = jnp.where(live, row, -1.0).astype(jnp.int32)
        kept[d] = jnp.broadcast_to(row, kept.shape[1:])
    meet((chip, across, diag, mate))

    used = [0]
    local = []

    def send(src, dst, device):
        copy = remote(src, dst, ssem.at[used[0]], rsem.at[used[0]], device)
        used[0] += 1
        copy.start()
        return copy

    def keep(src, dst):
        copy = pltpu.make_async_copy(src, dst, lsem.at[len(local)])
        copy.start()
        local.append(copy)

    def cut(start, size, which):
        return rows(start + which * (size // 2), size // 2)

    def quarter(band, which, k):
        return rows(band * qr + which * (qr // 2) + k * (qr // 4), qr // 4)

    def strip(k):
        return rows(x * (half // 2) + k * (half // 4), half // 4)

    ea, qa = rows(b * er, er), rows(b * qr, qr)
    far_vec = send(vec, vecf.at[b], across)
    far_emb = send(emb.at[cut(0, er, x)], embf.at[cut(b * er, er, x)], across)
    small = [
        send(kept.at[c], tgt.at[b], across),
        send(vis.at[:, c], enc.at[b], across),
        send(kept.at[1 - c], tgt.at[b], diag),
        send(vis.at[:, 1 - c], enc.at[b], diag),
        send(kept.at[1 - c], tgt.at[b], chip),
        send(vec, vecf.at[b], chip),
        send(vis.at[:, 1 - c], enc.at[b], chip),
        send(emb, embf.at[ea], chip),
    ]
    far_pos = [send(pos.at[strip(k)], posf.at[y, strip(k)], across) for k in range(2)]
    far_qkv = [send(qkv.at[quarter(0, x, k)], qkvf.at[quarter(b, x, k)], across) for k in range(2)]
    near_qkv = send(qkv, qkvf.at[qa], chip)
    keep(kept.at[c], tgt.at[b])
    keep(vec, vecf.at[b])
    keep(vis.at[:, c], enc.at[b])
    keep(emb, embf.at[ea])
    keep(pos, posf.at[y])
    keep(qkv, qkvf.at[qa])

    far_vec.wait()
    relays = [send(vecf.at[bq], vecf.at[bq], chip)]
    far_emb.wait()
    got = cut(bq * er, er, x)
    side_emb = send(embf.at[got], embf.at[got], mate)
    relays.append(send(embf.at[got], embf.at[got], chip))
    side_emb.wait()
    got = cut(bq * er, er, 1 - x)
    relays.append(send(embf.at[got], embf.at[got], chip))
    side_pos = []
    for k in range(2):
        far_pos[k].wait()
        got = posf.at[1 - y, strip(k)]
        side_pos.append(send(got, got, mate))
    for copy in small + local + relays:
        copy.wait()

    target = jnp.max(tgt[...].astype(f32), axis=0)[0:1].astype(jnp.int32)
    tgt_out[...] = jnp.broadcast_to(target, tgt_out.shape)
    slots = 8 * cap
    enc_all = enc[...].reshape(slots, enc.shape[3])
    results = []

    def give(src, dst):
        copy = pltpu.make_async_copy(src, dst, lsem.at[8 + len(results)])
        copy.start()
        results.append(copy)

    give(enc, enc_out)
    give(embf, emb_out)
    embedbias, mask, gain, bias, qbias, vbias = unpack(
        vecf, ((0, 1, ALL), (1, 1, ALL), (2, 1, ALL), (3, 1, ALL), (4, 2, (0, 1)), (4, 2, (2, 3)))
    )

    def lift(h):
        span = rows(h * half, half)
        cells = iota((half, slots), 0) + (y * half + h * 2 * half)
        hit = (cells == target).astype(f32)
        flag = jnp.sum(hit, axis=1, keepdims=True)
        picked = jnp.dot(hit.astype(bf16), enc_all, preferred_element_type=f32).astype(bf16)
        rows_in = jnp.dot(picked, embf[...], preferred_element_type=f32)
        v = rows_in + flag * embedbias + (1.0 - flag) * mask + posf[h].astype(f32)
        ebuf[span] = v
        fbuf[span] = (normalize(v) * gain + bias).astype(bf16)
        give(ebuf.at[span], embedded.at[span])
        give(fbuf.at[span], first_in.at[span])

    lift(y)
    side_qkv, late = [], []
    for k in range(2):
        far_qkv[k].wait()
        got = quarter(bq, x, k)
        side_qkv.append(send(qkvf.at[got], qkvf.at[got], mate))
        late.append(send(qkvf.at[got], qkvf.at[got], chip))
    for copy in side_pos:
        copy.wait()
    lift(1 - y)
    for k in range(2):
        side_qkv[k].wait()
        got = quarter(bq, 1 - x, k)
        late.append(send(qkvf.at[got], qkvf.at[got], chip))
    near_qkv.wait()
    for copy in late:
        copy.wait()
    give(qkvf, qkv_out)
    mine = rows(c * 2 * half, 2 * half)
    first = fbuf[...]
    k = jnp.dot(first, qkvf[:, model : 2 * model], preferred_element_type=f32)
    kbuf[...] = k.astype(bf16)
    out = [send(kbuf, k_out.at[mine], chip)]
    give(kbuf, k_out.at[mine])
    v = jnp.dot(first, qkvf[:, 2 * model :], preferred_element_type=f32)
    vbuf[...] = (v + vbias).astype(bf16)
    out.append(send(vbuf, v_out.at[mine], chip))
    give(vbuf, v_out.at[mine])
    q = jnp.dot(first, qkvf[:, :model], preferred_element_type=f32)
    qbuf[...] = ((q + qbias) * QSCALE).astype(bf16)
    give(qbuf, q_out)
    for copy in out + results:
        copy.wait()


def embed(vis, kept_rows, counts, emb, qkv, pos, vecs):
    er, model = emb.shape
    qr, wide = qkv.shape
    half = pos.shape[0]
    enc_width = vis.shape[-1]
    cap = vis.shape[2]
    slots = 8 * cap
    tokens = 2 * half
    sds = jax.ShapeDtypeStruct
    return pl.pallas_call(
        embed_kernel,
        name="embed_project",
        out_shape=(
            sds((tokens, model), f32),
            sds((tokens, model), bf16),
            sds((tokens, model), bf16),
            sds((2 * tokens, model), bf16),
            sds((2 * tokens, model), bf16),
            sds((4 * er, model), bf16),
            sds((4 * qr, wide), bf16),
            sds((4, 2, cap, enc_width), bf16),
            sds((8, slots), jnp.int32),
            sds((4, 16, 128), bf16),
        ),
        in_specs=[ANY, VM, pl.BlockSpec(memory_space=pltpu.SMEM), ANY, ANY, ANY] + [VM] * 10,
        out_specs=(ANY,) * 8 + (VM, VM),
        scratch_shapes=[
            pltpu.VMEM((4, 2, cap, enc_width), bf16),
            pltpu.VMEM((4, 8, slots), jnp.int32),
            pltpu.VMEM((4 * er, model), bf16),
            pltpu.VMEM((4 * qr, wide), bf16),
            pltpu.VMEM((2, half, model), bf16),
            pltpu.VMEM((16, 128), bf16),
            pltpu.VMEM((tokens, model), bf16),
            pltpu.VMEM((tokens, model), bf16),
            pltpu.VMEM((tokens, model), bf16),
            pltpu.VMEM((tokens, model), f32),
            pltpu.VMEM((tokens, model), bf16),
            pltpu.VMEM((2, 8, slots), jnp.int32),
            pltpu.SemaphoreType.DMA((20,)),
            pltpu.SemaphoreType.DMA((32,)),
            pltpu.SemaphoreType.DMA((32,)),
        ],
        compiler_params=params(0),
    )(vis, kept_rows, counts, emb, qkv, pos, *vecs)


def forward_kernel(
    patch, q_ref, k_ref, v_ref, outw, upw, downw, cot,
    e_ref, o_ref, linv_ref, mix_ref, out_full, up_full, down_full, cot_full,
    kx, vt, sa, sb, ots, ssem, rsem,
):
    p = pl.program_id(0)
    last = pl.num_programs(0) - 1
    cube, b, y, c = place()
    x = cube % 2
    chip, across, _ = peers()
    mate = mate_of(0)
    bq = 2 * (1 - y) + c
    shards = ((upw, up_full), (outw, out_full), (downw, down_full))

    def cut(k, band, which):
        size = shards[k][0].shape[0]
        return rows(band * size + which * (size // 2), size // 2)

    def far(k):
        size = shards[k][0].shape[0]
        part = rows(x * (size // 2), size // 2)
        return remote(shards[k][0].at[part], shards[k][1].at[cut(k, b, x)], ssem.at[k], rsem.at[k], across)

    def near(k):
        size = shards[k][0].shape[0]
        return remote(shards[k][0], shards[k][1].at[rows(b * size, size)], ssem.at[3 + k], rsem.at[3 + k], chip)

    def side(k):
        ref = shards[k][1].at[cut(k, bq, x)]
        return remote(ref, ref, ssem.at[6 + k], rsem.at[6 + k], mate)

    def relay(k, which):
        ref = shards[k][1].at[cut(k, bq, x if which == 0 else 1 - x)]
        at = 9 + 2 * k + which
        return remote(ref, ref, ssem.at[at], rsem.at[at], chip)

    def cot_far():
        return remote(cot.at[1 - y], cot_full, ssem.at[15], rsem.at[15], across)

    @pl.when(p == 0)
    def _():
        hail((chip, across, mate))

    keys = k_ref.shape[0]
    tokens = q_ref.shape[0]
    lane = iota((keys, 128), 1)
    pieces = 3
    block = tokens // pieces

    @pl.when(p == 0)
    def _():
        row = iota((keys, 128), 0)
        bias = jnp.where((row % cot.shape[1] >= patch[y]) & (lane == 0), -1e30, 0.0).astype(bf16)
        for g in range(v_ref.shape[1] // 128):
            cols = slice(g * 128, (g + 1) * 128)
            kx[g, :, 0:128] = k_ref[:, cols]
            kx[g, :, 128:256] = bias
            vt[cols] = v_ref[:, cols].astype(f32).T.astype(bf16)

    def lanes(h):
        return pl.ds(pl.multiple_of((h // 4) * 128, 128), 128)

    narrow = iota((block, 128), 1) // HDIM

    def score(h, s, j):
        span = slice(j * block, (j + 1) * block)
        q = q_ref[span, lanes(h)]
        q = jnp.where(narrow == h % 4, q, jnp.zeros_like(q))
        qx = jnp.concatenate([q, jnp.ones((block, 128), bf16)], axis=1)
        s[span] = lax.dot_general(qx, kx[h // 4], NT, preferred_element_type=f32)

    ones = jnp.ones((16, keys), bf16)

    def soften(at, h, s, j):
        span = slice(j * block, (j + 1) * block)
        v = s[span]
        e = jnp.exp2(v - jnp.max(v, axis=1, keepdims=True)).astype(bf16)
        e_ref[at, span] = e
        lhs = jnp.concatenate([vt[pl.ds(pl.multiple_of(h * HDIM, HDIM), HDIM)], ones], axis=0)
        ot = lax.dot_general(lhs, e, NT, preferred_element_type=f32)
        li = 1.0 / ot[HDIM : HDIM + 8]
        o = ot[:HDIM] * li[0:1]
        o_ref[at * HDIM : (at + 1) * HDIM, span] = o
        ots[pl.ds(pl.multiple_of((p % 2) * 2 * HDIM + at * HDIM, HDIM), HDIM), span] = o
        linv_ref[at, :, span] = li

    @pl.when(p == 0)
    def _():
        for j in range(pieces):
            score(0, sa, j)
        meet((chip, across, mate))
        far(0).start()
        far(1).start()
        far(2).start()
        cot_far().start()
        for k in range(3):
            near(k).start()

    for k, at in ((0, 2), (1, 3), (2, 4)):

        @pl.when(p == at)
        def _(k=k):
            far(k).wait()
            side(k).start()
            relay(k, 0).start()

    for k, at in ((0, 5), (1, 6), (2, 7)):

        @pl.when(p == at)
        def _(k=k):
            side(k).wait()
            relay(k, 1).start()

    after = jnp.minimum(2 * p + 2, 2 * last + 1)
    for j in range(pieces):
        score(2 * p + 1, sb, j)
        soften(0, 2 * p, sa, j)
    for j in range(pieces):
        score(after, sa, j)
        soften(1, 2 * p + 1, sb, j)

    @pl.when(p % 2 == 1)
    def _():
        mix_ref[...] = ots[...].T.astype(bf16)

    @pl.when(p == last)
    def _():
        cot_far().wait()
        for k in range(3):
            near(k).wait()
            relay(k, 0).wait()
            relay(k, 1).wait()


def attend(patch, q, k, v, outw, upw, downw, cot):
    tokens, model = q.shape
    keys = k.shape[0]
    sds = jax.ShapeDtypeStruct

    def fixed(shape):
        return pl.BlockSpec(shape, lambda p: (0, 0))

    return pl.pallas_call(
        forward_kernel,
        name="attend",
        grid=(HEADS // 2,),
        in_specs=[
            pl.BlockSpec(memory_space=pltpu.SMEM),
            fixed(q.shape),
            fixed(k.shape),
            fixed(v.shape),
            ANY, ANY, ANY, ANY,
        ],
        out_specs=[
            pl.BlockSpec((2, tokens, keys), lambda p: (p, 0, 0)),
            pl.BlockSpec((2 * HDIM, tokens), lambda p: (p, 0)),
            pl.BlockSpec((2, 8, tokens), lambda p: (p, 0, 0)),
            pl.BlockSpec((tokens, 128), lambda p: (0, p // 2)),
            ANY, ANY, ANY, ANY,
        ],
        out_shape=[
            sds((HEADS, tokens, keys), bf16),
            sds((model, tokens), f32),
            sds((HEADS, 8, tokens), f32),
            sds((tokens, model), bf16),
            sds((4 * outw.shape[0], outw.shape[1]), bf16),
            sds((4 * upw.shape[0], upw.shape[1]), bf16),
            sds((4 * downw.shape[0], downw.shape[1]), bf16),
            sds(cot.shape[1:], bf16),
        ],
        scratch_shapes=[
            pltpu.VMEM((model // 128, keys, 256), bf16),
            pltpu.VMEM((model, keys), bf16),
            pltpu.VMEM((tokens, keys), f32),
            pltpu.VMEM((tokens, keys), f32),
            pltpu.VMEM((128, tokens), f32),
            pltpu.SemaphoreType.DMA((16,)),
            pltpu.SemaphoreType.DMA((16,)),
        ],
        compiler_params=params(1),
    )(patch, q, k, v, outw, upw, downw, cot)


def mlp_kernel(
    patch, vecf, mixed, mixed_t_in, embedded_in, out_got, up_got, down_got, cot_got, out_own, up_own, down_own, cot_own,
    act_out, grads_out, middle_out, mixed_out, sums,
    act, grads, grad_middle, grad_mixed, mixed_f, embedded_f, outw, upf, downf, cot, second_t, gout_t, second, active, hid, branch_b, wsem,
):
    _, b, y, _ = place()
    tokens, model = mixed.shape
    half = tokens // 2
    wide = upf.shape[1]
    parts = wide // model
    loads = []

    def load(src, dst):
        copy = pltpu.make_async_copy(src, dst, wsem.at[len(loads)])
        copy.start()
        loads.append(copy)

    mixed_t, embedded = mixed_f, embedded_f
    results = []

    def give(src, dst):
        copy = pltpu.make_async_copy(src, dst, wsem.at[16 + len(results)])
        copy.start()
        results.append(copy)

    for own, got, full in ((out_own, out_got, outw), (up_own, up_got, upf), (down_own, down_got, downf)):
        size = own.shape[0]
        load(own, full.at[rows(b * size, size)])
        for k in range(1, 4):
            part = rows((b + k) % 4 * size, size)
            load(got.at[part], full.at[part])
        if own is out_own:
            load(embedded_in, embedded_f)
    load(cot_own.at[y], cot.at[y])
    load(cot_got, cot.at[1 - y])
    load(mixed_t_in, mixed_f)
    vectors = vecf[...].astype(f32)

    def whole(k):
        return jnp.concatenate([vectors[d, k : k + 1] for d in range(4)], axis=1)

    outbias, gain, bias, downbias = whole(6), whole(7), whole(8), whole(13)
    upbias = [jnp.concatenate([vectors[d, 9 + k : 10 + k] for k in range(4)], axis=1) for d in range(parts)]
    live = iota((half, 1), 0) < patch[y]
    valid = jnp.where(live, 1.0, 0.0)
    total = [jnp.zeros((1, model), f32)] * (4 + parts)
    for copy in loads[:5]:
        copy.wait()
    for h in range(2):
        span = pl.ds(h * half, half)
        mix = mixed[span]
        middle = embedded[span] + (jnp.dot(mix, outw[...], preferred_element_type=f32) + outbias)
        center = middle - jnp.mean(middle, axis=-1, keepdims=True)
        rstd = lax.rsqrt(jnp.mean(center * center, axis=-1, keepdims=True) + EPS)
        normed = center * rstd
        sec = normed * gain + bias
        second_t[:, span] = sec.T.astype(bf16)
        sec = sec.astype(bf16)
        if h == 0:
            for copy in loads[5:-1]:
                copy.wait()
        gout = cot[h].astype(f32) * valid
        gout_t[:, span] = gout.T.astype(bf16)
        gout_b = gout.astype(bf16)
        total[0] += jnp.sum(gout, axis=0, keepdims=True)
        result = middle + downbias
        gsec = None
        for k in range(parts):
            cols = slice(k * model, (k + 1) * model)
            hidden = jnp.dot(sec, upf[:, cols], preferred_element_type=f32) + upbias[k]
            cdf = 0.5 + 0.5 * lax.erf(hidden * 0.7071067811865476)
            low = (hidden * cdf).astype(bf16)
            active[span, cols] = low
            slope = cdf + hidden * (0.3989422804014327 * jnp.exp(-0.5 * hidden * hidden))
            result += jnp.dot(low, downf[cols], preferred_element_type=f32)
            gact = lax.dot_general(gout_b, downf[cols], NT, preferred_element_type=f32)
            ghid = (gact * slope).astype(bf16)
            hid[span, cols] = ghid
            total[4 + k] += jnp.sum(ghid.astype(f32), axis=0, keepdims=True)
            term = lax.dot_general(ghid, upf[:, cols], NT, preferred_element_type=f32)
            gsec = term if gsec is None else gsec + term
        act[h] = (valid * result).astype(bf16)
        total[2] += jnp.sum(gsec * normed, axis=0, keepdims=True)
        total[3] += jnp.sum(gsec, axis=0, keepdims=True)
        gn = gsec * gain
        back = rstd * (
            gn - jnp.mean(gn, axis=-1, keepdims=True) - normed * jnp.mean(gn * normed, axis=-1, keepdims=True)
        )
        gmid = gout + back
        grad_middle[span] = gmid
        gb = gmid.astype(bf16)
        branch_b[span] = gb
        total[1] += jnp.sum(gb.astype(f32), axis=0, keepdims=True)
        grad_mixed[:, span] = lax.dot_general(outw[...], gb, NT, preferred_element_type=f32).astype(bf16)
        give(act.at[h], act_out.at[h])
        give(grad_middle.at[span], middle_out.at[span])
    give(grad_mixed, mixed_out)
    for k in range(parts):
        cols = slice(k * model, (k + 1) * model)
        grads[k, 0:model] = jnp.dot(gout_t[...], active[:, cols], preferred_element_type=f32).astype(bf16)
        gup = jnp.dot(second_t[...], hid[:, cols], preferred_element_type=f32).astype(bf16)
        size = model // 4
        for d in range(4):
            grads[d, model + k * size : model + (k + 1) * size] = gup[d * size : (d + 1) * size]
        give(grads.at[k, pl.ds(0, model)], grads_out.at[k, pl.ds(0, model)])
        part = pl.ds(model + k * size, size)
        give(grads.at[:, part], grads_out.at[:, part])
    base = model + parts * (model // 4)
    loads[-1].wait()
    gout_w = jnp.dot(mixed_t[...].astype(bf16), branch_b[...], preferred_element_type=f32).astype(bf16)
    for d in range(4):
        grads[d, base : base + model // 4] = gout_w[d * (model // 4) : (d + 1) * (model // 4)]
    spare = grads.shape[1] - base - model // 4
    if spare:
        grads[:, base + model // 4 :] = jnp.zeros((4, spare, model), bf16)
    part = pl.ds(base, grads.shape[1] - base)
    give(grads.at[:, part], grads_out.at[:, part])
    sums[...] = jnp.concatenate(total, axis=0)
    for copy in results:
        copy.wait()


def mlp(cubes, patch, vecf, mixed, mixed_t, embedded, gathered, own):
    tokens, model = mixed.shape
    outw, upw, downw, cot = own
    wide = upw.shape[1]
    half = cot.shape[1]
    depth = model + wide // 4 + model // 4
    depth += -depth % chunk_rows(cubes)
    sds = jax.ShapeDtypeStruct
    return pl.pallas_call(
        mlp_kernel,
        name="mlp_both",
        out_shape=(
            sds((2, half, model), bf16),
            sds((4, depth, model), bf16),
            sds((tokens, model), f32),
            sds((model, tokens), bf16),
            sds((4 + wide // model, model), f32),
        ),
        in_specs=[pl.BlockSpec(memory_space=pltpu.SMEM), VM, VM] + [ANY] * 10,
        out_specs=(ANY, ANY, ANY, ANY, VM),
        scratch_shapes=[
            pltpu.VMEM((2, half, model), bf16),
            pltpu.VMEM((4, depth, model), bf16),
            pltpu.VMEM((tokens, model), f32),
            pltpu.VMEM((model, tokens), bf16),
            pltpu.VMEM((model, tokens), f32),
            pltpu.VMEM((tokens, model), f32),
            pltpu.VMEM((model, model), bf16),
            pltpu.VMEM((model, wide), bf16),
            pltpu.VMEM((wide, model), bf16),
            pltpu.VMEM((2, half, model), bf16),
            pltpu.VMEM((model, tokens), bf16),
            pltpu.VMEM((model, tokens), bf16),
            pltpu.VMEM((tokens, model), bf16),
            pltpu.VMEM((tokens, wide), bf16),
            pltpu.VMEM((tokens, wide), bf16),
            pltpu.VMEM((tokens, model), bf16),
            pltpu.SemaphoreType.DMA((32,)),
        ],
        compiler_params=params(),
    )(patch, vecf, mixed, mixed_t, embedded, *gathered, *own)


def chunk_rows(cubes):
    return max(128, 8 * cubes)


def reducer(cubes, chunk, grads, mine, got_core, got_y, work, gots, total, ssem, rsem):
    cube, b, y, c = place()
    chip, across, _ = peers()
    bits = cubes.bit_length() - 1
    own, other = 2 * y + c, 2 * (1 - y) + c
    top = bits + 1

    def kept(k):
        start = 0
        for j in range(k):
            start = start + ((cube // (1 << j)) % 2) * (chunk >> (j + 1))
        return start

    def back(s, t):
        k = 2 * bits - s
        span = rows(t * chunk + kept(k + 1), chunk >> (k + 1))
        return total.at[span], total.at[span], mate_of(k)

    def core(t):
        span = rows(t * chunk, chunk)
        return [
            remote(grads.at[1 - c, span], got_core.at[0, span], ssem.at[t, 0], rsem.at[t, 0], chip),
            remote(grads.at[3 - c, span], got_core.at[1, span], ssem.at[t, 1], rsem.at[t, 1], chip),
        ]

    def step(k, t, both):
        side = pl.ds(0, 2) if both else pl.ds(0, 1)
        if k < bits - 1:
            size = chunk >> (k + 1)
            bit = (cube // (1 << k)) % 2
            away = rows(t * chunk + kept(k) + (1 - bit) * size, size)
        else:
            size = chunk >> k
            away = rows(t * chunk + kept(k), size)
        return work.at[side, away], gots[k].at[side, rows(t * size, size)], mate_of(k)

    def copies(s, t, side):
        if s == 0:
            return core(t)
        if side == "joint":
            first, second, part = halves(t)
            return [
                remote(work.at[1, first], got_y.at[first], ssem.at[t, 2], rsem.at[t, 2], across),
                remote(work.at[0, second], gots[0].at[0, part], ssem.at[t, 3], rsem.at[t, 3], mate_of(0)),
                remote(work.at[1, second], gots[0].at[1, part], ssem.at[t, more], rsem.at[t, more], corner()),
            ]
        if not side:
            if s == 1:
                span = rows(t * chunk, chunk)
                move = work.at[1, span], got_y.at[span], across
            elif s <= top:
                move = step(s - 2, t, False)
            else:
                move = back(s, t)
        elif s < top:
            move = step(s - 1, t, True)
        elif s == top:
            size = chunk >> (bits - 1)
            span = rows(t * chunk + kept(bits - 1), size)
            move = work.at[1, span], got_y.at[span], across
        else:
            move = back(s, t)
        return [remote(move[0], move[1], ssem.at[t, s + 1], rsem.at[t, s + 1], move[2])]

    more = 2 + 2 * bits

    def halves(t):
        size = chunk // 2
        x = cube % 2
        base = t * chunk
        return rows(base + x * size, size), rows(base + (1 - x) * size, size), rows(t * size, size)

    def run(s, t, side=False):
        if side == "joint" and s > 2:
            s, side = s + 1, False
        if side == "joint" and s == 2:
            for copy in copies(1, t, side):
                copy.wait()
            first, _, part = halves(t)
            work[0, first] = (work[0, first] + got_y[first]) + (gots[0][0, part] + gots[0][1, part])
            for copy in copies(3, t, False):
                copy.start()
            return
        if s > 0:
            for copy in copies(s - 1, t, side):
                copy.wait()
        span = rows(t * chunk, chunk)
        if s == 1:
            work[1, span] = mine(other, span) + got_core[1 - y, span]
            if side:
                work[0, span] = mine(own, span) + got_core[y, span]
        elif s == 2 and not side:
            work[0, span] = (mine(own, span) + got_core[y, span]) + got_y[span]
        elif 2 <= s <= top + 1:
            k = s - 2 if side else s - 3
            if side and s == top + 1:
                size = chunk >> (bits - 1)
                span = rows(t * chunk + kept(bits - 1), size)
                total[span] = work[0, span] + got_y[span]
            else:
                size = chunk >> min(k + 1, bits - 1)
                span = rows(t * chunk + kept(min(k + 1, bits - 1)), size)
                part = rows(t * size, size)
                if side:
                    work[:, span] = work[:, span] + gots[k][:, part]
                elif s <= top:
                    work[0, span] = work[0, span] + gots[k][0, part]
                else:
                    total[span] = work[0, span] + gots[k][0, part]
        if s < 1 + 2 * bits:
            for copy in copies(s, t, side):
                copy.start()

    return run, 1 + 2 * bits


def reducer_scratch(cubes, count, depth, width):
    bits = cubes.bit_length() - 1
    return [
        pltpu.VMEM((2, depth, width), bf16),
        pltpu.VMEM((depth, width), bf16),
        pltpu.VMEM((2, depth, width), bf16),
    ] + [pltpu.VMEM((2, depth >> min(k + 1, bits - 1), width), bf16) for k in range(bits)] + [
        pltpu.SemaphoreType.DMA((count, 3 + 2 * bits)),
        pltpu.SemaphoreType.DMA((count, 3 + 2 * bits)),
    ]


def backward_kernel(
    cubes, chunk,
    q_ref, k_ref, v_ref, do_ref, o_ref, linv_ref, e_ref, act, grads,
    dq_ref, dk_out, dv_out, act_full, total_out,
    vb, kt, qt, dox, dopb, dkt, dvt, dk, dv, dk_in, dv_in, lsem, ssem, rsem,
    total, terms, got_core, got_y, work, *rest,
):
    gots, (rs, rr) = rest[:-2], rest[-2:]
    n = pl.program_id(0)
    last = pl.num_programs(0) - 1
    h, g = n % 4, n // 4
    cube, b, y, c = place()
    chip, across, _ = peers()
    bits = cubes.bit_length() - 1
    keys = k_ref.shape[0]
    half_keys = keys // 2
    tokens = q_ref.shape[0]
    count = total.shape[0] // chunk

    def mine(d, span):
        return terms[d // 2, span]

    def term_copy(k):
        return pltpu.make_async_copy(grads.at[2 * k + c, pl.ds(0, count * chunk)], terms.at[k], lsem.at[2 + k])

    run, stages = reducer(cubes, chunk, grads, mine, got_core, got_y, work, gots, total, rs, rr)
    direct = count - SIDE_CHUNKS
    when = ([7, 11, 14, 18, 21, 25] + [28 + 3 * k for k in range(stages)])[: stages - 1]
    beside = ([2, 7, 11, 16, 19, 22, 26] + [29 + 3 * k for k in range(stages)])[:stages]
    polls = 2 * (last + 1)
    plan = [(at, s, 0, direct, False) for s, at in enumerate(when, 2)]
    plan += [(at, s, direct, SIDE_CHUNKS, True) for s, at in enumerate(beside, 1)]
    plan = sorted(plan, key=lambda entry: -entry[1])

    def poll(parity):
        @pl.when(2 * n + parity <= (direct + 1) // 2)
        def _():
            for u in range(2):
                t = 2 * (2 * n + parity - 1) + u

                @pl.when((t >= 0) & (t < direct))
                def _(t=t):
                    run(1, t)

        for at, s, first, size, side in plan:
            if at % 2 == parity and size:
                t = n - at // 2

                @pl.when((t >= 0) & (t < size))
                def _(s=s, t=t, first=first, side=side):
                    run(s, first + t, side)

    def act_far():
        return remote(act.at[1 - y], act_full.at[y], ssem.at[8], rsem.at[8], across)

    def act_own():
        return pltpu.make_async_copy(act.at[y], act_full.at[y], lsem.at[0])

    greeted = (chip, across) + tuple(mate_of(k) for k in range(bits))

    @pl.when(n == 0)
    def _():
        term_copy(0).start()
        term_copy(1).start()
        hail(greeted)
        act_own().start()

    lane = iota((keys, 128), 1)

    @pl.when(h == 0)
    def _():
        vb[:, 0:128] = v_ref[...]
        vb[:, 128:256] = jnp.where(lane < 16, 1.0, 0.0).astype(bf16)
        kt[...] = k_ref[...].astype(f32).T.astype(bf16)
        qt[...] = q_ref[...].astype(f32).T.astype(bf16)
        parts, sums = [], []
        for k in range(4):
            span = slice(k * HDIM, (k + 1) * HDIM)
            part = do_ref[span].astype(f32) * linv_ref[k, 0:1, :]
            parts.append(part)
            sums.append(jnp.sum(part * o_ref[span], axis=0, keepdims=True))
        part = jnp.concatenate(parts, axis=0)
        dopb[...] = part.astype(bf16)
        dox[:, 0:128] = part.T.astype(bf16)
        inner = -jnp.concatenate(sums + [jnp.zeros((4, tokens), f32)], axis=0)
        high = inner.astype(bf16).astype(f32)
        ext = jnp.concatenate([high, inner - high, jnp.zeros((112, tokens), f32)], axis=0)
        dox[:, 128:256] = ext.T.astype(bf16)

    @pl.when(n == 0)
    def _():
        meet(greeted)
        for t in range(direct):
            run(0, t)
            if t < SIDE_CHUNKS:
                run(0, direct + t)
        term_copy(0).wait()
        term_copy(1).wait()

    @pl.when(n > 0)
    def _():
        poll(0)

    @pl.when(n == 9)
    def _():
        act_far().start()

    span = pl.ds(pl.multiple_of(h * HDIM, HDIM), HDIM)
    pieces = 2
    block = tokens // pieces
    wide = iota((block, 256), 1)
    ours = ((wide < 128) & (wide // HDIM == h)) | (wide == 128 + h) | (wide == 136 + h)
    for j in range(pieces):
        cols = slice(j * block, (j + 1) * block)
        part = dox[cols]
        part = jnp.where(ours, part, jnp.zeros_like(part))
        dp = lax.dot_general(part, vb[...], NT, preferred_element_type=f32)
        e = e_ref[0, cols]
        ds = (e.astype(f32) * dp).astype(bf16)
        dqt = lax.dot_general(kt[span], ds, NT, preferred_element_type=f32)
        dq_ref[:, cols] = (dqt * HDIM ** (-0.5)).astype(bf16)
        kk = jnp.dot(qt[span, cols], ds, preferred_element_type=f32)
        vv = jnp.dot(dopb[span, cols], e, preferred_element_type=f32)
        if j == 0:
            dkt[...] = kk
            dvt[...] = vv
            poll(1)
        else:
            dk[g, span] = ((dkt[...] + kk) * (1.0 / LOG2E)).astype(bf16)
            dv[g, span] = (dvt[...] + vv).astype(bf16)

    def exchange(k):
        theirs = pl.ds(pl.multiple_of((1 - c) * half_keys, 128), half_keys)
        return (
            remote(dk.at[k, :, theirs], dk_in.at[k], ssem.at[2 * k], rsem.at[2 * k], chip),
            remote(dv.at[k, :, theirs], dv_in.at[k], ssem.at[2 * k + 1], rsem.at[2 * k + 1], chip),
        )

    @pl.when(h == 3)
    def _():
        for copy in exchange(g):
            copy.start()

    @pl.when(n == last)
    def _():
        mine = pl.ds(pl.multiple_of(c * half_keys, 128), half_keys)
        for tick in range(polls, max(when[-1] + 2 * direct, beside[-1] + 2 * SIDE_CHUNKS)):
            for at, s, first, size, side in plan:
                late = tick - at
                if late >= 0 and late % 2 == 0 and late // 2 < size:
                    run(s, first + late // 2, side)
        give = pltpu.make_async_copy(total, total_out, lsem.at[1])
        give.start()
        for k in range(4):
            for copy in exchange(k):
                copy.wait()
            band = slice(k * 128, (k + 1) * 128)
            dk_out[band] = dk[k, :, mine] + dk_in[k]
            dv_out[band] = dv[k, :, mine] + dv_in[k]
        act_far().wait()
        act_own().wait()
        give.wait()


def attend_back(cubes, q, k, v, do, ot, linv, e, act, grads):
    tokens, model = q.shape
    keys = k.shape[0]
    width = grads.shape[2]
    chunk = chunk_rows(cubes)
    depth = grads.shape[1] - LATE_CHUNKS * chunk
    sds = jax.ShapeDtypeStruct

    def cols(size):
        return pl.BlockSpec((size, 128), lambda n: (0, n // 4))

    fixed = pl.BlockSpec((model, tokens), lambda n: (0, 0))
    return pl.pallas_call(
        functools.partial(backward_kernel, cubes, chunk),
        name="attend_back",
        grid=(HEADS,),
        in_specs=[
            cols(tokens), cols(keys), cols(keys),
            pl.BlockSpec((128, tokens), lambda n: (n // 4, 0)),
            pl.BlockSpec((128, tokens), lambda n: (n // 4, 0)),
            pl.BlockSpec((4, 8, tokens), lambda n: (n // 4, 0, 0)),
            pl.BlockSpec((1, tokens, keys), lambda n: (n, 0, 0)),
            ANY,
            ANY,
        ],
        out_specs=[pl.BlockSpec((HDIM, tokens), lambda n: (n, 0)), fixed, fixed, ANY, ANY],
        out_shape=[
            sds((model, tokens), bf16),
            sds((model, tokens), bf16),
            sds((model, tokens), bf16),
            sds(act.shape, bf16),
            sds((depth, width), bf16),
        ],
        scratch_shapes=[
            pltpu.VMEM((keys, 256), bf16),
            pltpu.VMEM((128, keys), bf16),
            pltpu.VMEM((128, tokens), bf16),
            pltpu.VMEM((tokens, 256), bf16),
            pltpu.VMEM((128, tokens), bf16),
            pltpu.VMEM((HDIM, keys), f32),
            pltpu.VMEM((HDIM, keys), f32),
            pltpu.VMEM((4, 128, keys), bf16),
            pltpu.VMEM((4, 128, keys), bf16),
            pltpu.VMEM((4, 128, tokens), bf16),
            pltpu.VMEM((4, 128, tokens), bf16),
            pltpu.SemaphoreType.DMA((4,)),
            pltpu.SemaphoreType.DMA((9,)),
            pltpu.SemaphoreType.DMA((9,)),
            pltpu.VMEM((depth, width), bf16),
            pltpu.VMEM((2, depth, width), bf16),
        ] + reducer_scratch(cubes, depth // chunk, depth, width),
        compiler_params=params(2),
    )(q, k, v, do, ot, linv, e, act, grads)


def project_back_kernel(
    cubes, chunk,
    dq_in, dk_in, dv_in, first_hbm, embedded_in, middle_in, qkvw_in, embw_in, enc_in, tgt, vecf, sums, early,
    total, vis_out,
    dq, dk, dv, first_in, embedded, grad_middle, qkvw, embw, enc, isem,
    grads, first_t, gft, vgrad, vis_in, lsem, vs, vr, got_core, got_y, work, *rest,
):
    gots, (rs, rr) = rest[:-2], rest[-2:]
    cube, b, y, c = place()
    chip, across, diag = peers()
    bits = cubes.bit_length() - 1
    tokens, model = first_in.shape
    half = tokens // 2
    slots = enc.shape[0]
    er = embw.shape[0] // 4
    qr = model // 4
    first = LATE_CHUNKS * chunk
    left = range(LATE_CHUNKS)
    count = grads.shape[1] // chunk
    middle = range(LATE_CHUNKS, LATE_CHUNKS + 3 * qr // chunk)
    final = range(LATE_CHUNKS + 3 * qr // chunk, count)

    def mine(d, span):
        return grads[d, span]

    run, stages = reducer(cubes, chunk, grads, mine, got_core, got_y, work, gots, total, rs, rr)

    def runs(s, chunks):
        for t in chunks:
            run(s, t, "joint" if chunks is not left else True)

    fetch = pltpu.make_async_copy(
        early.at[:, pl.ds(early.shape[1] - first, first)], grads.at[:, pl.ds(0, first)], lsem.at[1]
    ) if first else None
    if first:
        fetch.start()
    greeted = (chip, across, diag, corner()) + tuple(mate_of(k) for k in range(bits))
    hail(greeted)

    loads = []
    for k, (src, dst) in enumerate((
        (first_hbm, first_in), (dq_in, dq), (dk_in, dk), (dv_in, dv), (qkvw_in, qkvw), (embedded_in, embedded),
        (middle_in, grad_middle), (enc_in, enc), (embw_in, embw),
    )):
        loads.append(pltpu.make_async_copy(src, dst, isem.at[k]))
        loads[-1].start()
    loads[0].wait()
    first_t[...] = first_in[...].astype(f32).T.astype(bf16)
    if first:
        fetch.wait()
    meet(greeted)
    runs(0, left)
    for k, part in enumerate((dq, dk, dv)):
        loads[1 + k].wait()
        term = lax.dot_general(first_t[...], part[...], NT, preferred_element_type=f32).astype(bf16)
        for d in range(4):
            grads[d, first + k * qr : first + (k + 1) * qr] = term[d * qr : (d + 1) * qr]
        if k == 1:
            runs(1, left)
    runs(0, middle)
    ones = jnp.ones((8, tokens), bf16)
    qsum = lax.dot_general(ones, dq[...], NT, preferred_element_type=f32)[0:1]
    vsum = lax.dot_general(ones, dv[...], NT, preferred_element_type=f32)[0:1]
    (gain,) = unpack(vecf, ((2, 1, ALL),))
    column = tgt[...].astype(f32).T[:, 0:1].astype(jnp.int32)
    for copy in loads[4:]:
        copy.wait()
    gft[...] = (
        jnp.dot(qkvw[:, 0:model], dq[...], preferred_element_type=f32)
        + jnp.dot(qkvw[:, model : 2 * model], dk[...], preferred_element_type=f32)
        + jnp.dot(qkvw[:, 2 * model :], dv[...], preferred_element_type=f32)
    )
    runs(1, middle)
    gsum = [jnp.zeros((1, model), f32)] * 3
    lifted = None
    for h in range(2):
        span = pl.ds(h * half, half)
        gf = gft[:, span].T
        value = embedded[span]
        center = value - jnp.mean(value, axis=-1, keepdims=True)
        rstd = lax.rsqrt(jnp.mean(center * center, axis=-1, keepdims=True) + EPS)
        normed = center * rstd
        gsum[0] += jnp.sum(gf * normed, axis=0, keepdims=True)
        gsum[1] += jnp.sum(gf, axis=0, keepdims=True)
        gn = gf * gain
        back = rstd * (
            gn - jnp.mean(gn, axis=-1, keepdims=True) - normed * jnp.mean(gn * normed, axis=-1, keepdims=True)
        )
        ge = grad_middle[span] + back
        offset = y * half + h * 2 * half
        hit = (iota((half, slots), 0) + offset == tgt[0:1]).astype(f32)
        flag = jnp.sum(hit, axis=1, keepdims=True)
        gsum[2] += jnp.sum((1.0 - flag) * ge, axis=0, keepdims=True)
        hit_t = (iota((slots, half), 1) + offset == column).astype(bf16)
        term = jnp.dot(hit_t, ge.astype(bf16), preferred_element_type=f32)
        lifted = term if lifted is None else lifted + term
        runs(2 + h, left)
    bsum = jnp.sum(lifted, axis=0, keepdims=True)
    low = lifted.astype(bf16)
    at = first + 3 * qr
    gemb = jnp.dot(enc[...].astype(f32).T.astype(bf16), low, preferred_element_type=f32).astype(bf16)
    for d in range(4):
        grads[d, at : at + er] = gemb[d * er : (d + 1) * er]

    def lanes(value, d, size=128):
        return value[:, d * size : (d + 1) * size]

    down_s, out_s, gain_s, bias_s = (sums[k : k + 1] for k in range(4))
    pad = grads.shape[1] - at - er
    for d in range(4):
        part = qsum if d < 2 else vsum
        blank = jnp.zeros((1, model // 2), f32)
        packed = [
            jnp.concatenate([lanes(bsum, d), lanes(gsum[2], d), lanes(gsum[0], d), lanes(gsum[1], d)], axis=1),
            jnp.concatenate([lanes(part, d % 2, 256), lanes(out_s, d), lanes(gain_s, d)], axis=1),
            sums[4 + d : 5 + d],
            jnp.concatenate([lanes(bias_s, d), lanes(down_s, d), blank], axis=1),
        ]
        packed = jnp.concatenate(packed + [jnp.zeros((pad - 4, model), f32)], axis=0)
        grads[d, at + er :] = packed.astype(bf16)
    runs(0, final)
    runs(2, middle)
    runs(4, left)
    vgrad[...] = (
        lax.dot_general(low, embw[...], NT, preferred_element_type=f32).astype(bf16).reshape(vgrad.shape)
    )
    vis_copies = [
        remote(vgrad.at[2 * (1 - y) + c], vis_in.at[y, :, c], vs.at[0], vr.at[0], across),
        remote(vgrad.at[2 * (1 - y) + 1 - c], vis_in.at[y, :, c], vs.at[1], vr.at[1], diag),
        remote(vgrad.at[2 * y + 1 - c], vis_in.at[y, :, c], vs.at[2], vr.at[2], chip),
        pltpu.make_async_copy(vgrad.at[b], vis_in.at[y, :, c], lsem.at[0]),
    ]
    runs(1, final)
    for copy in vis_copies:
        copy.start()
    runs(3, middle)
    runs(5, left)
    for step in range(2, stages + 1):
        if 4 + step <= stages:
            runs(4 + step, left)
        if step + 2 < stages:
            runs(step + 2, middle)
        if step < stages:
            runs(step, final)
    for copy in vis_copies:
        copy.wait()
    vis_out[...] = vis_in[0] + vis_in[1]


def project_back(cubes, dq, dk, dv, first_in, embedded, grad_middle, qkvw, embw, enc, tgt, vecf, sums, early, cap):
    tokens, model = first_in.shape
    chunk = chunk_rows(cubes)
    depth = 3 * model // 4 + embw.shape[0] // 4 + 16
    depth = depth + -depth % chunk + LATE_CHUNKS * chunk
    enc_width = enc.shape[1]
    slots = enc.shape[0]
    sds = jax.ShapeDtypeStruct
    return pl.pallas_call(
        functools.partial(project_back_kernel, cubes, chunk),
        name="project_back",
        out_shape=(sds((depth, model), bf16), sds((2, 2, cap, enc_width), bf16)),
        in_specs=[ANY] * 9 + [VM] * 3 + [ANY],
        out_specs=(VM, VM),
        scratch_shapes=[pltpu.VMEM((model, tokens), bf16)] * 3 + [
            pltpu.VMEM((tokens, model), bf16),
            pltpu.VMEM((tokens, model), f32),
            pltpu.VMEM((tokens, model), f32),
            pltpu.VMEM(qkvw.shape, bf16),
            pltpu.VMEM(embw.shape, bf16),
            pltpu.VMEM(enc.shape, bf16),
            pltpu.SemaphoreType.DMA((9,)),
            pltpu.VMEM((4, depth, model), bf16),
            pltpu.VMEM((model, tokens), bf16),
            pltpu.VMEM((model, tokens), f32),
            pltpu.VMEM((4, 2, cap, enc_width), bf16),
            pltpu.VMEM((2, 2, 2, cap, enc_width), bf16),
            pltpu.SemaphoreType.DMA((2,)),
            pltpu.SemaphoreType.DMA((3,)),
            pltpu.SemaphoreType.DMA((3,)),
        ] + reducer_scratch(cubes, depth // chunk, depth, model),
        compiler_params=params(3),
    )(dq, dk, dv, first_in, embedded, grad_middle, qkvw, embw, enc, tgt, vecf, sums, early)


def finish_kernel(late, first, second, down, up, out, qkv, emb, *vectors):
    model = down.shape[1]
    parts = up.shape[1] // model
    size = up.shape[0]
    start = first.shape[0]

    def early(at, count):
        if at + count <= start:
            return first[at : at + count].astype(f32)
        if at >= start:
            return second[at - start : at - start + count].astype(f32)
        return jnp.concatenate(
            [first[at:start].astype(f32), second[0 : at + count - start].astype(f32)], axis=0
        )

    down[...] = early(0, model).T
    for k in range(parts):
        up[:, k * model : (k + 1) * model] = early(model + k * size, size)
    out[...] = early(model + parts * size, size)
    for k in range(3):
        qkv[:, k * model : (k + 1) * model] = second[late + k * size : late + (k + 1) * size].astype(f32)
    at = late + 3 * size
    er = emb.shape[0]
    emb[...] = second[at : at + er].astype(f32)
    packed = second[at + er : at + er + 16].astype(f32)
    pieces = iter(vectors)
    for row, widths in enumerate(((128, 128, 128, 128), (256, 128, 128), (512,), (128, 128))):
        lane = 0
        for width in widths:
            next(pieces)[...] = packed[row : row + 1, lane : lane + width]
            lane += width


def finish(late, first, second, shapes):
    sds = jax.ShapeDtypeStruct
    widths = (128, 128, 128, 128, 256, 128, 128, 512, 128, 128)
    return pl.pallas_call(
        functools.partial(finish_kernel, late),
        name="results",
        out_shape=tuple(sds(s, f32) for s in shapes) + tuple(sds((1, w), f32) for w in widths),
        in_specs=[VM, VM],
        out_specs=tuple([VM] * (len(shapes) + len(widths))),
        compiler_params=params(),
    )(first, second)


def shards(
    cubes,
    visible, kept_rows, slot_counts, patches, positions, embedder, embedbias, masktoken, attngain, attnbias,
    qkvproj, qvbias, outproj, outbias, mlpgain, mlpbias, upproj, upbias, downproj, downbias, cotangent,
):
    cap, enc_width = visible.shape[2:]
    vis = visible.reshape(2, 2, cap, enc_width)
    vecs = [
        m.reshape(-1, 128)
        for m in (embedbias, masktoken, attngain, attnbias, qvbias, outbias, mlpgain, mlpbias, upbias, downbias)
    ]
    embedded, first_in, q, k, v, emb_full, qkv_full, enc, target, vecf = embed(
        vis, kept_rows[0], slot_counts, embedder, qkvproj, positions, vecs
    )
    own = (outproj, upproj, downproj, cotangent)
    e, ot, linv, mixed, *gathered = attend(patches, q, k, v, *own)
    act, grads, grad_middle, grad_mixed, sums = mlp(cubes, patches, vecf, mixed, ot, embedded, gathered, own)
    dq, dk, dv, activations, first = attend_back(cubes, q, k, v, grad_mixed, ot, linv, e, act, grads)
    second, visible_grad = project_back(
        cubes, dq, dk, dv, first_in, embedded, grad_middle, qkv_full, emb_full, enc.reshape(-1, enc_width), target, vecf, sums, grads, cap
    )
    shapes = (downproj.shape, upproj.shape, outproj.shape, qkvproj.shape, embedder.shape)
    down_o, up_o, out_o, qkv_o, emb_o, *small = finish(LATE_CHUNKS * chunk_rows(cubes), first, second, shapes)
    ebias, mask, again, abias, qv, outb, mgain, upb, mbias, downb = (m.reshape(-1) for m in small)
    return (
        activations, visible_grad.reshape(visible.shape), emb_o, ebias, mask, again, abias, qkv_o, qv,
        out_o, outb, mgain, mbias, up_o, upb, down_o, downb,
    )


def solution(mesh):
    cubes = mesh.shape["cube"]
    split = P(("cube", "band"), None, None, None)
    mat, row = P("band", None), P("band")
    placed = (
        split, P(("cube", "band"), None, None), P(("cube", "band"), None), P("cube"), mat,
        mat, row, row, row, row, mat, row, mat, row, row, row, mat, row, mat, row, P("cube", "band", None),
    )
    return jax.shard_map(
        functools.partial(shards, cubes),
        mesh=mesh,
        in_specs=placed,
        out_specs=(
            P("cube", "band", None), split, mat, row, row, row, row, mat, row, mat, row, row, row, mat, row, mat, row,
        ),
        check_vma=False,
    )
```

```python
import functools

import jax
import jax.numpy as jnp
from jax import lax
from jax.experimental import pallas as pl
from jax.experimental.pallas import tpu as pltpu
from jax.sharding import PartitionSpec as P

HEADS = 16
LATE_CHUNKS = 0
SIDE_CHUNKS = 2
HDIM = 32
EPS = 1e-06
LOG2E = 1.4426950408889634
QSCALE = HDIM ** (-0.5) * LOG2E
MESH = pl.DeviceIdType.MESH
NT = (((1,), (1,)), ((), ()))
f32 = jnp.float32
bf16 = jnp.bfloat16
ANY = pl.BlockSpec(memory_space=pl.ANY)
VM = pl.BlockSpec(memory_space=pltpu.VMEM)
VMEM_LIMIT = 60 * 2**20


def iota(shape, dim):
    return lax.broadcasted_iota(jnp.int32, shape, dim)


def normalize(values):
    center = values - jnp.mean(values, axis=-1, keepdims=True)
    spread = jnp.mean(center * center, axis=-1, keepdims=True)
    return center * lax.rsqrt(spread + EPS)


def place():
    cube, band = lax.axis_index("cube"), lax.axis_index("band")
    y, c = band // 2, band % 2
    return cube, band, y, c


def peers():
    cube, band, y, c = place()
    same_chip = (cube, 2 * y + 1 - c)
    across = (cube, 2 * (1 - y) + c)
    diagonal = (cube, 2 * (1 - y) + 1 - c)
    return same_chip, across, diagonal


def hail(devices):
    barrier = pltpu.get_barrier_semaphore()
    for device in devices:
        pl.semaphore_signal(barrier, inc=1, device_id=device, device_id_type=MESH)


def meet(devices):
    pl.semaphore_wait(pltpu.get_barrier_semaphore(), len(devices))


def remote(src, dst, send, recv, device):
    return pltpu.make_async_remote_copy(
        src_ref=src, dst_ref=dst, send_sem=send, recv_sem=recv, device_id=device, device_id_type=MESH
    )


def rows(start, size):
    return pl.ds(pl.multiple_of(start, 16), size)


def params(collective_id=None):
    if collective_id is None:
        return pltpu.CompilerParams(vmem_limit_bytes=VMEM_LIMIT)
    return pltpu.CompilerParams(collective_id=collective_id, has_side_effects=True, vmem_limit_bytes=VMEM_LIMIT)


def mate_of(k):
    cube, b, _, _ = place()
    d = 1 << k
    return (cube + d - 2 * d * ((cube // d) % 2), b)


def corner():
    _, _, y, c = place()
    return (mate_of(0)[0], 2 * (1 - y) + c)


def unpack(vecf, spans):
    vectors = vecf[...].astype(f32)
    out = []
    for first, count, bands in spans:
        out.append(
            jnp.concatenate([vectors[d, k : k + 1] for d in bands for k in range(first, first + count)], axis=1)
        )
    return out


ALL = (0, 1, 2, 3)


def embed_kernel(
    vis, kept_rows, counts, emb, qkv, pos, *refs,
):
    vecs = refs[:10]
    (embedded, first_in, q_out, k_out, v_out, emb_out, qkv_out, enc_out, tgt_out, vecf,
     enc, tgt, embf, qkvf, posf, vec, kbuf, vbuf, qbuf, ebuf, fbuf, kept, lsem, ssem, rsem) = refs[10:]
    cube, b, y, c = place()
    x = cube % 2
    chip, across, diag = peers()
    mate = mate_of(0)
    bq = 2 * (1 - y) + c
    er, qr = emb.shape[0], qkv.shape[0]
    half = pos.shape[0]
    model = emb.shape[1]
    hail((chip, across, diag, mate))
    fill = jnp.zeros((vec.shape[0] - sum(v.shape[0] for v in vecs), 128), f32)
    vec[...] = jnp.concatenate([v[...].astype(f32) for v in vecs] + [fill], axis=0).astype(bf16)
    cap = vis.shape[2]
    names = kept_rows[...].astype(f32)
    high = jnp.floor(names * (1.0 / 32.0))
    wide = tgt.shape[2]
    spread = (iota((cap, wide), 1) % cap == iota((cap, wide), 0)).astype(bf16)
    names = 32.0 * jnp.dot(high.astype(bf16), spread, preferred_element_type=f32) + jnp.dot(
        (names - 32.0 * high).astype(bf16), spread, preferred_element_type=f32
    )
    lane = iota((1, wide), 1)
    upper = (lane // cap) % 2 == 1
    for d in range(2):
        row = jnp.where(upper, names[2 + d : 3 + d] + 4.0 * pos.shape[0] / 2.0, names[d : d + 1])
        bound = jnp.where(upper, counts[0, 2 + d], counts[0, d])
        live = (lane % cap < bound) & (lane // (2 * cap) == b)
        row = jnp.where(live, row, -1.0).astype(jnp.int32)
        kept[d] = jnp.broadcast_to(row, kept.shape[1:])
    meet((chip, across, diag, mate))

    used = [0]
    local = []

    def send(src, dst, device):
        copy = remote(src, dst, ssem.at[used[0]], rsem.at[used[0]], device)
        used[0] += 1
        copy.start()
        return copy

    def keep(src, dst):
        copy = pltpu.make_async_copy(src, dst, lsem.at[len(local)])
        copy.start()
        local.append(copy)

    def cut(start, size, which):
        return rows(start + which * (size // 2), size // 2)

    def quarter(band, which, k):
        return rows(band * qr + which * (qr // 2) + k * (qr // 4), qr // 4)

    def strip(k):
        return rows(x * (half // 2) + k * (half // 4), half // 4)

    ea, qa = rows(b * er, er), rows(b * qr, qr)
    far_vec = send(vec, vecf.at[b], across)
    far_emb = send(emb.at[cut(0, er, x)], embf.at[cut(b * er, er, x)], across)
    small = [
        send(kept.at[c], tgt.at[b], across),
        send(vis.at[:, c], enc.at[b], across),
        send(kept.at[1 - c], tgt.at[b], diag),
        send(vis.at[:, 1 - c], enc.at[b], diag),
        send(kept.at[1 - c], tgt.at[b], chip),
        send(vec, vecf.at[b], chip),
        send(vis.at[:, 1 - c], enc.at[b], chip),
        send(emb, embf.at[ea], chip),
    ]
    far_pos = [send(pos.at[strip(k)], posf.at[y, strip(k)], across) for k in range(2)]
    far_qkv = [send(qkv.at[quarter(0, x, k)], qkvf.at[quarter(b, x, k)], across) for k in range(2)]
    near_qkv = send(qkv, qkvf.at[qa], chip)
    keep(kept.at[c], tgt.at[b])
    keep(vec, vecf.at[b])
    keep(vis.at[:, c], enc.at[b])
    keep(emb, embf.at[ea])
    keep(pos, posf.at[y])
    keep(qkv, qkvf.at[qa])

    far_vec.wait()
    relays = [send(vecf.at[bq], vecf.at[bq], chip)]
    far_emb.wait()
    got = cut(bq * er, er, x)
    side_emb = send(embf.at[got], embf.at[got], mate)
    relays.append(send(embf.at[got], embf.at[got], chip))
    side_emb.wait()
    got = cut(bq * er, er, 1 - x)
    relays.append(send(embf.at[got], embf.at[got], chip))
    side_pos = []
    for k in range(2):
        far_pos[k].wait()
        got = posf.at[1 - y, strip(k)]
        side_pos.append(send(got, got, mate))
    for copy in small + local + relays:
        copy.wait()

    target = jnp.max(tgt[...].astype(f32), axis=0)[0:1].astype(jnp.int32)
    tgt_out[...] = jnp.broadcast_to(target, tgt_out.shape)
    slots = 8 * cap
    enc_all = enc[...].reshape(slots, enc.shape[3])
    results = []

    def give(src, dst):
        copy = pltpu.make_async_copy(src, dst, lsem.at[8 + len(results)])
        copy.start()
        results.append(copy)

    give(enc, enc_out)
    give(embf, emb_out)
    embedbias, mask, gain, bias, qbias, vbias = unpack(
        vecf, ((0, 1, ALL), (1, 1, ALL), (2, 1, ALL), (3, 1, ALL), (4, 2, (0, 1)), (4, 2, (2, 3)))
    )

    def lift(h):
        span = rows(h * half, half)
        cells = iota((half, slots), 0) + (y * half + h * 2 * half)
        hit = (cells == target).astype(f32)
        flag = jnp.sum(hit, axis=1, keepdims=True)
        picked = jnp.dot(hit.astype(bf16), enc_all, preferred_element_type=f32).astype(bf16)
        rows_in = jnp.dot(picked, embf[...], preferred_element_type=f32)
        v = rows_in + flag * embedbias + (1.0 - flag) * mask + posf[h].astype(f32)
        ebuf[span] = v
        fbuf[span] = (normalize(v) * gain + bias).astype(bf16)
        give(ebuf.at[span], embedded.at[span])
        give(fbuf.at[span], first_in.at[span])

    lift(y)
    side_qkv, late = [], []
    for k in range(2):
        far_qkv[k].wait()
        got = quarter(bq, x, k)
        side_qkv.append(send(qkvf.at[got], qkvf.at[got], mate))
        late.append(send(qkvf.at[got], qkvf.at[got], chip))
    for copy in side_pos:
        copy.wait()
    lift(1 - y)
    for k in range(2):
        side_qkv[k].wait()
        got = quarter(bq, 1 - x, k)
        late.append(send(qkvf.at[got], qkvf.at[got], chip))
    near_qkv.wait()
    for copy in late:
        copy.wait()
    give(qkvf, qkv_out)
    mine = rows(c * 2 * half, 2 * half)
    first = fbuf[...]
    k = jnp.dot(first, qkvf[:, model : 2 * model], preferred_element_type=f32)
    kbuf[...] = k.astype(bf16)
    out = [send(kbuf, k_out.at[mine], chip)]
    give(kbuf, k_out.at[mine])
    v = jnp.dot(first, qkvf[:, 2 * model :], preferred_element_type=f32)
    vbuf[...] = (v + vbias).astype(bf16)
    out.append(send(vbuf, v_out.at[mine], chip))
    give(vbuf, v_out.at[mine])
    q = jnp.dot(first, qkvf[:, :model], preferred_element_type=f32)
    qbuf[...] = ((q + qbias) * QSCALE).astype(bf16)
    give(qbuf, q_out)
    for copy in out + results:
        copy.wait()


def embed(vis, kept_rows, counts, emb, qkv, pos, vecs):
    er, model = emb.shape
    qr, wide = qkv.shape
    half = pos.shape[0]
    enc_width = vis.shape[-1]
    cap = vis.shape[2]
    slots = 8 * cap
    tokens = 2 * half
    sds = jax.ShapeDtypeStruct
    return pl.pallas_call(
        embed_kernel,
        name="embed_project",
        out_shape=(
            sds((tokens, model), f32),
            sds((tokens, model), bf16),
            sds((tokens, model), bf16),
            sds((2 * tokens, model), bf16),
            sds((2 * tokens, model), bf16),
            sds((4 * er, model), bf16),
            sds((4 * qr, wide), bf16),
            sds((4, 2, cap, enc_width), bf16),
            sds((8, slots), jnp.int32),
            sds((4, 16, 128), bf16),
        ),
        in_specs=[ANY, VM, pl.BlockSpec(memory_space=pltpu.SMEM), ANY, ANY, ANY] + [VM] * 10,
        out_specs=(ANY,) * 8 + (VM, VM),
        scratch_shapes=[
            pltpu.VMEM((4, 2, cap, enc_width), bf16),
            pltpu.VMEM((4, 8, slots), jnp.int32),
            pltpu.VMEM((4 * er, model), bf16),
            pltpu.VMEM((4 * qr, wide), bf16),
            pltpu.VMEM((2, half, model), bf16),
            pltpu.VMEM((16, 128), bf16),
            pltpu.VMEM((tokens, model), bf16),
            pltpu.VMEM((tokens, model), bf16),
            pltpu.VMEM((tokens, model), bf16),
            pltpu.VMEM((tokens, model), f32),
            pltpu.VMEM((tokens, model), bf16),
            pltpu.VMEM((2, 8, slots), jnp.int32),
            pltpu.SemaphoreType.DMA((20,)),
            pltpu.SemaphoreType.DMA((32,)),
            pltpu.SemaphoreType.DMA((32,)),
        ],
        compiler_params=params(0),
    )(vis, kept_rows, counts, emb, qkv, pos, *vecs)


def forward_kernel(
    patch, q_ref, k_ref, v_ref, outw, upw, downw, cot,
    e_ref, o_ref, linv_ref, mix_ref, out_full, up_full, down_full, cot_full,
    kx, vt, sa, sb, ots, ssem, rsem,
):
    p = pl.program_id(0)
    last = pl.num_programs(0) - 1
    cube, b, y, c = place()
    x = cube % 2
    chip, across, _ = peers()
    mate = mate_of(0)
    bq = 2 * (1 - y) + c
    shards = ((upw, up_full), (outw, out_full), (downw, down_full))

    def cut(k, band, which):
        size = shards[k][0].shape[0]
        return rows(band * size + which * (size // 2), size // 2)

    def far(k):
        size = shards[k][0].shape[0]
        part = rows(x * (size // 2), size // 2)
        return remote(shards[k][0].at[part], shards[k][1].at[cut(k, b, x)], ssem.at[k], rsem.at[k], across)

    def near(k):
        size = shards[k][0].shape[0]
        return remote(shards[k][0], shards[k][1].at[rows(b * size, size)], ssem.at[3 + k], rsem.at[3 + k], chip)

    def side(k):
        ref = shards[k][1].at[cut(k, bq, x)]
        return remote(ref, ref, ssem.at[6 + k], rsem.at[6 + k], mate)

    def relay(k, which):
        ref = shards[k][1].at[cut(k, bq, x if which == 0 else 1 - x)]
        at = 9 + 2 * k + which
        return remote(ref, ref, ssem.at[at], rsem.at[at], chip)

    def cot_far():
        return remote(cot.at[1 - y], cot_full, ssem.at[15], rsem.at[15], across)

    @pl.when(p == 0)
    def _():
        hail((chip, across, mate))

    keys = k_ref.shape[0]
    tokens = q_ref.shape[0]
    lane = iota((keys, 128), 1)
    pieces = 3
    block = tokens // pieces

    @pl.when(p == 0)
    def _():
        row = iota((keys, 128), 0)
        bias = jnp.where((row % cot.shape[1] >= patch[y]) & (lane == 0), -1e30, 0.0).astype(bf16)
        for g in range(v_ref.shape[1] // 128):
            cols = slice(g * 128, (g + 1) * 128)
            kx[g, :, 0:128] = k_ref[:, cols]
            kx[g, :, 128:256] = bias
            vt[cols] = v_ref[:, cols].astype(f32).T.astype(bf16)

    def lanes(h):
        return pl.ds(pl.multiple_of((h // 4) * 128, 128), 128)

    narrow = iota((block, 128), 1) // HDIM

    def score(h, s, j):
        span = slice(j * block, (j + 1) * block)
        q = q_ref[span, lanes(h)]
        q = jnp.where(narrow == h % 4, q, jnp.zeros_like(q))
        qx = jnp.concatenate([q, jnp.ones((block, 128), bf16)], axis=1)
        s[span] = lax.dot_general(qx, kx[h // 4], NT, preferred_element_type=f32)

    ones = jnp.ones((16, keys), bf16)

    def soften(at, h, s, j):
        span = slice(j * block, (j + 1) * block)
        v = s[span]
        e = jnp.exp2(v - jnp.max(v, axis=1, keepdims=True)).astype(bf16)
        e_ref[at, span] = e
        lhs = jnp.concatenate([vt[pl.ds(pl.multiple_of(h * HDIM, HDIM), HDIM)], ones], axis=0)
        ot = lax.dot_general(lhs, e, NT, preferred_element_type=f32)
        li = 1.0 / ot[HDIM : HDIM + 8]
        o = ot[:HDIM] * li[0:1]
        o_ref[at * HDIM : (at + 1) * HDIM, span] = o
        ots[pl.ds(pl.multiple_of((p % 2) * 2 * HDIM + at * HDIM, HDIM), HDIM), span] = o
        linv_ref[at, :, span] = li

    @pl.when(p == 0)
    def _():
        for j in range(pieces):
            score(0, sa, j)
        meet((chip, across, mate))
        far(0).start()
        far(1).start()
        far(2).start()
        cot_far().start()
        for k in range(3):
            near(k).start()

    for k, at in ((0, 2), (1, 3), (2, 4)):

        @pl.when(p == at)
        def _(k=k):
            far(k).wait()
            side(k).start()
            relay(k, 0).start()

    for k, at in ((0, 5), (1, 6), (2, 7)):

        @pl.when(p == at)
        def _(k=k):
            side(k).wait()
            relay(k, 1).start()

    after = jnp.minimum(2 * p + 2, 2 * last + 1)
    for j in range(pieces):
        score(2 * p + 1, sb, j)
        soften(0, 2 * p, sa, j)
    for j in range(pieces):
        score(after, sa, j)
        soften(1, 2 * p + 1, sb, j)

    @pl.when(p % 2 == 1)
    def _():
        mix_ref[...] = ots[...].T.astype(bf16)

    @pl.when(p == last)
    def _():
        cot_far().wait()
        for k in range(3):
            near(k).wait()
            relay(k, 0).wait()
            relay(k, 1).wait()


def attend(patch, q, k, v, outw, upw, downw, cot):
    tokens, model = q.shape
    keys = k.shape[0]
    sds = jax.ShapeDtypeStruct

    def fixed(shape):
        return pl.BlockSpec(shape, lambda p: (0, 0))

    return pl.pallas_call(
        forward_kernel,
        name="attend",
        grid=(HEADS // 2,),
        in_specs=[
            pl.BlockSpec(memory_space=pltpu.SMEM),
            fixed(q.shape),
            fixed(k.shape),
            fixed(v.shape),
            ANY, ANY, ANY, ANY,
        ],
        out_specs=[
            pl.BlockSpec((2, tokens, keys), lambda p: (p, 0, 0)),
            pl.BlockSpec((2 * HDIM, tokens), lambda p: (p, 0)),
            pl.BlockSpec((2, 8, tokens), lambda p: (p, 0, 0)),
            pl.BlockSpec((tokens, 128), lambda p: (0, p // 2)),
            ANY, ANY, ANY, ANY,
        ],
        out_shape=[
            sds((HEADS, tokens, keys), bf16),
            sds((model, tokens), f32),
            sds((HEADS, 8, tokens), f32),
            sds((tokens, model), bf16),
            sds((4 * outw.shape[0], outw.shape[1]), bf16),
            sds((4 * upw.shape[0], upw.shape[1]), bf16),
            sds((4 * downw.shape[0], downw.shape[1]), bf16),
            sds(cot.shape[1:], bf16),
        ],
        scratch_shapes=[
            pltpu.VMEM((model // 128, keys, 256), bf16),
            pltpu.VMEM((model, keys), bf16),
            pltpu.VMEM((tokens, keys), f32),
            pltpu.VMEM((tokens, keys), f32),
            pltpu.VMEM((128, tokens), f32),
            pltpu.SemaphoreType.DMA((16,)),
            pltpu.SemaphoreType.DMA((16,)),
        ],
        compiler_params=params(1),
    )(patch, q, k, v, outw, upw, downw, cot)


def mlp_kernel(
    patch, vecf, mixed, mixed_t_in, embedded_in, out_got, up_got, down_got, cot_got, out_own, up_own, down_own, cot_own,
    act_out, grads_out, middle_out, mixed_out, sums,
    act, grads, grad_middle, grad_mixed, mixed_f, embedded_f, outw, upf, downf, cot, second_t, gout_t, second, active, hid, branch_b, wsem,
):
    _, b, y, _ = place()
    tokens, model = mixed.shape
    half = tokens // 2
    wide = upf.shape[1]
    parts = wide // model
    loads = []

    def load(src, dst):
        copy = pltpu.make_async_copy(src, dst, wsem.at[len(loads)])
        copy.start()
        loads.append(copy)

    mixed_t, embedded = mixed_f, embedded_f
    results = []

    def give(src, dst):
        copy = pltpu.make_async_copy(src, dst, wsem.at[16 + len(results)])
        copy.start()
        results.append(copy)

    for own, got, full in ((out_own, out_got, outw), (up_own, up_got, upf), (down_own, down_got, downf)):
        size = own.shape[0]
        load(own, full.at[rows(b * size, size)])
        for k in range(1, 4):
            part = rows((b + k) % 4 * size, size)
            load(got.at[part], full.at[part])
        if own is out_own:
            load(embedded_in, embedded_f)
    load(cot_own.at[y], cot.at[y])
    load(cot_got, cot.at[1 - y])
    load(mixed_t_in, mixed_f)
    vectors = vecf[...].astype(f32)

    def whole(k):
        return jnp.concatenate([vectors[d, k : k + 1] for d in range(4)], axis=1)

    outbias, gain, bias, downbias = whole(6), whole(7), whole(8), whole(13)
    upbias = [jnp.concatenate([vectors[d, 9 + k : 10 + k] for k in range(4)], axis=1) for d in range(parts)]
    live = iota((half, 1), 0) < patch[y]
    valid = jnp.where(live, 1.0, 0.0)
    total = [jnp.zeros((1, model), f32)] * (4 + parts)
    for copy in loads[:5]:
        copy.wait()
    for h in range(2):
        span = pl.ds(h * half, half)
        mix = mixed[span]
        middle = embedded[span] + (jnp.dot(mix, outw[...], preferred_element_type=f32) + outbias)
        center = middle - jnp.mean(middle, axis=-1, keepdims=True)
        rstd = lax.rsqrt(jnp.mean(center * center, axis=-1, keepdims=True) + EPS)
        normed = center * rstd
        sec = normed * gain + bias
        second_t[:, span] = sec.T.astype(bf16)
        sec = sec.astype(bf16)
        if h == 0:
            for copy in loads[5:-1]:
                copy.wait()
        gout = cot[h].astype(f32) * valid
        gout_t[:, span] = gout.T.astype(bf16)
        gout_b = gout.astype(bf16)
        total[0] += jnp.sum(gout, axis=0, keepdims=True)
        result = middle + downbias
        gsec = None
        for k in range(parts):
            cols = slice(k * model, (k + 1) * model)
            hidden = jnp.dot(sec, upf[:, cols], preferred_element_type=f32) + upbias[k]
            cdf = 0.5 + 0.5 * lax.erf(hidden * 0.7071067811865476)
            low = (hidden * cdf).astype(bf16)
            active[span, cols] = low
            slope = cdf + hidden * (0.3989422804014327 * jnp.exp(-0.5 * hidden * hidden))
            result += jnp.dot(low, downf[cols], preferred_element_type=f32)
            gact = lax.dot_general(gout_b, downf[cols], NT, preferred_element_type=f32)
            ghid = (gact * slope).astype(bf16)
            hid[span, cols] = ghid
            total[4 + k] += jnp.sum(ghid.astype(f32), axis=0, keepdims=True)
            term = lax.dot_general(ghid, upf[:, cols], NT, preferred_element_type=f32)
            gsec = term if gsec is None else gsec + term
        act[h] = (valid * result).astype(bf16)
        total[2] += jnp.sum(gsec * normed, axis=0, keepdims=True)
        total[3] += jnp.sum(gsec, axis=0, keepdims=True)
        gn = gsec * gain
        back = rstd * (
            gn - jnp.mean(gn, axis=-1, keepdims=True) - normed * jnp.mean(gn * normed, axis=-1, keepdims=True)
        )
        gmid = gout + back
        grad_middle[span] = gmid
        gb = gmid.astype(bf16)
        branch_b[span] = gb
        total[1] += jnp.sum(gb.astype(f32), axis=0, keepdims=True)
        grad_mixed[:, span] = lax.dot_general(outw[...], gb, NT, preferred_element_type=f32).astype(bf16)
        give(act.at[h], act_out.at[h])
        give(grad_middle.at[span], middle_out.at[span])
    give(grad_mixed, mixed_out)
    for k in range(parts):
        cols = slice(k * model, (k + 1) * model)
        grads[k, 0:model] = jnp.dot(gout_t[...], active[:, cols], preferred_element_type=f32).astype(bf16)
        gup = jnp.dot(second_t[...], hid[:, cols], preferred_element_type=f32).astype(bf16)
        size = model // 4
        for d in range(4):
            grads[d, model + k * size : model + (k + 1) * size] = gup[d * size : (d + 1) * size]
        give(grads.at[k, pl.ds(0, model)], grads_out.at[k, pl.ds(0, model)])
        part = pl.ds(model + k * size, size)
        give(grads.at[:, part], grads_out.at[:, part])
    base = model + parts * (model // 4)
    loads[-1].wait()
    gout_w = jnp.dot(mixed_t[...].astype(bf16), branch_b[...], preferred_element_type=f32).astype(bf16)
    for d in range(4):
        grads[d, base : base + model // 4] = gout_w[d * (model // 4) : (d + 1) * (model // 4)]
    spare = grads.shape[1] - base - model // 4
    if spare:
        grads[:, base + model // 4 :] = jnp.zeros((4, spare, model), bf16)
    part = pl.ds(base, grads.shape[1] - base)
    give(grads.at[:, part], grads_out.at[:, part])
    sums[...] = jnp.concatenate(total, axis=0)
    for copy in results:
        copy.wait()


def mlp(cubes, patch, vecf, mixed, mixed_t, embedded, gathered, own):
    tokens, model = mixed.shape
    outw, upw, downw, cot = own
    wide = upw.shape[1]
    half = cot.shape[1]
    depth = model + wide // 4 + model // 4
    depth += -depth % chunk_rows(cubes)
    sds = jax.ShapeDtypeStruct
    return pl.pallas_call(
        mlp_kernel,
        name="mlp_both",
        out_shape=(
            sds((2, half, model), bf16),
            sds((4, depth, model), bf16),
            sds((tokens, model), f32),
            sds((model, tokens), bf16),
            sds((4 + wide // model, model), f32),
        ),
        in_specs=[pl.BlockSpec(memory_space=pltpu.SMEM), VM, VM] + [ANY] * 10,
        out_specs=(ANY, ANY, ANY, ANY, VM),
        scratch_shapes=[
            pltpu.VMEM((2, half, model), bf16),
            pltpu.VMEM((4, depth, model), bf16),
            pltpu.VMEM((tokens, model), f32),
            pltpu.VMEM((model, tokens), bf16),
            pltpu.VMEM((model, tokens), f32),
            pltpu.VMEM((tokens, model), f32),
            pltpu.VMEM((model, model), bf16),
            pltpu.VMEM((model, wide), bf16),
            pltpu.VMEM((wide, model), bf16),
            pltpu.VMEM((2, half, model), bf16),
            pltpu.VMEM((model, tokens), bf16),
            pltpu.VMEM((model, tokens), bf16),
            pltpu.VMEM((tokens, model), bf16),
            pltpu.VMEM((tokens, wide), bf16),
            pltpu.VMEM((tokens, wide), bf16),
            pltpu.VMEM((tokens, model), bf16),
            pltpu.SemaphoreType.DMA((32,)),
        ],
        compiler_params=params(),
    )(patch, vecf, mixed, mixed_t, embedded, *gathered, *own)


def chunk_rows(cubes):
    return max(128, 8 * cubes)


def reducer(cubes, chunk, grads, mine, got_core, got_y, work, gots, total, ssem, rsem):
    cube, b, y, c = place()
    chip, across, _ = peers()
    bits = cubes.bit_length() - 1
    own, other = 2 * y + c, 2 * (1 - y) + c
    top = bits + 1

    def kept(k):
        start = 0
        for j in range(k):
            start = start + ((cube // (1 << j)) % 2) * (chunk >> (j + 1))
        return start

    def back(s, t):
        k = 2 * bits - s
        span = rows(t * chunk + kept(k + 1), chunk >> (k + 1))
        return total.at[span], total.at[span], mate_of(k)

    def core(t):
        span = rows(t * chunk, chunk)
        return [
            remote(grads.at[1 - c, span], got_core.at[0, span], ssem.at[t, 0], rsem.at[t, 0], chip),
            remote(grads.at[3 - c, span], got_core.at[1, span], ssem.at[t, 1], rsem.at[t, 1], chip),
        ]

    def step(k, t, both):
        side = pl.ds(0, 2) if both else pl.ds(0, 1)
        if k < bits - 1:
            size = chunk >> (k + 1)
            bit = (cube // (1 << k)) % 2
            away = rows(t * chunk + kept(k) + (1 - bit) * size, size)
        else:
            size = chunk >> k
            away = rows(t * chunk + kept(k), size)
        return work.at[side, away], gots[k].at[side, rows(t * size, size)], mate_of(k)

    def copies(s, t, side):
        if s == 0:
            return core(t)
        if side == "joint":
            first, second, part = halves(t)
            return [
                remote(work.at[1, first], got_y.at[first], ssem.at[t, 2], rsem.at[t, 2], across),
                remote(work.at[0, second], gots[0].at[0, part], ssem.at[t, 3], rsem.at[t, 3], mate_of(0)),
                remote(work.at[1, second], gots[0].at[1, part], ssem.at[t, more], rsem.at[t, more], corner()),
            ]
        if not side:
            if s == 1:
                span = rows(t * chunk, chunk)
                move = work.at[1, span], got_y.at[span], across
            elif s <= top:
                move = step(s - 2, t, False)
            else:
                move = back(s, t)
        elif s < top:
            move = step(s - 1, t, True)
        elif s == top:
            size = chunk >> (bits - 1)
            span = rows(t * chunk + kept(bits - 1), size)
            move = work.at[1, span], got_y.at[span], across
        else:
            move = back(s, t)
        return [remote(move[0], move[1], ssem.at[t, s + 1], rsem.at[t, s + 1], move[2])]

    more = 2 + 2 * bits

    def halves(t):
        size = chunk // 2
        x = cube % 2
        base = t * chunk
        return rows(base + x * size, size), rows(base + (1 - x) * size, size), rows(t * size, size)

    def run(s, t, side=False):
        if side == "joint" and s > 2:
            s, side = s + 1, False
        if side == "joint" and s == 2:
            for copy in copies(1, t, side):
                copy.wait()
            first, _, part = halves(t)
            work[0, first] = (work[0, first] + got_y[first]) + (gots[0][0, part] + gots[0][1, part])
            for copy in copies(3, t, False):
                copy.start()
            return
        if s > 0:
            for copy in copies(s - 1, t, side):
                copy.wait()
        span = rows(t * chunk, chunk)
        if s == 1:
            work[1, span] = mine(other, span) + got_core[1 - y, span]
            if side:
                work[0, span] = mine(own, span) + got_core[y, span]
        elif s == 2 and not side:
            work[0, span] = (mine(own, span) + got_core[y, span]) + got_y[span]
        elif 2 <= s <= top + 1:
            k = s - 2 if side else s - 3
            if side and s == top + 1:
                size = chunk >> (bits - 1)
                span = rows(t * chunk + kept(bits - 1), size)
                total[span] = work[0, span] + got_y[span]
            else:
                size = chunk >> min(k + 1, bits - 1)
                span = rows(t * chunk + kept(min(k + 1, bits - 1)), size)
                part = rows(t * size, size)
                if side:
                    work[:, span] = work[:, span] + gots[k][:, part]
                elif s <= top:
                    work[0, span] = work[0, span] + gots[k][0, part]
                else:
                    total[span] = work[0, span] + gots[k][0, part]
        if s < 1 + 2 * bits:
            for copy in copies(s, t, side):
                copy.start()

    return run, 1 + 2 * bits


def reducer_scratch(cubes, count, depth, width):
    bits = cubes.bit_length() - 1
    return [
        pltpu.VMEM((2, depth, width), bf16),
        pltpu.VMEM((depth, width), bf16),
        pltpu.VMEM((2, depth, width), bf16),
    ] + [pltpu.VMEM((2, depth >> min(k + 1, bits - 1), width), bf16) for k in range(bits)] + [
        pltpu.SemaphoreType.DMA((count, 3 + 2 * bits)),
        pltpu.SemaphoreType.DMA((count, 3 + 2 * bits)),
    ]


def backward_kernel(
    cubes, chunk,
    q_ref, k_ref, v_ref, do_ref, o_ref, linv_ref, e_ref, act, grads,
    dq_ref, dk_out, dv_out, act_full, total_out,
    vb, kt, qt, dox, dopb, dkt, dvt, dk, dv, dk_in, dv_in, lsem, ssem, rsem,
    total, terms, got_core, got_y, work, *rest,
):
    gots, (rs, rr) = rest[:-2], rest[-2:]
    n = pl.program_id(0)
    last = pl.num_programs(0) - 1
    h, g = n % 4, n // 4
    cube, b, y, c = place()
    chip, across, _ = peers()
    bits = cubes.bit_length() - 1
    keys = k_ref.shape[0]
    half_keys = keys // 2
    tokens = q_ref.shape[0]
    count = total.shape[0] // chunk

    def mine(d, span):
        return terms[d // 2, span]

    def term_copy(k):
        return pltpu.make_async_copy(grads.at[2 * k + c, pl.ds(0, count * chunk)], terms.at[k], lsem.at[2 + k])

    run, stages = reducer(cubes, chunk, grads, mine, got_core, got_y, work, gots, total, rs, rr)
    direct = count - SIDE_CHUNKS
    when = ([7, 11, 14, 18, 21, 25] + [28 + 3 * k for k in range(stages)])[: stages - 1]
    beside = ([2, 7, 11, 16, 19, 22, 26] + [29 + 3 * k for k in range(stages)])[:stages]
    polls = 2 * (last + 1)
    plan = [(at, s, 0, direct, False) for s, at in enumerate(when, 2)]
    plan += [(at, s, direct, SIDE_CHUNKS, True) for s, at in enumerate(beside, 1)]
    plan = sorted(plan, key=lambda entry: -entry[1])

    def poll(parity):
        @pl.when(2 * n + parity <= (direct + 1) // 2)
        def _():
            for u in range(2):
                t = 2 * (2 * n + parity - 1) + u

                @pl.when((t >= 0) & (t < direct))
                def _(t=t):
                    run(1, t)

        for at, s, first, size, side in plan:
            if at % 2 == parity and size:
                t = n - at // 2

                @pl.when((t >= 0) & (t < size))
                def _(s=s, t=t, first=first, side=side):
                    run(s, first + t, side)

    def act_far():
        return remote(act.at[1 - y], act_full.at[y], ssem.at[8], rsem.at[8], across)

    def act_own():
        return pltpu.make_async_copy(act.at[y], act_full.at[y], lsem.at[0])

    greeted = (chip, across) + tuple(mate_of(k) for k in range(bits))

    @pl.when(n == 0)
    def _():
        term_copy(0).start()
        term_copy(1).start()
        hail(greeted)
        act_own().start()

    lane = iota((keys, 128), 1)

    @pl.when(h == 0)
    def _():
        vb[:, 0:128] = v_ref[...]
        vb[:, 128:256] = jnp.where(lane < 16, 1.0, 0.0).astype(bf16)
        kt[...] = k_ref[...].astype(f32).T.astype(bf16)
        qt[...] = q_ref[...].astype(f32).T.astype(bf16)
        parts, sums = [], []
        for k in range(4):
            span = slice(k * HDIM, (k + 1) * HDIM)
            part = do_ref[span].astype(f32) * linv_ref[k, 0:1, :]
            parts.append(part)
            sums.append(jnp.sum(part * o_ref[span], axis=0, keepdims=True))
        part = jnp.concatenate(parts, axis=0)
        dopb[...] = part.astype(bf16)
        dox[:, 0:128] = part.T.astype(bf16)
        inner = -jnp.concatenate(sums + [jnp.zeros((4, tokens), f32)], axis=0)
        high = inner.astype(bf16).astype(f32)
        ext = jnp.concatenate([high, inner - high, jnp.zeros((112, tokens), f32)], axis=0)
        dox[:, 128:256] = ext.T.astype(bf16)

    @pl.when(n == 0)
    def _():
        meet(greeted)
        for t in range(direct):
            run(0, t)
            if t < SIDE_CHUNKS:
                run(0, direct + t)
        term_copy(0).wait()
        term_copy(1).wait()

    @pl.when(n > 0)
    def _():
        poll(0)

    @pl.when(n == 9)
    def _():
        act_far().start()

    span = pl.ds(pl.multiple_of(h * HDIM, HDIM), HDIM)
    pieces = 2
    block = tokens // pieces
    wide = iota((block, 256), 1)
    ours = ((wide < 128) & (wide // HDIM == h)) | (wide == 128 + h) | (wide == 136 + h)
    for j in range(pieces):
        cols = slice(j * block, (j + 1) * block)
        part = dox[cols]
        part = jnp.where(ours, part, jnp.zeros_like(part))
        dp = lax.dot_general(part, vb[...], NT, preferred_element_type=f32)
        e = e_ref[0, cols]
        ds = (e.astype(f32) * dp).astype(bf16)
        dqt = lax.dot_general(kt[span], ds, NT, preferred_element_type=f32)
        dq_ref[:, cols] = (dqt * HDIM ** (-0.5)).astype(bf16)
        kk = jnp.dot(qt[span, cols], ds, preferred_element_type=f32)
        vv = jnp.dot(dopb[span, cols], e, preferred_element_type=f32)
        if j == 0:
            dkt[...] = kk
            dvt[...] = vv
            poll(1)
        else:
            dk[g, span] = ((dkt[...] + kk) * (1.0 / LOG2E)).astype(bf16)
            dv[g, span] = (dvt[...] + vv).astype(bf16)

    def exchange(k):
        theirs = pl.ds(pl.multiple_of((1 - c) * half_keys, 128), half_keys)
        return (
            remote(dk.at[k, :, theirs], dk_in.at[k], ssem.at[2 * k], rsem.at[2 * k], chip),
            remote(dv.at[k, :, theirs], dv_in.at[k], ssem.at[2 * k + 1], rsem.at[2 * k + 1], chip),
        )

    @pl.when(h == 3)
    def _():
        for copy in exchange(g):
            copy.start()

    @pl.when(n == last)
    def _():
        mine = pl.ds(pl.multiple_of(c * half_keys, 128), half_keys)
        for tick in range(polls, max(when[-1] + 2 * direct, beside[-1] + 2 * SIDE_CHUNKS)):
            for at, s, first, size, side in plan:
                late = tick - at
                if late >= 0 and late % 2 == 0 and late // 2 < size:
                    run(s, first + late // 2, side)
        give = pltpu.make_async_copy(total, total_out, lsem.at[1])
        give.start()
        for k in range(4):
            for copy in exchange(k):
                copy.wait()
            band = slice(k * 128, (k + 1) * 128)
            dk_out[band] = dk[k, :, mine] + dk_in[k]
            dv_out[band] = dv[k, :, mine] + dv_in[k]
        act_far().wait()
        act_own().wait()
        give.wait()


def attend_back(cubes, q, k, v, do, ot, linv, e, act, grads):
    tokens, model = q.shape
    keys = k.shape[0]
    width = grads.shape[2]
    chunk = chunk_rows(cubes)
    depth = grads.shape[1] - LATE_CHUNKS * chunk
    sds = jax.ShapeDtypeStruct

    def cols(size):
        return pl.BlockSpec((size, 128), lambda n: (0, n // 4))

    fixed = pl.BlockSpec((model, tokens), lambda n: (0, 0))
    return pl.pallas_call(
        functools.partial(backward_kernel, cubes, chunk),
        name="attend_back",
        grid=(HEADS,),
        in_specs=[
            cols(tokens), cols(keys), cols(keys),
            pl.BlockSpec((128, tokens), lambda n: (n // 4, 0)),
            pl.BlockSpec((128, tokens), lambda n: (n // 4, 0)),
            pl.BlockSpec((4, 8, tokens), lambda n: (n // 4, 0, 0)),
            pl.BlockSpec((1, tokens, keys), lambda n: (n, 0, 0)),
            ANY,
            ANY,
        ],
        out_specs=[pl.BlockSpec((HDIM, tokens), lambda n: (n, 0)), fixed, fixed, ANY, ANY],
        out_shape=[
            sds((model, tokens), bf16),
            sds((model, tokens), bf16),
            sds((model, tokens), bf16),
            sds(act.shape, bf16),
            sds((depth, width), bf16),
        ],
        scratch_shapes=[
            pltpu.VMEM((keys, 256), bf16),
            pltpu.VMEM((128, keys), bf16),
            pltpu.VMEM((128, tokens), bf16),
            pltpu.VMEM((tokens, 256), bf16),
            pltpu.VMEM((128, tokens), bf16),
            pltpu.VMEM((HDIM, keys), f32),
            pltpu.VMEM((HDIM, keys), f32),
            pltpu.VMEM((4, 128, keys), bf16),
            pltpu.VMEM((4, 128, keys), bf16),
            pltpu.VMEM((4, 128, tokens), bf16),
            pltpu.VMEM((4, 128, tokens), bf16),
            pltpu.SemaphoreType.DMA((4,)),
            pltpu.SemaphoreType.DMA((9,)),
            pltpu.SemaphoreType.DMA((9,)),
            pltpu.VMEM((depth, width), bf16),
            pltpu.VMEM((2, depth, width), bf16),
        ] + reducer_scratch(cubes, depth // chunk, depth, width),
        compiler_params=params(2),
    )(q, k, v, do, ot, linv, e, act, grads)


def project_back_kernel(
    cubes, chunk,
    dq_in, dk_in, dv_in, first_hbm, embedded_in, middle_in, qkvw_in, embw_in, enc_in, tgt, vecf, sums, early,
    total, vis_out,
    dq, dk, dv, first_in, embedded, grad_middle, qkvw, embw, enc, isem,
    grads, first_t, gft, vgrad, vis_in, lsem, vs, vr, got_core, got_y, work, *rest,
):
    gots, (rs, rr) = rest[:-2], rest[-2:]
    cube, b, y, c = place()
    chip, across, diag = peers()
    bits = cubes.bit_length() - 1
    tokens, model = first_in.shape
    half = tokens // 2
    slots = enc.shape[0]
    er = embw.shape[0] // 4
    qr = model // 4
    first = LATE_CHUNKS * chunk
    left = range(LATE_CHUNKS)
    count = grads.shape[1] // chunk
    middle = range(LATE_CHUNKS, LATE_CHUNKS + 3 * qr // chunk)
    final = range(LATE_CHUNKS + 3 * qr // chunk, count)

    def mine(d, span):
        return grads[d, span]

    run, stages = reducer(cubes, chunk, grads, mine, got_core, got_y, work, gots, total, rs, rr)

    def runs(s, chunks):
        for t in chunks:
            run(s, t, "joint" if chunks is not left else True)

    fetch = pltpu.make_async_copy(
        early.at[:, pl.ds(early.shape[1] - first, first)], grads.at[:, pl.ds(0, first)], lsem.at[1]
    ) if first else None
    if first:
        fetch.start()
    greeted = (chip, across, diag, corner()) + tuple(mate_of(k) for k in range(bits))
    hail(greeted)

    loads = []
    for k, (src, dst) in enumerate((
        (first_hbm, first_in), (dq_in, dq), (dk_in, dk), (dv_in, dv), (qkvw_in, qkvw), (embedded_in, embedded),
        (middle_in, grad_middle), (enc_in, enc), (embw_in, embw),
    )):
        loads.append(pltpu.make_async_copy(src, dst, isem.at[k]))
        loads[-1].start()
    loads[0].wait()
    first_t[...] = first_in[...].astype(f32).T.astype(bf16)
    if first:
        fetch.wait()
    meet(greeted)
    runs(0, left)
    for k, part in enumerate((dq, dk, dv)):
        loads[1 + k].wait()
        term = lax.dot_general(first_t[...], part[...], NT, preferred_element_type=f32).astype(bf16)
        for d in range(4):
            grads[d, first + k * qr : first + (k + 1) * qr] = term[d * qr : (d + 1) * qr]
        if k == 1:
            runs(1, left)
    runs(0, middle)
    ones = jnp.ones((8, tokens), bf16)
    qsum = lax.dot_general(ones, dq[...], NT, preferred_element_type=f32)[0:1]
    vsum = lax.dot_general(ones, dv[...], NT, preferred_element_type=f32)[0:1]
    (gain,) = unpack(vecf, ((2, 1, ALL),))
    column = tgt[...].astype(f32).T[:, 0:1].astype(jnp.int32)
    for copy in loads[4:]:
        copy.wait()
    gft[...] = (
        jnp.dot(qkvw[:, 0:model], dq[...], preferred_element_type=f32)
        + jnp.dot(qkvw[:, model : 2 * model], dk[...], preferred_element_type=f32)
        + jnp.dot(qkvw[:, 2 * model :], dv[...], preferred_element_type=f32)
    )
    runs(1, middle)
    gsum = [jnp.zeros((1, model), f32)] * 3
    lifted = None
    for h in range(2):
        span = pl.ds(h * half, half)
        gf = gft[:, span].T
        value = embedded[span]
        center = value - jnp.mean(value, axis=-1, keepdims=True)
        rstd = lax.rsqrt(jnp.mean(center * center, axis=-1, keepdims=True) + EPS)
        normed = center * rstd
        gsum[0] += jnp.sum(gf * normed, axis=0, keepdims=True)
        gsum[1] += jnp.sum(gf, axis=0, keepdims=True)
        gn = gf * gain
        back = rstd * (
            gn - jnp.mean(gn, axis=-1, keepdims=True) - normed * jnp.mean(gn * normed, axis=-1, keepdims=True)
        )
        ge = grad_middle[span] + back
        offset = y * half + h * 2 * half
        hit = (iota((half, slots), 0) + offset == tgt[0:1]).astype(f32)
        flag = jnp.sum(hit, axis=1, keepdims=True)
        gsum[2] += jnp.sum((1.0 - flag) * ge, axis=0, keepdims=True)
        hit_t = (iota((slots, half), 1) + offset == column).astype(bf16)
        term = jnp.dot(hit_t, ge.astype(bf16), preferred_element_type=f32)
        lifted = term if lifted is None else lifted + term
        runs(2 + h, left)
    bsum = jnp.sum(lifted, axis=0, keepdims=True)
    low = lifted.astype(bf16)
    at = first + 3 * qr
    gemb = jnp.dot(enc[...].astype(f32).T.astype(bf16), low, preferred_element_type=f32).astype(bf16)
    for d in range(4):
        grads[d, at : at + er] = gemb[d * er : (d + 1) * er]

    def lanes(value, d, size=128):
        return value[:, d * size : (d + 1) * size]

    down_s, out_s, gain_s, bias_s = (sums[k : k + 1] for k in range(4))
    pad = grads.shape[1] - at - er
    for d in range(4):
        part = qsum if d < 2 else vsum
        blank = jnp.zeros((1, model // 2), f32)
        packed = [
            jnp.concatenate([lanes(bsum, d), lanes(gsum[2], d), lanes(gsum[0], d), lanes(gsum[1], d)], axis=1),
            jnp.concatenate([lanes(part, d % 2, 256), lanes(out_s, d), lanes(gain_s, d)], axis=1),
            sums[4 + d : 5 + d],
            jnp.concatenate([lanes(bias_s, d), lanes(down_s, d), blank], axis=1),
        ]
        packed = jnp.concatenate(packed + [jnp.zeros((pad - 4, model), f32)], axis=0)
        grads[d, at + er :] = packed.astype(bf16)
    runs(0, final)
    runs(2, middle)
    runs(4, left)
    vgrad[...] = (
        lax.dot_general(low, embw[...], NT, preferred_element_type=f32).astype(bf16).reshape(vgrad.shape)
    )
    vis_copies = [
        remote(vgrad.at[2 * (1 - y) + c], vis_in.at[y, :, c], vs.at[0], vr.at[0], across),
        remote(vgrad.at[2 * (1 - y) + 1 - c], vis_in.at[y, :, c], vs.at[1], vr.at[1], diag),
        remote(vgrad.at[2 * y + 1 - c], vis_in.at[y, :, c], vs.at[2], vr.at[2], chip),
        pltpu.make_async_copy(vgrad.at[b], vis_in.at[y, :, c], lsem.at[0]),
    ]
    runs(1, final)
    for copy in vis_copies:
        copy.start()
    runs(3, middle)
    runs(5, left)
    for step in range(2, stages + 1):
        if 4 + step <= stages:
            runs(4 + step, left)
        if step + 2 < stages:
            runs(step + 2, middle)
        if step < stages:
            runs(step, final)
    for copy in vis_copies:
        copy.wait()
    vis_out[...] = vis_in[0] + vis_in[1]


def project_back(cubes, dq, dk, dv, first_in, embedded, grad_middle, qkvw, embw, enc, tgt, vecf, sums, early, cap):
    tokens, model = first_in.shape
    chunk = chunk_rows(cubes)
    depth = 3 * model // 4 + embw.shape[0] // 4 + 16
    depth = depth + -depth % chunk + LATE_CHUNKS * chunk
    enc_width = enc.shape[1]
    slots = enc.shape[0]
    sds = jax.ShapeDtypeStruct
    return pl.pallas_call(
        functools.partial(project_back_kernel, cubes, chunk),
        name="project_back",
        out_shape=(sds((depth, model), bf16), sds((2, 2, cap, enc_width), bf16)),
        in_specs=[ANY] * 9 + [VM] * 3 + [ANY],
        out_specs=(VM, VM),
        scratch_shapes=[pltpu.VMEM((model, tokens), bf16)] * 3 + [
            pltpu.VMEM((tokens, model), bf16),
            pltpu.VMEM((tokens, model), f32),
            pltpu.VMEM((tokens, model), f32),
            pltpu.VMEM(qkvw.shape, bf16),
            pltpu.VMEM(embw.shape, bf16),
            pltpu.VMEM(enc.shape, bf16),
            pltpu.SemaphoreType.DMA((9,)),
            pltpu.VMEM((4, depth, model), bf16),
            pltpu.VMEM((model, tokens), bf16),
            pltpu.VMEM((model, tokens), f32),
            pltpu.VMEM((4, 2, cap, enc_width), bf16),
            pltpu.VMEM((2, 2, 2, cap, enc_width), bf16),
            pltpu.SemaphoreType.DMA((2,)),
            pltpu.SemaphoreType.DMA((3,)),
            pltpu.SemaphoreType.DMA((3,)),
        ] + reducer_scratch(cubes, depth // chunk, depth, model),
        compiler_params=params(3),
    )(dq, dk, dv, first_in, embedded, grad_middle, qkvw, embw, enc, tgt, vecf, sums, early)


def finish_kernel(late, first, second, down, up, out, qkv, emb, *vectors):
    model = down.shape[1]
    parts = up.shape[1] // model
    size = up.shape[0]
    start = first.shape[0]

    def early(at, count):
        if at + count <= start:
            return first[at : at + count].astype(f32)
        if at >= start:
            return second[at - start : at - start + count].astype(f32)
        return jnp.concatenate(
            [first[at:start].astype(f32), second[0 : at + count - start].astype(f32)], axis=0
        )

    down[...] = early(0, model).T
    for k in range(parts):
        up[:, k * model : (k + 1) * model] = early(model + k * size, size)
    out[...] = early(model + parts * size, size)
    for k in range(3):
        qkv[:, k * model : (k + 1) * model] = second[late + k * size : late + (k + 1) * size].astype(f32)
    at = late + 3 * size
    er = emb.shape[0]
    emb[...] = second[at : at + er].astype(f32)
    packed = second[at + er : at + er + 16].astype(f32)
    pieces = iter(vectors)
    for row, widths in enumerate(((128, 128, 128, 128), (256, 128, 128), (512,), (128, 128))):
        lane = 0
        for width in widths:
            next(pieces)[...] = packed[row : row + 1, lane : lane + width]
            lane += width


def finish(late, first, second, shapes):
    sds = jax.ShapeDtypeStruct
    widths = (128, 128, 128, 128, 256, 128, 128, 512, 128, 128)
    return pl.pallas_call(
        functools.partial(finish_kernel, late),
        name="results",
        out_shape=tuple(sds(s, f32) for s in shapes) + tuple(sds((1, w), f32) for w in widths),
        in_specs=[VM, VM],
        out_specs=tuple([VM] * (len(shapes) + len(widths))),
        compiler_params=params(),
    )(first, second)


def shards(
    cubes,
    visible, kept_rows, slot_counts, patches, positions, embedder, embedbias, masktoken, attngain, attnbias,
    qkvproj, qvbias, outproj, outbias, mlpgain, mlpbias, upproj, upbias, downproj, downbias, cotangent,
):
    cap, enc_width = visible.shape[2:]
    vis = visible.reshape(2, 2, cap, enc_width)
    vecs = [
        m.reshape(-1, 128)
        for m in (embedbias, masktoken, attngain, attnbias, qvbias, outbias, mlpgain, mlpbias, upbias, downbias)
    ]
    embedded, first_in, q, k, v, emb_full, qkv_full, enc, target, vecf = embed(
        vis, kept_rows[0], slot_counts, embedder, qkvproj, positions, vecs
    )
    own = (outproj, upproj, downproj, cotangent)
    e, ot, linv, mixed, *gathered = attend(patches, q, k, v, *own)
    act, grads, grad_middle, grad_mixed, sums = mlp(cubes, patches, vecf, mixed, ot, embedded, gathered, own)
    dq, dk, dv, activations, first = attend_back(cubes, q, k, v, grad_mixed, ot, linv, e, act, grads)
    second, visible_grad = project_back(
        cubes, dq, dk, dv, first_in, embedded, grad_middle, qkv_full, emb_full, enc.reshape(-1, enc_width), target, vecf, sums, grads, cap
    )
    shapes = (downproj.shape, upproj.shape, outproj.shape, qkvproj.shape, embedder.shape)
    down_o, up_o, out_o, qkv_o, emb_o, *small = finish(LATE_CHUNKS * chunk_rows(cubes), first, second, shapes)
    ebias, mask, again, abias, qv, outb, mgain, upb, mbias, downb = (m.reshape(-1) for m in small)
    return (
        activations, visible_grad.reshape(visible.shape), emb_o, ebias, mask, again, abias, qkv_o, qv,
        out_o, outb, mgain, mbias, up_o, upb, down_o, downb,
    )


def solution(mesh):
    cubes = mesh.shape["cube"]
    split = P(("cube", "band"), None, None, None)
    mat, row = P("band", None), P("band")
    placed = (
        split, P(("cube", "band"), None, None), P(("cube", "band"), None), P("cube"), mat,
        mat, row, row, row, row, mat, row, mat, row, row, row, mat, row, mat, row, P("cube", "band", None),
    )
    return jax.shard_map(
        functools.partial(shards, cubes),
        mesh=mesh,
        in_specs=placed,
        out_specs=(
            P("cube", "band", None), split, mat, row, row, row, row, mat, row, mat, row, row, row, mat, row, mat, row,
        ),
        check_vma=False,
    )
```
